32 devices in a mesh: grp: 2 (over y), chan: 4 (over z), sub: 4 (over x, core).
Axes of the slice: x: 2, y: 2, z: 4, core: 2. Of those that a mesh axis runs over, the one named last changes fastest.
Arguments:
- voltages: bfloat16 [2048, 2, 5504], P(('grp', 'chan', 'sub')), parts along dimension 0, may hold values from -6 to 6
- taps: float32 [1536], replicated, may hold values from -0.15625 to 0.15625
- input_id: int32 [1024], replicated, may hold values from 0 to 1023, each once
- counts: int32 [8], P('grp'), parts along dimension 0, may hold values from 2 to 8, as said below
- delays: int32 [512, 1024], P(('grp', 'sub')), parts along dimension 0, may hold values from 0 to 127
- beam_owner: int32 [512, 1], P('grp'), parts along dimension 0, may hold values from 0 to 3; in each aligned block of 64 rows (0 to 63, 64 to 127, ...) at most 32 rows name the same one
Outputs:
- visibility: bfloat16 [256, 2, 1024, 1024], P(('grp', 'chan'), None, 'sub'), parts along dimension 0
- resynth: float32 [1024, 2, 5504], P(('grp', 'chan', 'sub')), parts along dimension 0
The draws below stay inside these ranges and needn't reach their ends.
There are 2 independent parts, one for each index of `grp`. The reference program is written for one: setup_inputs(seed, part) draws one part's arguments, and reference() takes and returns one part's arrays. A program takes and returns all parts, laid end to end along the dimension named above; an argument that names none is the same for every part. Nothing has to cross between parts.
Inputs may be any that keep to these rules, and one draw needn't show every extreme that they name: `input_id`: each input id appears once. `counts`: every draw has a block with all 8 spectra valid. `beam_owner`: within each section of 64 consecutive beams no owner is named more than 32 times; some owner is named exactly 32 times in some section.
All inputs are finite; a program needn't handle non-finite values.
Results may differ from the reference program's by a relative error of at most 0.007.
Values may be sent and summed in bfloat16 or wider, within the bound.
A program may use at most 192 MiB of HBM per device.

```python
import math
import jax
import jax.numpy as jnp
import numpy as np
from jax import lax

INPUTS = 1024
NCH = 128
TAPS = 12
SPEC = 8
BLOCKS = 4
BEAMS = 256
NSPEC = 32
SAMPLES = 5504
BEAMS_SEC = 64
MOST = 32
SLOTS = 512
N_CHAN = 4
N_SUB = 4


def draw_counts(key, part):
    lowest = max(1, SPEC // 4)
    drawn = jax.random.randint(key, (BLOCKS,), lowest, SPEC + 1)
    chosen = jax.random.randint(jax.random.fold_in(key, 7), (), 0, BLOCKS)
    return jnp.where(jnp.arange(BLOCKS) == chosen, SPEC, drawn).astype(jnp.int32)


def plant(values, key, smallest, high):
    dims = values.shape
    place = [jax.random.randint(jax.random.fold_in(key, axis), (), 0, dims[axis]) for axis in range(len(dims))]
    values = values.at[tuple(place)].set(smallest)
    longest = dims.index(max(dims))
    place[longest] = (place[longest] + 1) % dims[longest]
    return values.at[tuple(place)].set(high)


def level_of(own_key, extent, cuts, low, high):
    def one(axis_at, blocks):
        heights = jax.random.uniform(jax.random.fold_in(jax.random.fold_in(own_key, 6), axis_at), (blocks,), jnp.float32, low / len(cuts), high / len(cuts))
        return jnp.repeat(jnp.exp(heights), extent[axis_at] // blocks).reshape((-1,) + (1,) * (len(extent) - axis_at - 1))

    factor_of = one(*cuts[0])
    for cut in cuts[1:]:
        factor_of = factor_of * one(*cut)
    return factor_of


def shared_out(rng, own, number, rows, count, top, bound, skew):
    order = jax.random.permutation(rng, count)
    crowded, usual = load_shares(count, rows * top, bound, skew, True), load_shares(count, rows * top, bound, skew, False)
    places = jnp.arange(count)

    def named(tallies, rotation):
        used = int((tallies > 0).sum())
        fixed = max(1, used // 4)
        shifted = fixed + (places - fixed + rotation * (used - fixed)) % max(1, count - fixed)
        return jnp.zeros((count,), jnp.int32).at[order[jnp.where(places < fixed, places, shifted)]].set(jnp.asarray(tallies, jnp.int32))

    tallies = jnp.where(number % 4 == 0, named(crowded, number // 4), named(usual, number - number // 4 - 1))
    mixed = jax.random.permutation(jax.random.fold_in(own, 3), count)
    donor, sink = mixed[0:count // 2 * 2:2], mixed[1:count // 2 * 2:2]
    slack = jnp.minimum(tallies[donor] - 1, bound - tallies[sink]) // 2
    slack = jnp.where((donor == order[0]) | (sink == order[0]) | (tallies[sink] == 0), 0, jnp.maximum(slack, 0))
    shifted = jax.random.randint(jax.random.fold_in(own, 4), (count // 2,), 0, 1 << 20) % (slack + 1)
    tallies = tallies.at[donor].add(-shifted).at[sink].add(shifted)
    members = jnp.searchsorted(jnp.cumsum(tallies), jnp.arange(rows * top), side="right").astype(jnp.int32)
    table = members.reshape(top, rows).T
    table = table[jax.random.permutation(jax.random.fold_in(own, 1), rows)]
    rotation = jax.random.randint(jax.random.fold_in(own, 2), (rows, 1), 0, top)
    return jnp.take_along_axis(table, (jnp.arange(top)[None, :] + rotation) % top, axis=1)


def load_shares(number_of, total, bound, skew, full):
    loads = [(1 << 20) // math.isqrt(standing ** skew) + 1 for standing in range(1, number_of + 1)]
    largest = bound if full else min(bound, max(-(-total // number_of), total * loads[0] // sum(loads)))
    least = 1 if total - largest >= number_of - 1 else 0
    holding, spare = [largest] + [least] * (number_of - 1), total - largest - least * (number_of - 1)
    while spare > 0:
        candidates = [i for i in range(1, number_of) if holding[i] < largest] or [i for i in range(1, number_of) if holding[i] < bound]
        whole, left = sum([loads[i] for i in candidates]), spare
        for i in candidates:
            more = min(bound - holding[i], max(1, left * loads[i] // whole), spare)
            holding[i] = holding[i] + more
            spare = spare - more
    return np.array(holding)


def centred(stream_key, dims, deviation, most, pieces=(), held_as=jnp.bfloat16):
    loudness = level_of(stream_key, dims, pieces, -0.22, 0.18) if pieces else 1.0
    array = jax.random.normal(stream_key, dims, jnp.float32) * deviation * loudness
    return jnp.minimum(jnp.maximum(array, -most), most).astype(held_as)


def setup_inputs(seed: int = 0, part: int = 0) -> dict:
    seeds = jax.random.split(jax.random.key(seed), 7)
    own_keys = jax.random.split(jax.random.fold_in(seeds[6], part), 7)
    voltages = centred(own_keys[0], (INPUTS, 2, SAMPLES), 1.0, 6.0, ((0, 16),))
    taps = centred(seeds[1], (TAPS * NCH,), (TAPS * NCH) ** -0.5, 0.15625, (), jnp.float32)
    input_id = jax.random.permutation(seeds[2], INPUTS).astype(jnp.int32)
    counts = draw_counts(jax.random.fold_in(jax.random.fold_in(seeds[6], part), 71), part)
    delays = plant(jax.random.randint(own_keys[4], (BEAMS, INPUTS), 0, NCH), jax.random.fold_in(own_keys[4], 1), 0, NCH - 1).astype(jnp.int32)
    beam_owner_keys = jax.random.split(jax.random.fold_in(own_keys[5], 1), BEAMS // BEAMS_SEC)
    beam_owner_turns = jax.random.permutation(jax.random.fold_in(own_keys[5], 3), BEAMS // BEAMS_SEC)
    beam_owner = jax.vmap(lambda own, number: shared_out(jax.random.fold_in(own_keys[5], 2), own, number, BEAMS_SEC, N_CHAN, 1, MOST, 2))(beam_owner_keys, beam_owner_turns).reshape((BEAMS, 1))
    return dict(voltages=voltages, taps=taps, input_id=input_id, counts=counts, delays=delays, beam_owner=beam_owner)


def filter_table(taps):
    length = taps.shape[0]
    position = jnp.arange(length, dtype=jnp.int32) % NCH
    channel = jnp.arange(NCH, dtype=jnp.int32)
    phase = (position[:, None] * channel[None, :] % NCH).astype(jnp.float32) * (2.0 * math.pi / NCH)
    cosine = taps[:, None] * jnp.cos(phase)
    sine = taps[:, None] * jnp.sin(phase)
    upper = jnp.concatenate([cosine, -sine], axis=1)
    lower = jnp.concatenate([sine, cosine], axis=1)
    return jnp.concatenate([upper, lower], axis=0).astype(jnp.bfloat16)

def valid_mask(counts):
    position = jnp.arange(NSPEC, dtype=jnp.int32)
    return (position % SPEC < jnp.repeat(counts, SPEC)).astype(jnp.float32)

def channelize(volts, table, valid):
    count = volts.shape[0]
    frames = volts.reshape(count, 2, NSPEC + TAPS - 1, NCH).astype(jnp.float32)
    windows = jnp.concatenate([frames[:, :, k:k + NSPEC, :] for k in range(TAPS)], axis=3)
    table3 = table.astype(jnp.float32).reshape(2, TAPS * NCH, 2 * NCH)
    out = jnp.einsum('icth,chm->mit', windows, table3)
    out = out * valid[None, None, :]
    return out.reshape(2, NCH, count, NSPEC).astype(jnp.bfloat16)

def resynthesize(received, table):
    count = received.shape[0]
    table3 = table.astype(jnp.float32).reshape(2 * TAPS * NCH, 2, NCH)
    grid = jnp.einsum('pcht,mch->ptm', received.astype(jnp.float32), table3)
    grid = grid.reshape(count, NSPEC, 2, TAPS, NCH)
    total = jnp.zeros((count, NSPEC + TAPS - 1, 2, NCH), jnp.float32)
    for k in range(TAPS):
        total = total + jnp.pad(grid[:, :, :, k, :], ((0, 0), (k, TAPS - 1 - k), (0, 0), (0, 0)))
    return jnp.transpose(total, (0, 2, 1, 3)).reshape(count, 2, SAMPLES)

def reference(voltages, taps, input_id, counts, delays, beam_owner):
    table = filter_table(taps)
    valid = valid_mask(counts)
    total = jnp.sum(counts.astype(jnp.float32))
    group = math.gcd(64, INPUTS)
    grouped = voltages.reshape(INPUTS // group, group, 2, SAMPLES)
    parts = lax.map(lambda volts: channelize(volts, table, valid), grouped)
    spectra = jnp.transpose(parts, (1, 2, 0, 3, 4)).reshape(2, NCH, INPUTS, NSPEC)
    slot_of = jnp.zeros((INPUTS,), jnp.int32).at[input_id].set(jnp.arange(INPUTS, dtype=jnp.int32))
    by_id = jnp.take(spectra, slot_of, axis=2)
    per_channel = jnp.transpose(by_id, (1, 0, 2, 3))

    def correlate(data):
        first = data[0].astype(jnp.float32)
        second = data[1].astype(jnp.float32)
        real_part = jnp.dot(first, first.T) + jnp.dot(second, second.T)
        imag_part = jnp.dot(second, first.T) - jnp.dot(first, second.T)
        return (jnp.stack([real_part, imag_part]) / total).astype(jnp.bfloat16)
    visibility = lax.map(correlate, per_channel)

    def form(item):
        data, channel = item
        phase = (delays * channel % NCH).astype(jnp.float32) * (2.0 * math.pi / NCH)
        scale = 1.0 / math.sqrt(INPUTS)
        weight_cos = (jnp.cos(phase) * scale).astype(jnp.bfloat16).astype(jnp.float32)
        weight_sin = (jnp.sin(phase) * scale).astype(jnp.bfloat16).astype(jnp.float32)
        first = data[0].astype(jnp.float32)
        second = data[1].astype(jnp.float32)
        real_part = jnp.dot(weight_cos, first) - jnp.dot(weight_sin, second)
        imag_part = jnp.dot(weight_cos, second) + jnp.dot(weight_sin, first)
        return jnp.stack([real_part, imag_part]).astype(jnp.bfloat16)
    channels = jnp.arange(NCH, dtype=jnp.int32)
    beams = lax.map(form, (per_channel, channels))
    per_beam = jnp.transpose(beams, (2, 1, 0, 3))
    bunch = math.gcd(16, BEAMS)
    voices = lax.map(lambda rows: resynthesize(rows, table), per_beam.reshape(BEAMS // bunch, bunch, 2, NCH, NSPEC))
    voices = voices.reshape(BEAMS, 2, SAMPLES)
    owner = beam_owner[:, 0]
    beam = jnp.arange(BEAMS, dtype=jnp.int32)
    section = beam // BEAMS_SEC
    earlier = (section[:, None] == section[None, :]) & (owner[:, None] == owner[None, :]) & (beam[None, :] < beam[:, None])
    rank = lax.optimization_barrier(jnp.sum(earlier.astype(jnp.int32), axis=1)).astype(jnp.int32)
    slot = (owner * N_SUB + section) * MOST + rank
    resynth = jnp.zeros((SLOTS, 2, SAMPLES), jnp.float32).at[slot].set(voices)
    return (visibility, resynth)
```

```python
import functools
import math

import jax
import jax.numpy as jnp
from jax import lax
from jax.experimental import pallas as pl
from jax.experimental.pallas import tpu as pltpu
from jax.sharding import PartitionSpec as P

NCH = 128
TAPS = 12
SPEC = 8
BLOCKS = 4
BEAMS = 256


def filter_table(taps, chans):
    length = taps.shape[0]
    position = jnp.arange(length, dtype=jnp.int32) % chans
    channel = jnp.arange(chans, dtype=jnp.int32)
    phase = (position[:, None] * channel[None, :] % chans).astype(jnp.float32) * (
        2.0 * math.pi / chans
    )
    cosine = taps[:, None] * jnp.cos(phase)
    sine = taps[:, None] * jnp.sin(phase)
    upper = jnp.concatenate([cosine, -sine], axis=1)
    lower = jnp.concatenate([sine, cosine], axis=1)
    return jnp.concatenate([upper, lower], axis=0).astype(jnp.bfloat16)


def resynthesize(received, table, taps_count, chans):
    count = received.shape[0]
    spectra_n = received.shape[3]
    table3 = table.reshape(2 * taps_count * chans, 2, chans)
    grid = jnp.einsum("pcht,mch->ptm", received, table3, preferred_element_type=jnp.float32)
    grid = grid.reshape(count, spectra_n, 2, taps_count, chans)
    total = jnp.zeros((count, spectra_n + taps_count - 1, 2, chans), jnp.float32)
    for k in range(taps_count):
        total = total + jnp.pad(
            grid[:, :, :, k, :], ((0, 0), (k, taps_count - 1 - k), (0, 0), (0, 0))
        )
    return jnp.transpose(total, (0, 2, 1, 3)).reshape(
        count, 2, (spectra_n + taps_count - 1) * chans
    )


def local_plain(voltages, taps, input_id, counts, delays, beam_owner):
    n_chan = lax.axis_size("chan")
    n_sub = lax.axis_size("sub")
    inp_dev = voltages.shape[0]
    inputs = input_id.shape[0]
    chans = NCH
    taps_count = TAPS
    spectra_n = BLOCKS * SPEC
    ch_dev = chans // n_chan
    rows = inputs // n_sub
    section = BEAMS // n_sub
    most = min(section, max(2, 2 * section // n_chan))
    table = filter_table(taps, chans)
    position = jnp.arange(spectra_n, dtype=jnp.int32)
    valid = (position % SPEC < jnp.repeat(counts, SPEC)).astype(jnp.float32)
    total = jnp.sum(counts.astype(jnp.float32))
    frames = voltages.reshape(inp_dev, 2, spectra_n + taps_count - 1, chans)
    windows = jnp.concatenate(
        [frames[:, :, k : k + spectra_n, :] for k in range(taps_count)], axis=3
    )
    table3 = table.reshape(2, taps_count * chans, 2 * chans)
    filtered = jnp.einsum("icth,chm->mit", windows, table3, preferred_element_type=jnp.float32)
    filtered = filtered * valid[None, None, :]
    spectra = filtered.reshape(2, chans, inp_dev, spectra_n).astype(jnp.bfloat16)
    slot_of = jnp.zeros((inputs,), jnp.int32).at[input_id].set(jnp.arange(inputs, dtype=jnp.int32))
    turned = lax.all_to_all(spectra, "chan", split_axis=1, concat_axis=2, tiled=True)
    gathered = lax.all_gather(turned, "sub", axis=2, tiled=True)
    chan_part = slot_of // (n_sub * inp_dev)
    sub_part = slot_of // inp_dev % n_sub
    order = (sub_part * n_chan + chan_part) * inp_dev + slot_of % inp_dev
    by_id = jnp.take(gathered, order, axis=2)
    sub_index = lax.axis_index("sub")
    mine = lax.dynamic_slice_in_dim(by_id, sub_index * rows, rows, 2)
    real_part = jnp.einsum("cxit,cxjt->xij", mine, by_id, preferred_element_type=jnp.float32)
    imag_part = jnp.einsum("xit,xjt->xij", mine[1], by_id[0], preferred_element_type=jnp.float32)
    imag_part = imag_part - jnp.einsum(
        "xit,xjt->xij", mine[0], by_id[1], preferred_element_type=jnp.float32
    )
    visibility = (jnp.stack([real_part, imag_part], axis=1) / total).astype(jnp.bfloat16)
    channel = lax.axis_index("chan") * ch_dev + jnp.arange(ch_dev, dtype=jnp.int32)
    phase = (delays[None, :, :] * channel[:, None, None] % chans).astype(jnp.float32) * (
        2.0 * math.pi / chans
    )
    scale = 1.0 / math.sqrt(inputs)
    weight_cos = (jnp.cos(phase) * scale).astype(jnp.bfloat16)
    weight_sin = (jnp.sin(phase) * scale).astype(jnp.bfloat16)
    from_cos = jnp.einsum("xbi,cxit->cxbt", weight_cos, by_id, preferred_element_type=jnp.float32)
    from_sin = jnp.einsum("xbi,cxit->cxbt", weight_sin, by_id, preferred_element_type=jnp.float32)
    beams = jnp.stack([from_cos[0] - from_sin[1], from_cos[1] + from_sin[0]]).astype(jnp.bfloat16)
    owner = lax.dynamic_slice_in_dim(beam_owner[:, 0], sub_index * section, section)
    beam = jnp.arange(section, dtype=jnp.int32)
    earlier = (owner[None, :] == owner[:, None]) & (beam[None, :] < beam[:, None])
    rank = jnp.sum(earlier.astype(jnp.int32), axis=1)
    target = owner * most + rank
    select = (jnp.arange(n_chan * most, dtype=jnp.int32)[:, None] == target[None, :]).astype(
        jnp.bfloat16
    )
    placed = jnp.einsum("pb,cxbt->pcxt", select, beams, preferred_element_type=jnp.float32).astype(
        jnp.bfloat16
    )
    placed = placed.reshape(n_chan, most, 2, ch_dev, spectra_n)
    resynth = resynthesize(
        lax.all_to_all(placed, "chan", split_axis=0, concat_axis=3, tiled=True)[0],
        table,
        taps_count,
        chans,
    )
    return (visibility, resynth)


def turn_of(steps):
    quarter = NCH // 4
    turn = steps & (NCH - 1)
    quadrant = (turn + quarter // 2) >> (quarter.bit_length() - 1)
    x = (turn - quadrant * quarter).astype(jnp.float32) * (2.0 * math.pi / NCH)
    y = x * x
    even = 1.0 + y * (-1 / 2 + y * (1 / 24 + y * (-1 / 720 + y * (1 / 40320))))
    odd = x * (1.0 + y * (-1 / 6 + y * (1 / 120 + y * (-1 / 5040 + y * (1 / 362880)))))
    swap = (quadrant & 1) == 1
    cosine, sine = jnp.where(swap, odd, even), jnp.where(swap, even, odd)
    cosine = jnp.where(((quadrant + 1) & 2) == 2, -cosine, cosine)
    return cosine, jnp.where((quadrant & 2) == 2, -sine, sine)


def weigh(first, scale, delay_ref, out_ref, at, left, high, wide):
    beams_n = delay_ref.shape[0]
    delay = delay_ref[at : at + high, left : left + wide]
    step_cos, step_sin = turn_of(delay)
    cosine, sine = turn_of(delay * first)

    def body(f, held):
        cosine, sine = held
        out_ref[f, at : at + high, left : left + wide] = cosine.astype(jnp.bfloat16)
        low = at + beams_n
        out_ref[f, low : low + high, left : left + wide] = sine.astype(jnp.bfloat16)
        return (
            cosine * step_cos - sine * step_sin,
            sine * step_cos + cosine * step_sin,
        )

    lax.fori_loop(0, out_ref.shape[0], body, (cosine * scale, sine * scale))


QUAD = 4


def trig_of(shape, n_grp):
    row = lax.broadcasted_iota(jnp.int32, shape, 0)
    lane = lax.broadcasted_iota(jnp.int32, shape, 1)
    tile = 2 * QUAD
    part = row // QUAD % 2
    channel = row // tile * QUAD + row % QUAD
    to_part = lane // NCH
    cosine, sine = turn_of(channel * (lane % NCH))
    return jnp.where(part == to_part, cosine, jnp.where(to_part == 1, sine, -sine))


def partner(x, lanes):
    pieces = [x[:, at : at + 128] for at in range(0, lanes, 128)]
    after = jnp.concatenate([pltpu.roll(p, 128 - QUAD, 1) for p in pieces], axis=1)
    before = jnp.concatenate([pltpu.roll(p, QUAD, 1) for p in pieces], axis=1)
    lane = lax.broadcasted_iota(jnp.int32, x.shape, 1)
    return lane // QUAD % 2 == 0, after, before


def front_kernel(
    n_chan, n_sub, most,
    frames_ref, taps_ref, counts_ref, names_ref, delay_ref, slot_ref,
    sorted_ref, beams_ref,
    x_ref, g_ref, y_ref, d_ref, perm_ref, c_ref, held, weight_ref, place_ref, ready,
    own_sem, out_sem, keep_sem, zs, zr, xs, xr, cs, cr, es, er,
):
    me_c, me_s = lax.axis_index("chan"), lax.axis_index("sub")
    core, across = me_s % 2, me_s // 2
    n_x = n_sub // 2
    twin = me_s + 1 - 2 * core
    mesh_id = pl.DeviceIdType.MESH
    pieces, per = x_ref.shape[1], x_ref.shape[2]
    n_grp = pieces * per
    spectra_n = BLOCKS * SPEC
    rows = frames_ref.shape[2]
    inputs = names_ref.shape[1]
    beams_n = delay_ref.shape[0]
    ch_dev = n_grp * QUAD
    tile = 2 * QUAD
    wide = 2 * NCH
    block = x_ref.shape[3]

    def chan_of(offset):
        return (me_c + offset) % n_chan

    def sub_of(offset):
        return (across + offset) % n_x * 2 + core

    barrier = pltpu.get_barrier_semaphore()
    for j in range(1, n_chan):
        pl.semaphore_signal(barrier, device_id={"chan": chan_of(j)}, device_id_type=mesh_id)
    for j in range(1, n_x):
        pl.semaphore_signal(barrier, device_id={"sub": sub_of(j)}, device_id_type=mesh_id)
    pl.semaphore_signal(barrier, device_id={"sub": twin}, device_id_type=mesh_id)

    def z_copy(j, q):
        return pltpu.make_async_remote_copy(
            src_ref=x_ref.at[chan_of(j), q],
            dst_ref=g_ref.at[q, me_c, me_s],
            send_sem=zs.at[j, q],
            recv_sem=zr.at[j, q],
            device_id={"chan": chan_of(j)},
            device_id_type=mesh_id,
        )

    def source(j, q):
        if j == 0:
            return x_ref.at[me_c, q]
        return g_ref.at[q, chan_of(n_chan - j), me_s]

    def x_copy(dx, j, q):
        return pltpu.make_async_remote_copy(
            src_ref=source(j, q),
            dst_ref=g_ref.at[q, chan_of(n_chan - j), me_s],
            send_sem=xs.at[dx, j, q],
            recv_sem=xr.at[dx, j, q],
            device_id={"sub": sub_of(dx)},
            device_id_type=mesh_id,
        )

    def core_copy(dx, j, q):
        home = g_ref.at[q, chan_of(n_chan - j), sub_of(n_x - dx)]
        return pltpu.make_async_remote_copy(
            src_ref=source(j, q) if dx == 0 else home,
            dst_ref=home,
            send_sem=cs.at[dx, j, q],
            recv_sem=cr.at[dx, j, q],
            device_id={"sub": twin},
            device_id_type=mesh_id,
        )

    def beam_copy(j, q):
        return pltpu.make_async_remote_copy(
            src_ref=ready.at[chan_of(j), q],
            dst_ref=beams_ref.at[me_c, q],
            send_sem=es.at[j, q],
            recv_sem=er.at[j, q],
            device_id={"chan": chan_of(j)},
            device_id_type=mesh_id,
        )

    trig = trig_of((n_chan * n_grp * tile, wide), n_grp)
    high = trig.astype(jnp.bfloat16)
    d_ref[:, :wide] = high
    d_ref[:, wide:] = (trig - high.astype(jnp.float32)).astype(jnp.bfloat16)

    valid = []
    for t in range(spectra_n):
        valid.append(jnp.where(counts_ref[t // SPEC] > t % SPEC, 1.0, 0.0))
    step = 16
    run = 4

    for c in range(2):

        @pl.loop(0, rows // step)
        def _(it):
            at = pl.multiple_of(it * step, step)
            taps = [taps_ref[k : k + 1, :] for k in range(TAPS)]
            for first in range(0, spectra_n, run):
                window = [
                    frames_ref[c, s, pl.ds(at, step), :].astype(jnp.float32)
                    for s in range(first, first + run + TAPS - 1)
                ]
                for j in range(run):
                    t = first + j
                    total = window[j] * taps[0]
                    for k in range(1, TAPS):
                        total = total + window[j + k] * taps[k]
                    total = total * valid[t]
                    high = total.astype(jnp.bfloat16)
                    low = (total - high.astype(jnp.float32)).astype(jnp.bfloat16)
                    slot = t // 2 * 2 + (t % 2 + core) % 2
                    to = pl.multiple_of(slot * rows + at, step)
                    y_ref[pl.ds(to, step), c * NCH : (c + 1) * NCH] = high
                    y_ref[pl.ds(to, step), wide + c * NCH : wide + (c + 1) * NCH] = low

    across_dims = (((1,), (1,)), ((), ()))

    @pl.loop(0, spectra_n // 4)
    def _(u):
        at = pl.multiple_of(u * 4 * rows, 4 * rows)
        high = y_ref[pl.ds(at, 4 * rows), :wide]
        low = y_ref[pl.ds(at, 4 * rows), wide:]
        out = lax.dot_general(d_ref[:, :wide], high, across_dims, preferred_element_type=jnp.float32)
        out = out + lax.dot_general(
            d_ref[:, wide:], high, across_dims, preferred_element_type=jnp.float32
        )
        out = out + lax.dot_general(
            d_ref[:, :wide], low, across_dims, preferred_element_type=jnp.float32
        )
        to = pl.multiple_of(u * 2 * tile, 2 * tile)
        for d in range(n_chan):
            for q in range(pieces):
                for e in range(per):
                    row = ((d * pieces + q) * per + e) * tile
                    both = jnp.concatenate(
                        [out[row : row + tile, :128], out[row : row + tile, 128:]], axis=0
                    )
                    x_ref[d, q, e, pl.ds(to, 2 * tile), :] = both.astype(jnp.bfloat16)

    pl.semaphore_wait(barrier, n_chan + n_x - 1)
    started = []

    def send(copy):
        copy.start()
        started.append(copy)

    def spread(j, q):
        for dx in range(1, n_x):
            send(x_copy(dx, j, q))
        send(core_copy(0, j, q))

    for q in range(pieces):
        for j in range(1, n_chan):
            send(z_copy(j, q))
    for q in range(pieces):
        spread(0, q)
    keeps = []
    for q in range(pieces):
        keep = pltpu.make_async_copy(x_ref.at[me_c, q], g_ref.at[q, me_c, me_s], keep_sem.at[q])
        keep.start()
        keeps.append(keep)

    half = inputs // 4
    first = me_c * ch_dev
    scale = 1.0 / math.sqrt(inputs)

    def name_unit(parity, m):
        def run_unit():
            name = names_ref[parity : parity + 1, :]
            low = lax.broadcasted_iota(jnp.int32, (half, inputs), 0) + m * half
            perm_ref[parity, m * half : (m + 1) * half, :] = jnp.where(
                name == low, 1.0, 0.0
            ).astype(jnp.bfloat16)

        return run_unit

    def weigh_unit(at, left):
        return lambda: weigh(first, scale, delay_ref, weight_ref, at, left, 16, 512)

    def place_unit():
        slots = place_ref.shape[1]
        lane = lax.broadcasted_iota(jnp.int32, (beams_n, slots), 1)
        for m in range(4):
            for e in range(per):
                want = slot_ref[...] + (e * n_chan * 4 + m) * most
                at = (m * per + e) * beams_n
                place_ref[at : at + beams_n, :] = jnp.where(lane == want, 1.0, 0.0).astype(
                    jnp.bfloat16
                )

    def join_unit(q):
        def run_unit():
            left = lax.broadcasted_iota(jnp.int32, (block, 128), 1) < 64
            for e in range(per):
                for c in range(n_chan):
                    for x in range(n_x):
                        a = g_ref[q, c, 2 * x, e].astype(jnp.float32)
                        b = g_ref[q, c, 2 * x + 1, e].astype(jnp.float32)
                        at = (c * n_x + x) * 128
                        c_ref[0, e * block : (e + 1) * block, at : at + 128] = jnp.where(
                            left, a, b
                        ).astype(jnp.bfloat16)
                        c_ref[1, e * block : (e + 1) * block, at : at + 128] = jnp.where(
                            left, b, a
                        ).astype(jnp.bfloat16)

        return run_unit

    def sort_unit(q, parity, m):
        def run_unit():
            out = lax.dot_general(
                perm_ref[parity, m * half : (m + 1) * half, :],
                c_ref[parity],
                across_dims,
                preferred_element_type=jnp.float32,
            ).astype(jnp.bfloat16)
            for e in range(per):
                held[q * per + e, m * half : (m + 1) * half, parity * block : (parity + 1) * block] = out[
                    :, e * block : (e + 1) * block
                ]

        return run_unit

    mixes = {}

    def mix_unit(q, e):
        def run_unit():
            at = q * per + e
            lane = lax.broadcasted_iota(jnp.int32, (2 * beams_n, 2 * block), 1)
            total = None
            for f in range(QUAD):
                mixed = jnp.dot(
                    weight_ref[at * QUAD + f], held[at], preferred_element_type=jnp.float32
                )
                total = mixed if total is None else jnp.where(lane % QUAD == f, mixed, total)
            real, after, before = partner(total[beams_n:], 2 * block)
            mixes[q, e] = total[:beams_n] + jnp.where(real, -after, before)

        return run_unit

    def place_beams(q):
        def run_unit():
            both = jnp.concatenate([mixes.pop((q, e)) for e in range(per)], axis=0)
            turned = both.T
            parts = []
            for m in range(4):
                parity, u = m % 2, m // 2
                picks = [
                    turned[parity * block + v * 2 * tile + u * tile :][:tile]
                    for v in range(spectra_n // 4)
                ]
                parts.append(jnp.concatenate(picks, axis=0))
            lined = jnp.concatenate(parts, axis=1).astype(jnp.bfloat16)
            out = jnp.dot(lined, place_ref[...], preferred_element_type=jnp.float32).astype(
                jnp.bfloat16
            )
            for e in range(per):
                for d in range(n_chan):
                    at = (e * n_chan + d) * 128
                    ready[d, q, e] = out[:, at : at + 128]
            for j in range(1, n_chan):
                send(beam_copy(j, q))
            keep = pltpu.make_async_copy(ready.at[me_c, q], beams_ref.at[me_c, q], own_sem.at[q])
            keep.start()
            keeps.append(keep)

        return run_unit

    def store_unit(q):
        def run_unit():
            part = pl.ds(q * per, per)
            keep = pltpu.make_async_copy(held.at[part], sorted_ref.at[part], out_sem.at[q])
            keep.start()
            keeps.append(keep)

        return run_unit

    def units_of(q):
        units = [join_unit(q)]
        units += [sort_unit(q, parity, m) for parity in range(2) for m in range(4)]
        units += [store_unit(q)] + [mix_unit(q, e) for e in range(per)] + [place_beams(q)]
        return units

    def z_step(j, q):
        def run_step():
            z_copy(j, q).wait_recv()
            spread(j, q)

        return run_step

    def x_step(j, q):
        for dx in range(1, n_x):
            x_copy(dx, j, q).wait_recv()
            send(core_copy(dx, j, q))

    def weave(units, steps):
        done = 0
        for i, one in enumerate(steps):
            upto = len(units) * (i + 1) // len(steps)
            for unit in units[done:upto]:
                unit()
            done = upto
            one()
        for unit in units[done:]:
            unit()

    def arrive(q):
        keeps[q].wait()
        for j in range(n_chan):
            for dx in range(n_x):
                core_copy(dx, j, q).wait_recv()

    setup = [name_unit(parity, m) for parity in range(2) for m in range(4)]
    setup += [
        weigh_unit(at, left) for at in range(0, beams_n, 16) for left in range(0, inputs, 512)
    ]
    setup.append(place_unit)
    weave(setup, [z_step(j, 0) for j in range(1, n_chan)])
    for q in range(1, pieces + 1):
        for j in range(n_chan):
            x_step(j, q - 1)
        arrive(q - 1)
        steps = [z_step(j, q) for j in range(1, n_chan)] if q < pieces else []
        weave(units_of(q - 1), steps)
    for q in range(pieces):
        for j in range(1, n_chan):
            beam_copy(j, q).wait_recv()
    for copy in started:
        copy.wait_send()
    for keep in keeps[pieces:]:
        keep.wait()


def front(frames, taps, counts, names, delays, slots, n_chan, n_sub, most):
    rows = frames.shape[2]
    beams_n, inputs = delays.shape
    spectra_n = BLOCKS * SPEC
    ch_dev = NCH // n_chan
    n_grp = ch_dev // QUAD
    per = 2
    pieces = n_grp // per
    n_x = n_sub // 2
    tile = 2 * QUAD
    block = spectra_n // 2 * tile
    dma = pltpu.SemaphoreType.DMA
    vmem = pl.BlockSpec(memory_space=pltpu.VMEM)
    travel = (n_chan, pieces, per, spectra_n // 4 * tile, 128)
    return pl.pallas_call(
        functools.partial(front_kernel, n_chan, n_sub, most),
        in_specs=[vmem, vmem, pl.BlockSpec(memory_space=pltpu.SMEM), vmem, vmem, vmem],
        out_specs=[pl.BlockSpec(memory_space=pl.ANY)] * 2,
        out_shape=[
            jax.ShapeDtypeStruct((n_grp, inputs, 2 * block), jnp.bfloat16),
            jax.ShapeDtypeStruct(travel, jnp.bfloat16),
        ],
        scratch_shapes=[
            pltpu.VMEM((n_chan, pieces, per, block, 128), jnp.bfloat16),
            pltpu.VMEM((pieces, n_chan, n_sub, per, block, 128), jnp.bfloat16),
            pltpu.VMEM((spectra_n * rows, 4 * NCH), jnp.bfloat16),
            pltpu.VMEM((2 * NCH, 4 * NCH), jnp.bfloat16),
            pltpu.VMEM((2, inputs, inputs), jnp.bfloat16),
            pltpu.VMEM((2, per * block, inputs), jnp.bfloat16),
            pltpu.VMEM((n_grp, inputs, 2 * block), jnp.bfloat16),
            pltpu.VMEM((ch_dev, 2 * beams_n, inputs), jnp.bfloat16),
            pltpu.VMEM((4 * per * beams_n, per * n_chan * 128), jnp.bfloat16),
            pltpu.VMEM(travel, jnp.bfloat16),
            dma((pieces,)),
            dma((pieces,)),
            dma((pieces,)),
            dma((n_chan, pieces)),
            dma((n_chan, pieces)),
            dma((n_x, n_chan, pieces)),
            dma((n_x, n_chan, pieces)),
            dma((n_x, n_chan, pieces)),
            dma((n_x, n_chan, pieces)),
            dma((n_chan, pieces)),
            dma((n_chan, pieces)),
        ],
        compiler_params=pltpu.CompilerParams(collective_id=0, has_side_effects=True),
        name="front",
    )(frames, taps, counts, names, delays, slots)


def back_kernel(
    per, sub_ref, counts_ref, mine_ref, all_ref, beams_ref, taps_ref,
    out_ref, voice_ref,
    turned_ref, bank_ref, table_ref,
):
    g, part = pl.program_id(0), pl.program_id(1)
    step = g * pl.num_programs(1) + part
    rows, lanes = mine_ref.shape[1], mine_ref.shape[2]
    inputs = all_ref.shape[1]
    count, _, samples = voice_ref.shape
    frames_n = samples // NCH
    spectra_n = frames_n - TAPS + 1
    n_chan, n_grp = beams_ref.shape[0], beams_ref.shape[1]
    tile = 2 * QUAD
    total = counts_ref[0]
    for i in range(1, BLOCKS):
        total = total + counts_ref[i]
    scale = 1.0 / jnp.full((8, 128), total.astype(jnp.float32))
    scale = scale[:1, :1]

    @pl.when(part == 0)
    def _():
        wide = mine_ref[0].astype(jnp.float32)
        real, after, before = partner(wide, lanes)
        turned_ref[...] = jnp.where(real, after, -before).astype(jnp.bfloat16)

    lane = lax.broadcasted_iota(jnp.int32, (rows, lanes), 1) % QUAD
    plain, turned = mine_ref[0].astype(jnp.float32), turned_ref[...].astype(jnp.float32)
    lefts = []
    for i in range(per):
        keep = lane == part * per + i
        lefts.append(jnp.where(keep, plain, 0.0).astype(jnp.bfloat16))
        lefts.append(jnp.where(keep, turned, 0.0).astype(jnp.bfloat16))
    left = jnp.concatenate(lefts, axis=0)
    for at in range(0, inputs, 256):
        product = lax.dot_general(
            left,
            all_ref[0, at : at + 256, :],
            (((1,), (1,)), ((), ())),
            preferred_element_type=jnp.float32,
        )
        product = (product * scale).astype(jnp.bfloat16)
        for i in range(per):
            for c in range(2):
                low = (2 * i + c) * rows
                out_ref[i, c, :, at : at + 256] = product[low : low + rows]

    @pl.when(step == 0)
    def _():
        edge = (TAPS - 1) * count
        bank_ref[:edge, :] = jnp.zeros((edge, 2 * NCH), jnp.bfloat16)
        end = edge + spectra_n * count
        bank_ref[end:, :] = jnp.zeros((bank_ref.shape[0] - end, 2 * NCH), jnp.bfloat16)
        for u in range(0, spectra_n // 4, 2):
            tiles = [
                beams_ref[c, e, u * tile : (u + 2) * tile, :].astype(jnp.float32)
                for c in range(n_chan)
                for e in range(n_grp)
            ]
            for v in range(2):
                stack = jnp.concatenate([t[v * tile : (v + 1) * tile] for t in tiles], axis=0)
                at = edge + (u + v) * 4 * count
                bank_ref[at : at + 4 * count, :] = stack.T.astype(jnp.bfloat16)

    @pl.when(step == 1)
    def _():
        trig = trig_of((2 * NCH, 2 * NCH), n_grp)
        for k in range(TAPS):
            taps = taps_ref[k : k + 1, :]
            table_ref[k] = (trig * jnp.concatenate([taps, taps], axis=1)).astype(jnp.bfloat16)

    run = 4
    chunk = step - 2

    @pl.when((chunk >= 0) & (chunk * run < frames_n))
    def _():
        acc = jnp.zeros((run * count, 2 * NCH), jnp.float32)
        for k in range(TAPS):
            start = pl.multiple_of((chunk * run - k + TAPS - 1) * count, count)
            acc = acc + jnp.dot(
                bank_ref[pl.ds(start, run * count), :],
                table_ref[k],
                preferred_element_type=jnp.float32,
            )
        for j in range(run):

            @pl.when(chunk * run + j < frames_n)
            def _():
                at = pl.multiple_of((chunk * run + j) * NCH, NCH)
                for c in range(2):
                    voice_ref[:, c, pl.ds(at, NCH)] = acc[
                        j * count : (j + 1) * count, c * NCH : (c + 1) * NCH
                    ]


def back(by_id, beams, taps, counts, sub_index, rows, count):
    n_grp, inputs, lanes = by_id.shape
    n_chan = beams.shape[0]
    beams = beams.reshape((n_chan, n_grp) + beams.shape[3:])
    spectra_n = BLOCKS * SPEC
    frames_n = spectra_n + TAPS - 1
    per = 2
    split = QUAD // per
    fixed = lambda shape: pl.BlockSpec(
        shape, lambda g, p, s: (0,) * len(shape), pipeline_mode=pl.Buffered(1)
    )
    return pl.pallas_call(
        functools.partial(back_kernel, per),
        grid_spec=pltpu.PrefetchScalarGridSpec(
            num_scalar_prefetch=1,
            grid=(n_grp, split),
            in_specs=[
                pl.BlockSpec(memory_space=pltpu.SMEM),
                pl.BlockSpec((1, rows, lanes), lambda g, p, s: (g, s[0], 0)),
                pl.BlockSpec((1, inputs, lanes), lambda g, p, s: (g, 0, 0)),
                fixed(beams.shape),
                fixed(taps.shape),
            ],
            out_specs=[
                pl.BlockSpec((per, 2, rows, inputs), lambda g, p, s: (g * split + p, 0, 0, 0)),
                fixed((count, 2, frames_n * NCH)),
            ],
            scratch_shapes=[
                pltpu.VMEM((rows, lanes), jnp.bfloat16),
                pltpu.VMEM(((spectra_n + 2 * TAPS) * count, 2 * NCH), jnp.bfloat16),
                pltpu.VMEM((TAPS, 2 * NCH, 2 * NCH), jnp.bfloat16),
            ],
        ),
        out_shape=[
            jax.ShapeDtypeStruct((n_grp * QUAD, 2, rows, inputs), jnp.bfloat16),
            jax.ShapeDtypeStruct((count, 2, frames_n * NCH), jnp.float32),
        ],
        compiler_params=pltpu.CompilerParams(dimension_semantics=("arbitrary", "arbitrary")),
        name="back",
    )(sub_index, counts, by_id, by_id, beams, taps)


def local(voltages, taps, input_id, counts, delays, beam_owner):
    n_chan = lax.axis_size("chan")
    n_sub = lax.axis_size("sub")
    inp_dev = voltages.shape[0]
    inputs = input_id.shape[0]
    spectra_n = BLOCKS * SPEC
    ch_dev = NCH // n_chan
    rows = inputs // n_sub
    section = BEAMS // n_sub
    most = min(section, max(2, 2 * section // n_chan))
    fits = inp_dev == 64 and most == 32 and section == 64 and NCH == 128
    fits = fits and n_sub % 2 == 0 and ch_dev % (2 * QUAD) == 0 and inputs % 512 == 0
    if not fits or 4 * ch_dev * QUAD < 11 + 2 * QUAD or rows % 128:
        return local_plain(voltages, taps, input_id, counts, delays, beam_owner)
    sub_index = lax.axis_index("sub")
    frames = voltages.reshape(inp_dev, 2, spectra_n + TAPS - 1, NCH)
    frames = jnp.transpose(frames, (1, 2, 0, 3))
    swapped = input_id.reshape(-1, 2, inp_dev)[:, ::-1].reshape(inputs)
    names = jnp.stack([input_id, swapped])
    owner = lax.dynamic_slice_in_dim(beam_owner[:, 0], sub_index * section, section)
    beam = jnp.arange(section, dtype=jnp.int32)
    earlier = (owner[None, :] == owner[:, None]) & (beam[None, :] < beam[:, None])
    rank = jnp.sum(earlier.astype(jnp.int32), axis=1)
    slots = (owner * (4 * most) + rank)[:, None]
    taps2 = taps.reshape(TAPS, NCH)
    by_id, beams = front(frames, taps2, counts, names, delays, slots, n_chan, n_sub, most)
    visibility, resynth = back(
        by_id, beams, taps2, counts, sub_index.astype(jnp.int32)[None], rows, most
    )
    return (visibility, resynth)


def solution(mesh):
    placed = (
        P(("grp", "chan", "sub"), None, None),
        P(),
        P(),
        P("grp"),
        P(("grp", "sub"), None),
        P("grp", None),
    )
    return jax.shard_map(
        local,
        mesh=mesh,
        in_specs=placed,
        out_specs=(P(("grp", "chan"), None, "sub", None), P(("grp", "chan", "sub"), None, None)),
        check_vma=False,
    )
```

```python
import functools
import math

import jax
import jax.numpy as jnp
from jax import lax
from jax.experimental import pallas as pl
from jax.experimental.pallas import tpu as pltpu
from jax.sharding import PartitionSpec as P

NCH = 128
TAPS = 12
SPEC = 8
BLOCKS = 4
BEAMS = 256


def filter_table(taps, chans):
    length = taps.shape[0]
    position = jnp.arange(length, dtype=jnp.int32) % chans
    channel = jnp.arange(chans, dtype=jnp.int32)
    phase = (position[:, None] * channel[None, :] % chans).astype(jnp.float32) * (
        2.0 * math.pi / chans
    )
    cosine = taps[:, None] * jnp.cos(phase)
    sine = taps[:, None] * jnp.sin(phase)
    upper = jnp.concatenate([cosine, -sine], axis=1)
    lower = jnp.concatenate([sine, cosine], axis=1)
    return jnp.concatenate([upper, lower], axis=0).astype(jnp.bfloat16)


def resynthesize(received, table, taps_count, chans):
    count = received.shape[0]
    spectra_n = received.shape[3]
    table3 = table.reshape(2 * taps_count * chans, 2, chans)
    grid = jnp.einsum("pcht,mch->ptm", received, table3, preferred_element_type=jnp.float32)
    grid = grid.reshape(count, spectra_n, 2, taps_count, chans)
    total = jnp.zeros((count, spectra_n + taps_count - 1, 2, chans), jnp.float32)
    for k in range(taps_count):
        total = total + jnp.pad(
            grid[:, :, :, k, :], ((0, 0), (k, taps_count - 1 - k), (0, 0), (0, 0))
        )
    return jnp.transpose(total, (0, 2, 1, 3)).reshape(
        count, 2, (spectra_n + taps_count - 1) * chans
    )


def local_plain(voltages, taps, input_id, counts, delays, beam_owner):
    n_chan = lax.axis_size("chan")
    n_sub = lax.axis_size("sub")
    inp_dev = voltages.shape[0]
    inputs = input_id.shape[0]
    chans = NCH
    taps_count = TAPS
    spectra_n = BLOCKS * SPEC
    ch_dev = chans // n_chan
    rows = inputs // n_sub
    section = BEAMS // n_sub
    most = min(section, max(2, 2 * section // n_chan))
    table = filter_table(taps, chans)
    position = jnp.arange(spectra_n, dtype=jnp.int32)
    valid = (position % SPEC < jnp.repeat(counts, SPEC)).astype(jnp.float32)
    total = jnp.sum(counts.astype(jnp.float32))
    frames = voltages.reshape(inp_dev, 2, spectra_n + taps_count - 1, chans)
    windows = jnp.concatenate(
        [frames[:, :, k : k + spectra_n, :] for k in range(taps_count)], axis=3
    )
    table3 = table.reshape(2, taps_count * chans, 2 * chans)
    filtered = jnp.einsum("icth,chm->mit", windows, table3, preferred_element_type=jnp.float32)
    filtered = filtered * valid[None, None, :]
    spectra = filtered.reshape(2, chans, inp_dev, spectra_n).astype(jnp.bfloat16)
    slot_of = jnp.zeros((inputs,), jnp.int32).at[input_id].set(jnp.arange(inputs, dtype=jnp.int32))
    turned = lax.all_to_all(spectra, "chan", split_axis=1, concat_axis=2, tiled=True)
    gathered = lax.all_gather(turned, "sub", axis=2, tiled=True)
    chan_part = slot_of // (n_sub * inp_dev)
    sub_part = slot_of // inp_dev % n_sub
    order = (sub_part * n_chan + chan_part) * inp_dev + slot_of % inp_dev
    by_id = jnp.take(gathered, order, axis=2)
    sub_index = lax.axis_index("sub")
    mine = lax.dynamic_slice_in_dim(by_id, sub_index * rows, rows, 2)
    real_part = jnp.einsum("cxit,cxjt->xij", mine, by_id, preferred_element_type=jnp.float32)
    imag_part = jnp.einsum("xit,xjt->xij", mine[1], by_id[0], preferred_element_type=jnp.float32)
    imag_part = imag_part - jnp.einsum(
        "xit,xjt->xij", mine[0], by_id[1], preferred_element_type=jnp.float32
    )
    visibility = (jnp.stack([real_part, imag_part], axis=1) / total).astype(jnp.bfloat16)
    channel = lax.axis_index("chan") * ch_dev + jnp.arange(ch_dev, dtype=jnp.int32)
    phase = (delays[None, :, :] * channel[:, None, None] % chans).astype(jnp.float32) * (
        2.0 * math.pi / chans
    )
    scale = 1.0 / math.sqrt(inputs)
    weight_cos = (jnp.cos(phase) * scale).astype(jnp.bfloat16)
    weight_sin = (jnp.sin(phase) * scale).astype(jnp.bfloat16)
    from_cos = jnp.einsum("xbi,cxit->cxbt", weight_cos, by_id, preferred_element_type=jnp.float32)
    from_sin = jnp.einsum("xbi,cxit->cxbt", weight_sin, by_id, preferred_element_type=jnp.float32)
    beams = jnp.stack([from_cos[0] - from_sin[1], from_cos[1] + from_sin[0]]).astype(jnp.bfloat16)
    owner = lax.dynamic_slice_in_dim(beam_owner[:, 0], sub_index * section, section)
    beam = jnp.arange(section, dtype=jnp.int32)
    earlier = (owner[None, :] == owner[:, None]) & (beam[None, :] < beam[:, None])
    rank = jnp.sum(earlier.astype(jnp.int32), axis=1)
    target = owner * most + rank
    select = (jnp.arange(n_chan * most, dtype=jnp.int32)[:, None] == target[None, :]).astype(
        jnp.bfloat16
    )
    placed = jnp.einsum("pb,cxbt->pcxt", select, beams, preferred_element_type=jnp.float32).astype(
        jnp.bfloat16
    )
    placed = placed.reshape(n_chan, most, 2, ch_dev, spectra_n)
    resynth = resynthesize(
        lax.all_to_all(placed, "chan", split_axis=0, concat_axis=3, tiled=True)[0],
        table,
        taps_count,
        chans,
    )
    return (visibility, resynth)


def turn_of(steps):
    quarter = NCH // 4
    turn = steps & (NCH - 1)
    quadrant = (turn + quarter // 2) >> (quarter.bit_length() - 1)
    x = (turn - quadrant * quarter).astype(jnp.float32) * (2.0 * math.pi / NCH)
    y = x * x
    even = 1.0 + y * (-1 / 2 + y * (1 / 24 + y * (-1 / 720 + y * (1 / 40320))))
    odd = x * (1.0 + y * (-1 / 6 + y * (1 / 120 + y * (-1 / 5040 + y * (1 / 362880)))))
    swap = (quadrant & 1) == 1
    cosine, sine = jnp.where(swap, odd, even), jnp.where(swap, even, odd)
    cosine = jnp.where(((quadrant + 1) & 2) == 2, -cosine, cosine)
    return cosine, jnp.where((quadrant & 2) == 2, -sine, sine)


def weigh(first, scale, delay_ref, out_ref, at, left, high, wide):
    beams_n = delay_ref.shape[0]
    delay = delay_ref[at : at + high, left : left + wide]
    step_cos, step_sin = turn_of(delay)
    cosine, sine = turn_of(delay * first)

    def body(f, held):
        cosine, sine = held
        out_ref[f, at : at + high, left : left + wide] = cosine.astype(jnp.bfloat16)
        low = at + beams_n
        out_ref[f, low : low + high, left : left + wide] = sine.astype(jnp.bfloat16)
        return (
            cosine * step_cos - sine * step_sin,
            sine * step_cos + cosine * step_sin,
        )

    lax.fori_loop(0, out_ref.shape[0], body, (cosine * scale, sine * scale))


QUAD = 4
VOICES = 8


def trig_of(shape, n_grp):
    row = lax.broadcasted_iota(jnp.int32, shape, 0)
    lane = lax.broadcasted_iota(jnp.int32, shape, 1)
    tile = 2 * QUAD
    part = row // QUAD % 2
    channel = row // tile * QUAD + row % QUAD
    to_part = lane // NCH
    cosine, sine = turn_of(channel * (lane % NCH))
    return jnp.where(part == to_part, cosine, jnp.where(to_part == 1, sine, -sine))


def partner(x, lanes):
    pieces = [x[:, at : at + 128] for at in range(0, lanes, 128)]
    after = jnp.concatenate([pltpu.roll(p, 128 - QUAD, 1) for p in pieces], axis=1)
    before = jnp.concatenate([pltpu.roll(p, QUAD, 1) for p in pieces], axis=1)
    lane = lax.broadcasted_iota(jnp.int32, x.shape, 1)
    return lane // QUAD % 2 == 0, after, before


def front_kernel(
    n_chan, n_sub, most,
    volt_ref, taps_ref, counts_ref, name_ref, delay_ref, owner_ref,
    sorted_ref, beams_ref,
    v_ref, late_ref, x_ref, g_ref, y_ref, d_ref, perm_ref, turn_ref, c_ref, held, weight_ref,
    place_ref, ready,
    load_sem, own_sem, out_sem, keep_sem, zs, zr, xs, xr, cs, cr, es, er,
):
    me_c, me_s = lax.axis_index("chan"), lax.axis_index("sub")
    core, across = me_s % 2, me_s // 2
    n_x = n_sub // 2
    twin = me_s + 1 - 2 * core
    mesh_id = pl.DeviceIdType.MESH
    pieces, per = x_ref.shape[1], x_ref.shape[2]
    n_grp = pieces * per
    spectra_n = BLOCKS * SPEC
    frames_n, rows = v_ref.shape[:2]
    inputs = name_ref.shape[1]
    beams_n = delay_ref.shape[0]
    ch_dev = n_grp * QUAD
    tile = 2 * QUAD
    wide = 2 * NCH
    block = x_ref.shape[3]

    def chan_of(offset):
        return (me_c + offset) % n_chan

    def sub_of(offset):
        return (across + offset) % n_x * 2 + core

    barrier = pltpu.get_barrier_semaphore()
    for j in range(1, n_chan):
        pl.semaphore_signal(barrier, device_id={"chan": chan_of(j)}, device_id_type=mesh_id)
    for j in range(1, n_x):
        pl.semaphore_signal(barrier, device_id={"sub": sub_of(j)}, device_id_type=mesh_id)
    pl.semaphore_signal(barrier, device_id={"sub": twin}, device_id_type=mesh_id)

    for s in range(frames_n):
        pltpu.make_async_copy(
            volt_ref.at[:, :, pl.ds(s * NCH, NCH)], v_ref.at[s], load_sem
        ).start()

    def z_copy(j, q):
        return pltpu.make_async_remote_copy(
            src_ref=x_ref.at[chan_of(j), q],
            dst_ref=g_ref.at[q, me_c, me_s],
            send_sem=zs,
            recv_sem=zr.at[j - 1, q],
            device_id={"chan": chan_of(j)},
            device_id_type=mesh_id,
        )

    def source(j, q):
        if j == 0:
            return x_ref.at[me_c, q]
        return g_ref.at[q, chan_of(n_chan - j), me_s]

    def x_copy(dx, j, q):
        return pltpu.make_async_remote_copy(
            src_ref=source(j, q),
            dst_ref=g_ref.at[q, chan_of(n_chan - j), me_s],
            send_sem=xs,
            recv_sem=xr.at[dx - 1, j, q],
            device_id={"sub": sub_of(dx)},
            device_id_type=mesh_id,
        )

    def core_copy(dx, j, q):
        home = g_ref.at[q, chan_of(n_chan - j), sub_of(n_x - dx)]
        return pltpu.make_async_remote_copy(
            src_ref=source(j, q) if dx == 0 else home,
            dst_ref=home,
            send_sem=cs,
            recv_sem=cr.at[q],
            device_id={"sub": twin},
            device_id_type=mesh_id,
        )

    def beam_copy(j, q):
        return pltpu.make_async_remote_copy(
            src_ref=ready.at[chan_of(j), q],
            dst_ref=beams_ref.at[me_c, q],
            send_sem=es,
            recv_sem=er,
            device_id={"chan": chan_of(j)},
            device_id_type=mesh_id,
        )

    trig = trig_of((n_chan * n_grp * tile, wide), n_grp)
    high = trig.astype(jnp.bfloat16)
    d_ref[:, :wide] = high
    d_ref[:, wide:] = (trig - high.astype(jnp.float32)).astype(jnp.bfloat16)

    valid = []
    for t in range(spectra_n):
        valid.append(jnp.where(counts_ref[t // SPEC] > t % SPEC, 1.0, 0.0))
    step = 16
    run = 4
    pltpu.make_async_copy(v_ref, v_ref, load_sem).wait()

    @pl.loop(0, rows // step)
    def _(it):
        at = pl.multiple_of(it * step, step)
        taps = [taps_ref[k : k + 1, :] for k in range(TAPS)]
        for h in range(2):
            for first in range(0, spectra_n, run):
                window = [
                    v_ref[s, pl.ds(at + h * (step // 2), step // 2)]
                    .reshape(step, NCH)
                    .astype(jnp.float32)
                    for s in range(first, first + run + TAPS - 1)
                ]
                for j in range(run):
                    t = first + j
                    total = window[j] * taps[0]
                    for k in range(1, TAPS):
                        total = total + window[j + k] * taps[k]
                    late_ref[t, h * step : (h + 1) * step, :] = total * valid[t]
        for t in range(spectra_n):
            slot = t // 2 * 2 + (t % 2 + core) % 2
            to = pl.multiple_of(slot * rows + at, step)
            for c in range(2):
                total = late_ref[t, pl.ds(c, step, stride=2), :]
                high = total.astype(jnp.bfloat16)
                low = (total - high.astype(jnp.float32)).astype(jnp.bfloat16)
                y_ref[pl.ds(to, step), c * NCH : (c + 1) * NCH] = high
                y_ref[pl.ds(to, step), wide + c * NCH : wide + (c + 1) * NCH] = low

    across_dims = (((1,), (1,)), ((), ()))

    @pl.loop(0, spectra_n // 4)
    def _(u):
        at = pl.multiple_of(u * 4 * rows, 4 * rows)
        high = y_ref[pl.ds(at, 4 * rows), :wide]
        low = y_ref[pl.ds(at, 4 * rows), wide:]
        out = lax.dot_general(d_ref[:, :wide], high, across_dims, preferred_element_type=jnp.float32)
        out = out + lax.dot_general(
            d_ref[:, wide:], high, across_dims, preferred_element_type=jnp.float32
        )
        out = out + lax.dot_general(
            d_ref[:, :wide], low, across_dims, preferred_element_type=jnp.float32
        )
        to = pl.multiple_of(u * 2 * tile, 2 * tile)
        for d in range(n_chan):
            for q in range(pieces):
                for e in range(per):
                    row = ((d * pieces + q) * per + e) * tile
                    both = jnp.concatenate(
                        [out[row : row + tile, :128], out[row : row + tile, 128:]], axis=0
                    )
                    x_ref[d, q, e, pl.ds(to, 2 * tile), :] = both.astype(jnp.bfloat16)

    pl.semaphore_wait(barrier, n_chan + n_x - 1)
    def spread(j, q):
        for dx in range(1, n_x):
            x_copy(dx, j, q).start()
        core_copy(0, j, q).start()

    for q in range(pieces):
        for j in range(1, n_chan):
            z_copy(j, q).start()
    for q in range(pieces):
        spread(0, q)
    for q in range(pieces):
        pltpu.make_async_copy(x_ref.at[me_c, q], g_ref.at[q, me_c, me_s], keep_sem).start()

    half = inputs // 4
    first = me_c * ch_dev
    scale = 1.0 / math.sqrt(inputs)

    def name_unit(m):
        def run_unit():
            low = lax.broadcasted_iota(jnp.int32, (half, inputs), 0) + m * half
            perm_ref[m * half : (m + 1) * half, :] = jnp.where(
                name_ref[...] == low, 1.0, 0.0
            ).astype(jnp.bfloat16)

        return run_unit

    def turn_unit():
        turned = jnp.dot(
            delay_ref[...].astype(jnp.float32).astype(jnp.bfloat16),
            perm_ref[...],
            preferred_element_type=jnp.float32,
        )
        turn_ref[...] = turned.astype(jnp.int32)

    def weigh_unit(at, left):
        return lambda: weigh(first, scale, turn_ref, weight_ref, at, left, 16, 512)

    def place_unit():
        lanes = per * beams_n
        owner = jnp.concatenate([owner_ref[...]] * per, axis=1)
        named = (lax.broadcasted_iota(jnp.int32, (8, lanes), 0) == owner).astype(jnp.float32)
        row = lax.broadcasted_iota(jnp.int32, (lanes, lanes), 0)
        lane = lax.broadcasted_iota(jnp.int32, (lanes, lanes), 1)
        before = (row < lane) & (row // beams_n == lane // beams_n)
        rank = jnp.dot(
            named.astype(jnp.bfloat16),
            jnp.where(before, 1.0, 0.0).astype(jnp.bfloat16),
            preferred_element_type=jnp.float32,
        )
        rank = jnp.sum(named * rank, axis=0, keepdims=True).astype(jnp.int32)
        lane = lax.broadcasted_iota(jnp.int32, (1, lanes), 1)
        slot = (lane // beams_n * n_chan + owner) * (4 * most) + rank
        row = lax.broadcasted_iota(jnp.int32, (place_ref.shape[0], lanes), 0)
        for m in range(4):
            place_ref[:, m * lanes : (m + 1) * lanes] = jnp.where(
                row == slot + m * most, 1.0, 0.0
            ).astype(jnp.bfloat16)

    def join_unit(q):
        def run_unit():
            left = lax.broadcasted_iota(jnp.int32, (block, 128), 1) < 64
            for e in range(per):
                low = 2 * e * block
                for c in range(n_chan):
                    for x in range(n_x):
                        a = g_ref[q, c, 2 * x, e].astype(jnp.float32)
                        b = g_ref[q, c, 2 * x + 1, e].astype(jnp.float32)
                        at = (c * n_x + x) * 128
                        c_ref[low : low + block, at : at + 128] = jnp.where(left, a, b).astype(
                            jnp.bfloat16
                        )
                        c_ref[low + block : low + 2 * block, at : at + 128] = pltpu.roll(
                            jnp.where(left, b, a), 64, 1
                        ).astype(jnp.bfloat16)

        return run_unit

    def sort_unit(q, e, m):
        def run_unit():
            held[q * per + e, m * half : (m + 1) * half, :] = lax.dot_general(
                perm_ref[m * half : (m + 1) * half, :],
                c_ref[2 * e * block : 2 * (e + 1) * block, :],
                across_dims,
                preferred_element_type=jnp.float32,
            ).astype(jnp.bfloat16)

        return run_unit

    mixes = {}

    def mix_unit(q, e):
        def run_unit():
            at = q * per + e
            lane = lax.broadcasted_iota(jnp.int32, (2 * beams_n, 2 * block), 1)
            total = None
            for f in range(QUAD):
                mixed = lax.dot_general(
                    weight_ref[at * QUAD + f],
                    c_ref[2 * e * block : 2 * (e + 1) * block, :],
                    across_dims,
                    preferred_element_type=jnp.float32,
                )
                total = mixed if total is None else jnp.where(lane % QUAD == f, mixed, total)
            real, after, before = partner(total[beams_n:], 2 * block)
            mixes[q, e] = total[:beams_n] + jnp.where(real, -after, before)

        return run_unit

    def place_beams(q):
        def run_unit():
            both = jnp.concatenate([mixes.pop((q, e)) for e in range(per)], axis=0)
            turned = both.T
            parts = []
            for m in range(4):
                parity, u = m % 2, m // 2
                picks = [
                    turned[parity * block + v * 2 * tile + u * tile :][:tile]
                    for v in range(spectra_n // 4)
                ]
                parts.append(jnp.concatenate(picks, axis=0))
            lined = jnp.concatenate(parts, axis=1).astype(jnp.bfloat16)
            out = lax.dot_general(
                lined, place_ref[...], across_dims, preferred_element_type=jnp.float32
            ).astype(jnp.bfloat16)
            for e in range(per):
                for d in range(n_chan):
                    at = (e * n_chan + d) * 128
                    ready[d, q, e] = out[:, at : at + 128]
            for j in range(1, n_chan):
                beam_copy(j, q).start()
            pltpu.make_async_copy(ready.at[me_c, q], beams_ref.at[me_c, q], own_sem).start()

        return run_unit

    def store_unit(q):
        def run_unit():
            part = pl.ds(q * per, per)
            pltpu.make_async_copy(held.at[part], sorted_ref.at[part], out_sem).start()

        return run_unit

    def units_of(q):
        units = [join_unit(q)] + [mix_unit(q, e) for e in range(per)] + [place_beams(q)]
        units += [sort_unit(q, e, m) for e in range(per) for m in range(4)]
        return units + [store_unit(q)]

    def z_step(j, q):
        def run_step():
            z_copy(j, q).wait_recv()
            spread(j, q)

        return run_step

    def x_step(j, q):
        for dx in range(1, n_x):
            x_copy(dx, j, q).wait_recv()
            core_copy(dx, j, q).start()

    def weave(units, steps):
        done = 0
        for i, one in enumerate(steps):
            upto = len(units) * (i + 1) // len(steps)
            for unit in units[done:upto]:
                unit()
            done = upto
            one()
        for unit in units[done:]:
            unit()

    def arrive(q):
        if q == 0:
            pltpu.make_async_copy(x_ref.at[me_c], g_ref.at[:, me_c, me_s], keep_sem).wait()
        part = g_ref.at[q, pl.ds(0, n_chan // 2)]
        pltpu.make_async_copy(part, part, cr.at[q]).wait()

    setup = [name_unit(m) for m in range(4)] + [turn_unit]
    setup += [
        weigh_unit(at, left) for at in range(0, beams_n, 16) for left in range(0, inputs, 512)
    ]
    setup.append(place_unit)
    weave(setup, [z_step(j, 0) for j in range(1, n_chan)])
    for q in range(1, pieces + 1):
        for j in range(n_chan):
            x_step(j, q - 1)
        arrive(q - 1)
        steps = [z_step(j, q) for j in range(1, n_chan)] if q < pieces else []
        weave(units_of(q - 1), steps)
    others = pl.ds(0, n_chan - 1)
    pltpu.make_async_copy(ready.at[others], beams_ref.at[others], er).wait()
    pltpu.make_async_copy(x_ref.at[others], x_ref.at[others], zs).wait()
    for dx in range(1, n_x):
        pltpu.make_async_copy(x_ref, x_ref, xs).wait()
    part = g_ref.at[pl.ds(0, pieces // 2)]
    pltpu.make_async_copy(part, part, cs).wait()
    pltpu.make_async_copy(ready.at[others], ready.at[others], es).wait()
    pltpu.make_async_copy(ready.at[me_c], beams_ref.at[me_c], own_sem).wait()
    pltpu.make_async_copy(held, sorted_ref, out_sem).wait()


def front(voltages, taps, counts, names, delays, owner, n_chan, n_sub, most):
    rows = voltages.shape[0]
    beams_n, inputs = delays.shape
    spectra_n = BLOCKS * SPEC
    ch_dev = NCH // n_chan
    n_grp = ch_dev // QUAD
    per = 2
    pieces = n_grp // per
    n_x = n_sub // 2
    tile = 2 * QUAD
    block = spectra_n // 2 * tile
    dma = pltpu.SemaphoreType.DMA
    vmem = pl.BlockSpec(memory_space=pltpu.VMEM)
    travel = (n_chan, pieces, per, spectra_n // 4 * tile, 128)
    return pl.pallas_call(
        functools.partial(front_kernel, n_chan, n_sub, most),
        in_specs=[
            pl.BlockSpec(memory_space=pl.ANY),
            vmem,
            pl.BlockSpec(memory_space=pltpu.SMEM),
            vmem,
            vmem,
            vmem,
        ],
        out_specs=[pl.BlockSpec(memory_space=pl.ANY)] * 2,
        out_shape=[
            jax.ShapeDtypeStruct((n_grp, inputs, 2 * block), jnp.bfloat16),
            jax.ShapeDtypeStruct(travel, jnp.bfloat16),
        ],
        scratch_shapes=[
            pltpu.VMEM((spectra_n + TAPS - 1, rows, 2, NCH), jnp.bfloat16),
            pltpu.VMEM((spectra_n, 32, NCH), jnp.float32),
            pltpu.VMEM((n_chan, pieces, per, block, 128), jnp.bfloat16),
            pltpu.VMEM((pieces, n_chan, n_sub, per, block, 128), jnp.bfloat16),
            pltpu.VMEM((spectra_n * rows, 4 * NCH), jnp.bfloat16),
            pltpu.VMEM((2 * NCH, 4 * NCH), jnp.bfloat16),
            pltpu.VMEM((inputs, inputs), jnp.bfloat16),
            pltpu.VMEM((beams_n, inputs), jnp.int32),
            pltpu.VMEM((2 * per * block, inputs), jnp.bfloat16),
            pltpu.VMEM((n_grp, inputs, 2 * block), jnp.bfloat16),
            pltpu.VMEM((ch_dev, 2 * beams_n, inputs), jnp.bfloat16),
            pltpu.VMEM((per * n_chan * 128, 4 * per * beams_n), jnp.bfloat16),
            pltpu.VMEM(travel, jnp.bfloat16),
            dma,
            dma,
            dma,
            dma,
            dma,
            dma((n_chan - 1, pieces)),
            dma,
            dma((n_x - 1, n_chan, pieces)),
            dma,
            dma((pieces,)),
            dma,
            dma,
        ],
        compiler_params=pltpu.CompilerParams(collective_id=0, has_side_effects=True),
        name="front",
    )(voltages, taps, counts, names, delays, owner)


def back_kernel(
    sub_ref, counts_ref, mine_ref, all_ref, beams_ref, taps_ref,
    out_ref, voice_ref,
    left_ref, bank_ref, table_ref,
):
    g, part = pl.program_id(0), pl.program_id(1)
    step = g * pl.num_programs(1) + part
    rows, lanes = mine_ref.shape[1], mine_ref.shape[2]
    span = all_ref.shape[1]
    count, _, samples = voice_ref.shape
    frames_n = samples // NCH
    spectra_n = frames_n - TAPS + 1
    n_chan, n_grp = beams_ref.shape[0], beams_ref.shape[1]
    tile = 2 * QUAD
    total = counts_ref[0]
    for i in range(1, BLOCKS):
        total = total + counts_ref[i]
    scale = 1.0 / jnp.full((8, 128), total.astype(jnp.float32))
    scale = scale[:1, :1]

    @pl.when(part == 0)
    def _():
        plain = mine_ref[0].astype(jnp.float32)
        real, after, before = partner(plain, lanes)
        turned = jnp.where(real, after, -before)
        lane = lax.broadcasted_iota(jnp.int32, (rows, lanes), 1) % QUAD
        for i in range(QUAD):
            at = 2 * i * rows
            left_ref[at : at + rows, :] = jnp.where(lane == i, plain, 0.0).astype(jnp.bfloat16)
            left_ref[at + rows : at + 2 * rows, :] = jnp.where(lane == i, turned, 0.0).astype(
                jnp.bfloat16
            )

    for at in range(0, span, 256):
        product = lax.dot_general(
            left_ref[...],
            all_ref[0, at : at + 256, :],
            (((1,), (1,)), ((), ())),
            preferred_element_type=jnp.float32,
        )
        product = (product * scale).astype(jnp.bfloat16)
        for i in range(QUAD):
            for c in range(2):
                low = (2 * i + c) * rows
                out_ref[i, c, :, at : at + 256] = product[low : low + rows]

    @pl.when(step == 0)
    def _():
        edge = (TAPS - 1) * count
        bank_ref[:edge, :] = jnp.zeros((edge, 2 * NCH), jnp.bfloat16)
        end = edge + spectra_n * count
        bank_ref[end:, :] = jnp.zeros((bank_ref.shape[0] - end, 2 * NCH), jnp.bfloat16)
        for u in range(0, spectra_n // 4, 2):
            tiles = [
                beams_ref[c, e, u * tile : (u + 2) * tile, :].astype(jnp.float32)
                for c in range(n_chan)
                for e in range(n_grp)
            ]
            for v in range(2):
                stack = jnp.concatenate([t[v * tile : (v + 1) * tile] for t in tiles], axis=0)
                at = edge + (u + v) * 4 * count
                bank_ref[at : at + 4 * count, :] = stack.T.astype(jnp.bfloat16)

    @pl.when(step == 1)
    def _():
        trig = trig_of((2 * NCH, 2 * NCH), n_grp)
        for k in range(TAPS):
            taps = taps_ref[k : k + 1, :]
            table_ref[k] = (trig * jnp.concatenate([taps, taps], axis=1)).astype(jnp.bfloat16)

    run = VOICES
    chunk = step - 2

    @pl.when((chunk >= 0) & (chunk * run < frames_n))
    def _():
        acc = jnp.zeros((run * count, 2 * NCH), jnp.float32)
        for k in range(TAPS):
            start = pl.multiple_of((chunk * run - k + TAPS - 1) * count, count)
            acc = acc + jnp.dot(
                bank_ref[pl.ds(start, run * count), :],
                table_ref[k],
                preferred_element_type=jnp.float32,
            )
        for j in range(run):

            @pl.when(chunk * run + j < frames_n)
            def _():
                at = pl.multiple_of((chunk * run + j) * NCH, NCH)
                for c in range(2):
                    voice_ref[:, c, pl.ds(at, NCH)] = acc[
                        j * count : (j + 1) * count, c * NCH : (c + 1) * NCH
                    ]


def back(by_id, beams, taps, counts, sub_index, rows, count):
    n_grp, inputs, lanes = by_id.shape
    n_chan = beams.shape[0]
    beams = beams.reshape((n_chan, n_grp) + beams.shape[3:])
    spectra_n = BLOCKS * SPEC
    frames_n = spectra_n + TAPS - 1
    split = 2
    span = inputs // split
    fixed = lambda shape: pl.BlockSpec(
        shape, lambda g, p, s: (0,) * len(shape), pipeline_mode=pl.Buffered(1)
    )
    return pl.pallas_call(
        back_kernel,
        grid_spec=pltpu.PrefetchScalarGridSpec(
            num_scalar_prefetch=1,
            grid=(n_grp, split),
            in_specs=[
                pl.BlockSpec(memory_space=pltpu.SMEM),
                pl.BlockSpec((1, rows, lanes), lambda g, p, s: (g, s[0], 0)),
                pl.BlockSpec((1, span, lanes), lambda g, p, s: (g, p, 0)),
                fixed(beams.shape),
                fixed(taps.shape),
            ],
            out_specs=[
                pl.BlockSpec((QUAD, 2, rows, span), lambda g, p, s: (g, 0, 0, p)),
                fixed((count, 2, frames_n * NCH)),
            ],
            scratch_shapes=[
                pltpu.VMEM((2 * QUAD * rows, lanes), jnp.bfloat16),
                pltpu.VMEM(((frames_n + VOICES + TAPS) * count, 2 * NCH), jnp.bfloat16),
                pltpu.VMEM((TAPS, 2 * NCH, 2 * NCH), jnp.bfloat16),
            ],
        ),
        out_shape=[
            jax.ShapeDtypeStruct((n_grp * QUAD, 2, rows, inputs), jnp.bfloat16),
            jax.ShapeDtypeStruct((count, 2, frames_n * NCH), jnp.float32),
        ],
        compiler_params=pltpu.CompilerParams(dimension_semantics=("arbitrary", "arbitrary")),
        name="back",
    )(sub_index, counts, by_id, by_id, beams, taps)


def local(voltages, taps, input_id, counts, delays, beam_owner):
    n_chan = lax.axis_size("chan")
    n_sub = lax.axis_size("sub")
    inp_dev = voltages.shape[0]
    inputs = input_id.shape[0]
    spectra_n = BLOCKS * SPEC
    ch_dev = NCH // n_chan
    rows = inputs // n_sub
    section = BEAMS // n_sub
    most = min(section, max(2, 2 * section // n_chan))
    fits = inp_dev == 64 and most == 32 and section == 64 and NCH == 128
    fits = fits and n_sub % 2 == 0 and ch_dev % (2 * QUAD) == 0 and inputs % 512 == 0
    if not fits or n_sub != 4 or n_chan % 2 or n_chan > 8 or rows % 128:
        return local_plain(voltages, taps, input_id, counts, delays, beam_owner)
    sub_index = lax.axis_index("sub")
    owner = lax.dynamic_slice_in_dim(beam_owner[:, 0], sub_index * section, section)[None]
    taps2 = taps.reshape(TAPS, NCH)
    names = input_id[None]
    by_id, beams = front(voltages, taps2, counts, names, delays, owner, n_chan, n_sub, most)
    visibility, resynth = back(
        by_id, beams, taps2, counts, sub_index.astype(jnp.int32)[None], rows, most
    )
    return (visibility, resynth)


def solution(mesh):
    placed = (
        P(("grp", "chan", "sub"), None, None),
        P(),
        P(),
        P("grp"),
        P(("grp", "sub"), None),
        P("grp", None),
    )
    return jax.shard_map(
        local,
        mesh=mesh,
        in_specs=placed,
        out_specs=(P(("grp", "chan"), None, "sub", None), P(("grp", "chan", "sub"), None, None)),
        check_vma=False,
    )
```

```python
import functools
import math

import jax
import jax.numpy as jnp
from jax import lax
from jax.experimental import pallas as pl
from jax.experimental.pallas import tpu as pltpu
from jax.sharding import PartitionSpec as P

NCH = 128
TAPS = 12
SPEC = 8
BLOCKS = 4
BEAMS = 256


def filter_table(taps, chans):
    length = taps.shape[0]
    position = jnp.arange(length, dtype=jnp.int32) % chans
    channel = jnp.arange(chans, dtype=jnp.int32)
    phase = (position[:, None] * channel[None, :] % chans).astype(jnp.float32) * (
        2.0 * math.pi / chans
    )
    cosine = taps[:, None] * jnp.cos(phase)
    sine = taps[:, None] * jnp.sin(phase)
    upper = jnp.concatenate([cosine, -sine], axis=1)
    lower = jnp.concatenate([sine, cosine], axis=1)
    return jnp.concatenate([upper, lower], axis=0).astype(jnp.bfloat16)


def resynthesize(received, table, taps_count, chans):
    count = received.shape[0]
    spectra_n = received.shape[3]
    table3 = table.reshape(2 * taps_count * chans, 2, chans)
    grid = jnp.einsum("pcht,mch->ptm", received, table3, preferred_element_type=jnp.float32)
    grid = grid.reshape(count, spectra_n, 2, taps_count, chans)
    total = jnp.zeros((count, spectra_n + taps_count - 1, 2, chans), jnp.float32)
    for k in range(taps_count):
        total = total + jnp.pad(
            grid[:, :, :, k, :], ((0, 0), (k, taps_count - 1 - k), (0, 0), (0, 0))
        )
    return jnp.transpose(total, (0, 2, 1, 3)).reshape(
        count, 2, (spectra_n + taps_count - 1) * chans
    )


def local_plain(voltages, taps, input_id, counts, delays, beam_owner):
    n_chan = lax.axis_size("chan")
    n_sub = lax.axis_size("sub")
    inp_dev = voltages.shape[0]
    inputs = input_id.shape[0]
    chans = NCH
    taps_count = TAPS
    spectra_n = BLOCKS * SPEC
    ch_dev = chans // n_chan
    rows = inputs // n_sub
    section = BEAMS // n_sub
    most = min(section, max(2, 2 * section // n_chan))
    table = filter_table(taps, chans)
    position = jnp.arange(spectra_n, dtype=jnp.int32)
    valid = (position % SPEC < jnp.repeat(counts, SPEC)).astype(jnp.float32)
    total = jnp.sum(counts.astype(jnp.float32))
    frames = voltages.reshape(inp_dev, 2, spectra_n + taps_count - 1, chans)
    windows = jnp.concatenate(
        [frames[:, :, k : k + spectra_n, :] for k in range(taps_count)], axis=3
    )
    table3 = table.reshape(2, taps_count * chans, 2 * chans)
    filtered = jnp.einsum("icth,chm->mit", windows, table3, preferred_element_type=jnp.float32)
    filtered = filtered * valid[None, None, :]
    spectra = filtered.reshape(2, chans, inp_dev, spectra_n).astype(jnp.bfloat16)
    slot_of = jnp.zeros((inputs,), jnp.int32).at[input_id].set(jnp.arange(inputs, dtype=jnp.int32))
    turned = lax.all_to_all(spectra, "chan", split_axis=1, concat_axis=2, tiled=True)
    gathered = lax.all_gather(turned, "sub", axis=2, tiled=True)
    chan_part = slot_of // (n_sub * inp_dev)
    sub_part = slot_of // inp_dev % n_sub
    order = (sub_part * n_chan + chan_part) * inp_dev + slot_of % inp_dev
    by_id = jnp.take(gathered, order, axis=2)
    sub_index = lax.axis_index("sub")
    mine = lax.dynamic_slice_in_dim(by_id, sub_index * rows, rows, 2)
    real_part = jnp.einsum("cxit,cxjt->xij", mine, by_id, preferred_element_type=jnp.float32)
    imag_part = jnp.einsum("xit,xjt->xij", mine[1], by_id[0], preferred_element_type=jnp.float32)
    imag_part = imag_part - jnp.einsum(
        "xit,xjt->xij", mine[0], by_id[1], preferred_element_type=jnp.float32
    )
    visibility = (jnp.stack([real_part, imag_part], axis=1) / total).astype(jnp.bfloat16)
    channel = lax.axis_index("chan") * ch_dev + jnp.arange(ch_dev, dtype=jnp.int32)
    phase = (delays[None, :, :] * channel[:, None, None] % chans).astype(jnp.float32) * (
        2.0 * math.pi / chans
    )
    scale = 1.0 / math.sqrt(inputs)
    weight_cos = (jnp.cos(phase) * scale).astype(jnp.bfloat16)
    weight_sin = (jnp.sin(phase) * scale).astype(jnp.bfloat16)
    from_cos = jnp.einsum("xbi,cxit->cxbt", weight_cos, by_id, preferred_element_type=jnp.float32)
    from_sin = jnp.einsum("xbi,cxit->cxbt", weight_sin, by_id, preferred_element_type=jnp.float32)
    beams = jnp.stack([from_cos[0] - from_sin[1], from_cos[1] + from_sin[0]]).astype(jnp.bfloat16)
    owner = lax.dynamic_slice_in_dim(beam_owner[:, 0], sub_index * section, section)
    beam = jnp.arange(section, dtype=jnp.int32)
    earlier = (owner[None, :] == owner[:, None]) & (beam[None, :] < beam[:, None])
    rank = jnp.sum(earlier.astype(jnp.int32), axis=1)
    target = owner * most + rank
    select = (jnp.arange(n_chan * most, dtype=jnp.int32)[:, None] == target[None, :]).astype(
        jnp.bfloat16
    )
    placed = jnp.einsum("pb,cxbt->pcxt", select, beams, preferred_element_type=jnp.float32).astype(
        jnp.bfloat16
    )
    placed = placed.reshape(n_chan, most, 2, ch_dev, spectra_n)
    resynth = resynthesize(
        lax.all_to_all(placed, "chan", split_axis=0, concat_axis=3, tiled=True)[0],
        table,
        taps_count,
        chans,
    )
    return (visibility, resynth)


def turn_of(steps):
    quarter = NCH // 4
    turn = steps & (NCH - 1)
    quadrant = (turn + quarter // 2) >> (quarter.bit_length() - 1)
    x = (turn - quadrant * quarter).astype(jnp.float32) * (2.0 * math.pi / NCH)
    y = x * x
    even = 1.0 + y * (-1 / 2 + y * (1 / 24 + y * (-1 / 720 + y * (1 / 40320))))
    odd = x * (1.0 + y * (-1 / 6 + y * (1 / 120 + y * (-1 / 5040 + y * (1 / 362880)))))
    swap = (quadrant & 1) == 1
    cosine, sine = jnp.where(swap, odd, even), jnp.where(swap, even, odd)
    cosine = jnp.where(((quadrant + 1) & 2) == 2, -cosine, cosine)
    return cosine, jnp.where((quadrant & 2) == 2, -sine, sine)


def weigh(first, scale, delay_ref, out_ref, at, left, high, wide):
    beams_n = delay_ref.shape[0]
    delay = delay_ref[at : at + high, left : left + wide]
    step_cos, step_sin = turn_of(delay)
    cosine, sine = turn_of(delay * first)

    def body(f, held):
        cosine, sine = held
        out_ref[f, at : at + high, left : left + wide] = cosine.astype(jnp.bfloat16)
        low = at + beams_n
        out_ref[f, low : low + high, left : left + wide] = sine.astype(jnp.bfloat16)
        return (
            cosine * step_cos - sine * step_sin,
            sine * step_cos + cosine * step_sin,
        )

    lax.fori_loop(0, out_ref.shape[0], body, (cosine * scale, sine * scale))


QUAD = 4
VOICES = 8


def trig_of(shape, n_grp):
    row = lax.broadcasted_iota(jnp.int32, shape, 0)
    lane = lax.broadcasted_iota(jnp.int32, shape, 1)
    tile = 2 * QUAD
    part = row // QUAD % 2
    channel = row // tile * QUAD + row % QUAD
    to_part = lane // NCH
    cosine, sine = turn_of(channel * (lane % NCH))
    return jnp.where(part == to_part, cosine, jnp.where(to_part == 1, sine, -sine))


def partner(x, lanes):
    pieces = [x[:, at : at + 128] for at in range(0, lanes, 128)]
    after = jnp.concatenate([pltpu.roll(p, 128 - QUAD, 1) for p in pieces], axis=1)
    before = jnp.concatenate([pltpu.roll(p, QUAD, 1) for p in pieces], axis=1)
    lane = lax.broadcasted_iota(jnp.int32, x.shape, 1)
    return lane // QUAD % 2 == 0, after, before


def front_kernel(
    n_chan, n_sub, most,
    volt_ref, taps_ref, counts_ref, name_ref, delay_ref, owner_ref,
    sorted_ref, beams_ref,
    v_ref, wide_ref, x_ref, g_ref, y_ref, d_ref, perm_ref, turn_ref, c_ref, held, weight_ref,
    place_ref, ready,
    load_sem, own_sem, out_sem, keep_sem, zs, zr, xs, xr, cs, cr, es, er,
):
    me_c, me_s = lax.axis_index("chan"), lax.axis_index("sub")
    core, across = me_s % 2, me_s // 2
    n_x = n_sub // 2
    twin = me_s + 1 - 2 * core
    mesh_id = pl.DeviceIdType.MESH
    pieces, per = x_ref.shape[1], x_ref.shape[2]
    n_grp = pieces * per
    spectra_n = BLOCKS * SPEC
    frames_n, rows = v_ref.shape[:2]
    inputs = name_ref.shape[1]
    beams_n = delay_ref.shape[0]
    ch_dev = n_grp * QUAD
    tile = 2 * QUAD
    wide = 2 * NCH
    block = x_ref.shape[3]

    def chan_of(offset):
        return (me_c + offset) % n_chan

    def sub_of(offset):
        return (across + offset) % n_x * 2 + core

    barrier = pltpu.get_barrier_semaphore()
    for j in range(1, n_chan):
        pl.semaphore_signal(barrier, device_id={"chan": chan_of(j)}, device_id_type=mesh_id)
    for j in range(1, n_x):
        pl.semaphore_signal(barrier, device_id={"sub": sub_of(j)}, device_id_type=mesh_id)
    pl.semaphore_signal(barrier, device_id={"sub": twin}, device_id_type=mesh_id)

    for s in range(frames_n):
        pltpu.make_async_copy(
            volt_ref.at[:, :, pl.ds(s * NCH, NCH)], v_ref.at[s], load_sem
        ).start()

    def z_copy(j, q):
        return pltpu.make_async_remote_copy(
            src_ref=x_ref.at[chan_of(j), q],
            dst_ref=g_ref.at[q, me_c, me_s],
            send_sem=zs,
            recv_sem=zr.at[j - 1, q],
            device_id={"chan": chan_of(j)},
            device_id_type=mesh_id,
        )

    def source(j, q):
        if j == 0:
            return x_ref.at[me_c, q]
        return g_ref.at[q, chan_of(n_chan - j), me_s]

    def x_copy(dx, j, q):
        return pltpu.make_async_remote_copy(
            src_ref=source(j, q),
            dst_ref=g_ref.at[q, chan_of(n_chan - j), me_s],
            send_sem=xs,
            recv_sem=xr.at[dx - 1, j, q],
            device_id={"sub": sub_of(dx)},
            device_id_type=mesh_id,
        )

    def core_copy(dx, j, q):
        home = g_ref.at[q, chan_of(n_chan - j), sub_of(n_x - dx)]
        return pltpu.make_async_remote_copy(
            src_ref=source(j, q) if dx == 0 else home,
            dst_ref=home,
            send_sem=cs,
            recv_sem=cr.at[q],
            device_id={"sub": twin},
            device_id_type=mesh_id,
        )

    def beam_copy(j, q):
        return pltpu.make_async_remote_copy(
            src_ref=ready.at[chan_of(j), q],
            dst_ref=beams_ref.at[me_c, q],
            send_sem=es,
            recv_sem=er,
            device_id={"chan": chan_of(j)},
            device_id_type=mesh_id,
        )

    trig = trig_of((n_chan * n_grp * tile, wide), n_grp)
    high = trig.astype(jnp.bfloat16)
    d_ref[:, :wide] = high
    d_ref[:, wide:] = (trig - high.astype(jnp.float32)).astype(jnp.bfloat16)

    valid = []
    for t in range(spectra_n):
        valid.append(jnp.where(counts_ref[t // SPEC] > t % SPEC, 1.0, 0.0))
    step = 16
    run = 4
    pltpu.make_async_copy(v_ref, v_ref, load_sem).wait()
    for s in range(frames_n):
        wide_ref[s] = v_ref[s].reshape(2 * rows, NCH).astype(jnp.float32)

    for c in range(2):

        @pl.loop(0, rows // step)
        def _(it):
            at = pl.multiple_of(it * step, step)
            taps = [taps_ref[k : k + 1, :] for k in range(TAPS)]
            for first in range(0, spectra_n, run):
                window = [
                    wide_ref[s, pl.ds(2 * at + c, step, stride=2), :]
                    for s in range(first, first + run + TAPS - 1)
                ]
                for j in range(run):
                    t = first + j
                    total = window[j] * taps[0]
                    for k in range(1, TAPS):
                        total = total + window[j + k] * taps[k]
                    total = total * valid[t]
                    high = total.astype(jnp.bfloat16)
                    low = (total - high.astype(jnp.float32)).astype(jnp.bfloat16)
                    slot = t // 2 * 2 + (t % 2 + core) % 2
                    to = pl.multiple_of(slot * rows + at, step)
                    y_ref[pl.ds(to, step), c * NCH : (c + 1) * NCH] = high
                    y_ref[pl.ds(to, step), wide + c * NCH : wide + (c + 1) * NCH] = low

    across_dims = (((1,), (1,)), ((), ()))

    @pl.loop(0, spectra_n // 4)
    def _(u):
        at = pl.multiple_of(u * 4 * rows, 4 * rows)
        high = y_ref[pl.ds(at, 4 * rows), :wide]
        low = y_ref[pl.ds(at, 4 * rows), wide:]
        out = lax.dot_general(d_ref[:, :wide], high, across_dims, preferred_element_type=jnp.float32)
        out = out + lax.dot_general(
            d_ref[:, wide:], high, across_dims, preferred_element_type=jnp.float32
        )
        out = out + lax.dot_general(
            d_ref[:, :wide], low, across_dims, preferred_element_type=jnp.float32
        )
        to = pl.multiple_of(u * 2 * tile, 2 * tile)
        for d in range(n_chan):
            for q in range(pieces):
                for e in range(per):
                    row = ((d * pieces + q) * per + e) * tile
                    both = jnp.concatenate(
                        [out[row : row + tile, :128], out[row : row + tile, 128:]], axis=0
                    )
                    x_ref[d, q, e, pl.ds(to, 2 * tile), :] = both.astype(jnp.bfloat16)

    pl.semaphore_wait(barrier, n_chan + n_x - 1)
    def spread(j, q):
        for dx in range(1, n_x):
            x_copy(dx, j, q).start()
        core_copy(0, j, q).start()

    for q in range(pieces):
        for j in range(1, n_chan):
            z_copy(j, q).start()
    for q in range(pieces):
        spread(0, q)
    for q in range(pieces):
        pltpu.make_async_copy(x_ref.at[me_c, q], g_ref.at[q, me_c, me_s], keep_sem).start()

    half = inputs // 4
    first = me_c * ch_dev
    scale = 1.0 / math.sqrt(inputs)

    def name_unit(m):
        def run_unit():
            low = lax.broadcasted_iota(jnp.int32, (half, inputs), 0) + m * half
            perm_ref[m * half : (m + 1) * half, :] = jnp.where(
                name_ref[...] == low, 1.0, 0.0
            ).astype(jnp.bfloat16)

        return run_unit

    def turn_unit():
        turned = jnp.dot(
            delay_ref[...].astype(jnp.float32).astype(jnp.bfloat16),
            perm_ref[...],
            preferred_element_type=jnp.float32,
        )
        turn_ref[...] = turned.astype(jnp.int32)

    def weigh_unit(at, left):
        return lambda: weigh(first, scale, turn_ref, weight_ref, at, left, 16, 512)

    def place_unit():
        lanes = per * beams_n
        owner = jnp.concatenate([owner_ref[...]] * per, axis=1)
        named = (lax.broadcasted_iota(jnp.int32, (8, lanes), 0) == owner).astype(jnp.float32)
        row = lax.broadcasted_iota(jnp.int32, (lanes, lanes), 0)
        lane = lax.broadcasted_iota(jnp.int32, (lanes, lanes), 1)
        before = (row < lane) & (row // beams_n == lane // beams_n)
        rank = jnp.dot(
            named.astype(jnp.bfloat16),
            jnp.where(before, 1.0, 0.0).astype(jnp.bfloat16),
            preferred_element_type=jnp.float32,
        )
        rank = jnp.sum(named * rank, axis=0, keepdims=True).astype(jnp.int32)
        lane = lax.broadcasted_iota(jnp.int32, (1, lanes), 1)
        slot = (lane // beams_n * n_chan + owner) * (4 * most) + rank
        row = lax.broadcasted_iota(jnp.int32, (place_ref.shape[0], lanes), 0)
        for m in range(4):
            place_ref[:, m * lanes : (m + 1) * lanes] = jnp.where(
                row == slot + m * most, 1.0, 0.0
            ).astype(jnp.bfloat16)

    def join_unit(q):
        def run_unit():
            left = lax.broadcasted_iota(jnp.int32, (block, 128), 1) < 64
            for e in range(per):
                low = 2 * e * block
                for c in range(n_chan):
                    for x in range(n_x):
                        a = g_ref[q, c, 2 * x, e].astype(jnp.float32)
                        b = g_ref[q, c, 2 * x + 1, e].astype(jnp.float32)
                        at = (c * n_x + x) * 128
                        c_ref[low : low + block, at : at + 128] = jnp.where(left, a, b).astype(
                            jnp.bfloat16
                        )
                        c_ref[low + block : low + 2 * block, at : at + 128] = pltpu.roll(
                            jnp.where(left, b, a), 64, 1
                        ).astype(jnp.bfloat16)

        return run_unit

    def sort_unit(q, e, m):
        def run_unit():
            held[q * per + e, m * half : (m + 1) * half, :] = lax.dot_general(
                perm_ref[m * half : (m + 1) * half, :],
                c_ref[2 * e * block : 2 * (e + 1) * block, :],
                across_dims,
                preferred_element_type=jnp.float32,
            ).astype(jnp.bfloat16)

        return run_unit

    mixes = {}

    def mix_unit(q, e):
        def run_unit():
            at = q * per + e
            lane = lax.broadcasted_iota(jnp.int32, (2 * beams_n, 2 * block), 1)
            total = None
            for f in range(QUAD):
                mixed = lax.dot_general(
                    weight_ref[at * QUAD + f],
                    c_ref[2 * e * block : 2 * (e + 1) * block, :],
                    across_dims,
                    preferred_element_type=jnp.float32,
                )
                total = mixed if total is None else jnp.where(lane % QUAD == f, mixed, total)
            real, after, before = partner(total[beams_n:], 2 * block)
            mixes[q, e] = total[:beams_n] + jnp.where(real, -after, before)

        return run_unit

    def place_beams(q):
        def run_unit():
            both = jnp.concatenate([mixes.pop((q, e)) for e in range(per)], axis=0)
            turned = both.T
            parts = []
            for m in range(4):
                parity, u = m % 2, m // 2
                picks = [
                    turned[parity * block + v * 2 * tile + u * tile :][:tile]
                    for v in range(spectra_n // 4)
                ]
                parts.append(jnp.concatenate(picks, axis=0))
            lined = jnp.concatenate(parts, axis=1).astype(jnp.bfloat16)
            out = lax.dot_general(
                lined, place_ref[...], across_dims, preferred_element_type=jnp.float32
            ).astype(jnp.bfloat16)
            for e in range(per):
                for d in range(n_chan):
                    at = (e * n_chan + d) * 128
                    ready[d, q, e] = out[:, at : at + 128]
            for j in range(1, n_chan):
                beam_copy(j, q).start()
            pltpu.make_async_copy(ready.at[me_c, q], beams_ref.at[me_c, q], own_sem).start()

        return run_unit

    def store_unit(q):
        def run_unit():
            part = pl.ds(q * per, per)
            pltpu.make_async_copy(held.at[part], sorted_ref.at[part], out_sem).start()

        return run_unit

    def units_of(q):
        units = [join_unit(q)] + [mix_unit(q, e) for e in range(per)] + [place_beams(q)]
        units += [sort_unit(q, e, m) for e in range(per) for m in range(4)]
        return units + [store_unit(q)]

    def z_step(j, q):
        def run_step():
            z_copy(j, q).wait_recv()
            spread(j, q)

        return run_step

    def x_step(j, q):
        for dx in range(1, n_x):
            x_copy(dx, j, q).wait_recv()
            core_copy(dx, j, q).start()

    def weave(units, steps):
        done = 0
        for i, one in enumerate(steps):
            upto = len(units) * (i + 1) // len(steps)
            for unit in units[done:upto]:
                unit()
            done = upto
            one()
        for unit in units[done:]:
            unit()

    def arrive(q):
        if q == 0:
            pltpu.make_async_copy(x_ref.at[me_c], g_ref.at[:, me_c, me_s], keep_sem).wait()
        part = g_ref.at[q, pl.ds(0, n_chan // 2)]
        pltpu.make_async_copy(part, part, cr.at[q]).wait()

    setup = [name_unit(m) for m in range(4)] + [turn_unit]
    setup += [
        weigh_unit(at, left) for at in range(0, beams_n, 16) for left in range(0, inputs, 512)
    ]
    setup.append(place_unit)
    weave(setup, [z_step(j, 0) for j in range(1, n_chan)])
    for q in range(1, pieces + 1):
        for j in range(n_chan):
            x_step(j, q - 1)
        arrive(q - 1)
        steps = [z_step(j, q) for j in range(1, n_chan)] if q < pieces else []
        weave(units_of(q - 1), steps)
    others = pl.ds(0, n_chan - 1)
    pltpu.make_async_copy(ready.at[others], beams_ref.at[others], er).wait()
    pltpu.make_async_copy(x_ref.at[others], x_ref.at[others], zs).wait()
    for dx in range(1, n_x):
        pltpu.make_async_copy(x_ref, x_ref, xs).wait()
    part = g_ref.at[pl.ds(0, pieces // 2)]
    pltpu.make_async_copy(part, part, cs).wait()
    pltpu.make_async_copy(ready.at[others], ready.at[others], es).wait()
    pltpu.make_async_copy(ready.at[me_c], beams_ref.at[me_c], own_sem).wait()
    pltpu.make_async_copy(held, sorted_ref, out_sem).wait()


def front(voltages, taps, counts, names, delays, owner, n_chan, n_sub, most):
    rows = voltages.shape[0]
    beams_n, inputs = delays.shape
    spectra_n = BLOCKS * SPEC
    ch_dev = NCH // n_chan
    n_grp = ch_dev // QUAD
    per = 2
    pieces = n_grp // per
    n_x = n_sub // 2
    tile = 2 * QUAD
    block = spectra_n // 2 * tile
    dma = pltpu.SemaphoreType.DMA
    vmem = pl.BlockSpec(memory_space=pltpu.VMEM)
    travel = (n_chan, pieces, per, spectra_n // 4 * tile, 128)
    return pl.pallas_call(
        functools.partial(front_kernel, n_chan, n_sub, most),
        in_specs=[
            pl.BlockSpec(memory_space=pl.ANY),
            vmem,
            pl.BlockSpec(memory_space=pltpu.SMEM),
            vmem,
            vmem,
            vmem,
        ],
        out_specs=[pl.BlockSpec(memory_space=pl.ANY)] * 2,
        out_shape=[
            jax.ShapeDtypeStruct((n_grp, inputs, 2 * block), jnp.bfloat16),
            jax.ShapeDtypeStruct(travel, jnp.bfloat16),
        ],
        scratch_shapes=[
            pltpu.VMEM((spectra_n + TAPS - 1, rows, 2, NCH), jnp.bfloat16),
            pltpu.VMEM((spectra_n + TAPS - 1, 2 * rows, NCH), jnp.float32),
            pltpu.VMEM((n_chan, pieces, per, block, 128), jnp.bfloat16),
            pltpu.VMEM((pieces, n_chan, n_sub, per, block, 128), jnp.bfloat16),
            pltpu.VMEM((spectra_n * rows, 4 * NCH), jnp.bfloat16),
            pltpu.VMEM((2 * NCH, 4 * NCH), jnp.bfloat16),
            pltpu.VMEM((inputs, inputs), jnp.bfloat16),
            pltpu.VMEM((beams_n, inputs), jnp.int32),
            pltpu.VMEM((2 * per * block, inputs), jnp.bfloat16),
            pltpu.VMEM((n_grp, inputs, 2 * block), jnp.bfloat16),
            pltpu.VMEM((ch_dev, 2 * beams_n, inputs), jnp.bfloat16),
            pltpu.VMEM((per * n_chan * 128, 4 * per * beams_n), jnp.bfloat16),
            pltpu.VMEM(travel, jnp.bfloat16),
            dma,
            dma,
            dma,
            dma,
            dma,
            dma((n_chan - 1, pieces)),
            dma,
            dma((n_x - 1, n_chan, pieces)),
            dma,
            dma((pieces,)),
            dma,
            dma,
        ],
        compiler_params=pltpu.CompilerParams(collective_id=0, has_side_effects=True),
        name="front",
    )(voltages, taps, counts, names, delays, owner)


def back_kernel(
    sub_ref, counts_ref, start_ref, mine_ref, all_ref, beams_ref, taps_ref,
    out_ref, voice_ref,
    left_ref, bank_ref, table_ref,
):
    g = pl.program_id(0)
    rows, lanes = mine_ref.shape[1], mine_ref.shape[2]
    inputs = all_ref.shape[1]
    count, _, samples = voice_ref.shape
    frames_n = samples // NCH
    spectra_n = frames_n - TAPS + 1
    n_chan, n_grp = beams_ref.shape[0], beams_ref.shape[1]
    tile = 2 * QUAD
    total = counts_ref[0]
    for i in range(1, BLOCKS):
        total = total + counts_ref[i]
    scale = 1.0 / jnp.full((8, 128), total.astype(jnp.float32))
    scale = scale[:1, :1]

    def fill(ref, slot, lanes_kept):
        plain = ref[0]
        real, after, before = partner(plain.astype(jnp.float32), lanes)
        turned = jnp.where(real, after, -before).astype(jnp.bfloat16)
        lane = lax.broadcasted_iota(jnp.int32, (16, lanes), 1) % QUAD
        for i in lanes_kept:
            keep = jnp.where(lane == i, 1.0, 0.0).astype(jnp.bfloat16)
            keep = jnp.concatenate([keep] * (rows // 16), axis=0)
            at = pl.multiple_of(2 * i * rows, rows)
            left_ref[slot, pl.ds(at, rows), :] = plain * keep
            left_ref[slot, pl.ds(at + rows, rows), :] = turned * keep

    @pl.when(g == 0)
    def _():
        fill(start_ref, 0, range(QUAD))

    fill(mine_ref, (g + 1) % 2, range(QUAD))
    for at in range(0, inputs, 256):
        product = lax.dot_general(
            left_ref[g % 2],
            all_ref[0, at : at + 256, :],
            (((1,), (1,)), ((), ())),
            preferred_element_type=jnp.float32,
        )
        product = (product * scale).astype(jnp.bfloat16)
        for i in range(QUAD):
            for c in range(2):
                low = (2 * i + c) * rows
                out_ref[i, c, :, at : at + 256] = product[low : low + rows]

    @pl.when(g == 0)
    def _():
        edge = (TAPS - 1) * count
        bank_ref[:edge, :] = jnp.zeros((edge, 2 * NCH), jnp.bfloat16)
        end = edge + spectra_n * count
        bank_ref[end:, :] = jnp.zeros((bank_ref.shape[0] - end, 2 * NCH), jnp.bfloat16)
        for u in range(0, spectra_n // 4, 2):
            tiles = [
                beams_ref[c, e, u * tile : (u + 2) * tile, :].astype(jnp.float32)
                for c in range(n_chan)
                for e in range(n_grp)
            ]
            for v in range(2):
                stack = jnp.concatenate([t[v * tile : (v + 1) * tile] for t in tiles], axis=0)
                at = edge + (u + v) * 4 * count
                bank_ref[at : at + 4 * count, :] = stack.T.astype(jnp.bfloat16)

    @pl.when(g == 0)
    def _():
        trig = trig_of((2 * NCH, 2 * NCH), n_grp)
        for k in range(TAPS):
            taps = taps_ref[k : k + 1, :]
            table_ref[k] = (trig * jnp.concatenate([taps, taps], axis=1)).astype(jnp.bfloat16)

    run = VOICES
    chunk = g - 1

    @pl.when((chunk >= 0) & (chunk * run < frames_n))
    def _():
        acc = jnp.zeros((run * count, 2 * NCH), jnp.float32)
        for k in range(TAPS):
            start = pl.multiple_of((chunk * run - k + TAPS - 1) * count, count)
            acc = acc + jnp.dot(
                bank_ref[pl.ds(start, run * count), :],
                table_ref[k],
                preferred_element_type=jnp.float32,
            )
        for j in range(run):

            @pl.when(chunk * run + j < frames_n)
            def _():
                at = pl.multiple_of((chunk * run + j) * NCH, NCH)
                for c in range(2):
                    voice_ref[:, c, pl.ds(at, NCH)] = acc[
                        j * count : (j + 1) * count, c * NCH : (c + 1) * NCH
                    ]


def back(by_id, beams, taps, counts, sub_index, rows, count):
    n_grp, inputs, lanes = by_id.shape
    n_chan = beams.shape[0]
    beams = beams.reshape((n_chan, n_grp) + beams.shape[3:])
    spectra_n = BLOCKS * SPEC
    frames_n = spectra_n + TAPS - 1
    fixed = lambda shape: pl.BlockSpec(
        shape, lambda g, s: (0,) * len(shape), pipeline_mode=pl.Buffered(1)
    )
    return pl.pallas_call(
        back_kernel,
        grid_spec=pltpu.PrefetchScalarGridSpec(
            num_scalar_prefetch=1,
            grid=(n_grp,),
            in_specs=[
                pl.BlockSpec(memory_space=pltpu.SMEM),
                pl.BlockSpec(
                    (1, rows, lanes),
                    lambda g, s: (0, s[0], 0),
                    pipeline_mode=pl.Buffered(1),
                ),
                pl.BlockSpec(
                    (1, rows, lanes), lambda g, s: (jnp.minimum(g + 1, n_grp - 1), s[0], 0)
                ),
                pl.BlockSpec((1, inputs, lanes), lambda g, s: (g, 0, 0)),
                fixed(beams.shape),
                fixed(taps.shape),
            ],
            out_specs=[
                pl.BlockSpec((QUAD, 2, rows, inputs), lambda g, s: (g, 0, 0, 0)),
                fixed((count, 2, frames_n * NCH)),
            ],
            scratch_shapes=[
                pltpu.VMEM((2, 2 * QUAD * rows, lanes), jnp.bfloat16),
                pltpu.VMEM(((frames_n + VOICES + TAPS) * count, 2 * NCH), jnp.bfloat16),
                pltpu.VMEM((TAPS, 2 * NCH, 2 * NCH), jnp.bfloat16),
            ],
        ),
        out_shape=[
            jax.ShapeDtypeStruct((n_grp * QUAD, 2, rows, inputs), jnp.bfloat16),
            jax.ShapeDtypeStruct((count, 2, frames_n * NCH), jnp.float32),
        ],
        compiler_params=pltpu.CompilerParams(dimension_semantics=("arbitrary",)),
        name="back",
    )(sub_index, counts, by_id, by_id, by_id, beams, taps)


def local(voltages, taps, input_id, counts, delays, beam_owner):
    n_chan = lax.axis_size("chan")
    n_sub = lax.axis_size("sub")
    inp_dev = voltages.shape[0]
    inputs = input_id.shape[0]
    spectra_n = BLOCKS * SPEC
    ch_dev = NCH // n_chan
    rows = inputs // n_sub
    section = BEAMS // n_sub
    most = min(section, max(2, 2 * section // n_chan))
    fits = inp_dev == 64 and most == 32 and section == 64 and NCH == 128
    fits = fits and n_sub % 2 == 0 and ch_dev % (2 * QUAD) == 0 and inputs % 512 == 0
    if not fits or n_sub != 4 or n_chan % 2 or n_chan > 8 or rows % 128:
        return local_plain(voltages, taps, input_id, counts, delays, beam_owner)
    sub_index = lax.axis_index("sub")
    owner = lax.dynamic_slice_in_dim(beam_owner[:, 0], sub_index * section, section)[None]
    taps2 = taps.reshape(TAPS, NCH)
    names = input_id[None]
    by_id, beams = front(voltages, taps2, counts, names, delays, owner, n_chan, n_sub, most)
    visibility, resynth = back(
        by_id, beams, taps2, counts, sub_index.astype(jnp.int32)[None], rows, most
    )
    return (visibility, resynth)


def solution(mesh):
    placed = (
        P(("grp", "chan", "sub"), None, None),
        P(),
        P(),
        P("grp"),
        P(("grp", "sub"), None),
        P("grp", None),
    )
    return jax.shard_map(
        local,
        mesh=mesh,
        in_specs=placed,
        out_specs=(P(("grp", "chan"), None, "sub", None), P(("grp", "chan", "sub"), None, None)),
        check_vma=False,
    )
```

```python
import functools
import math

import jax
import jax.numpy as jnp
from jax import lax
from jax.experimental import pallas as pl
from jax.experimental.pallas import tpu as pltpu
from jax.sharding import PartitionSpec as P

NCH = 128
TAPS = 12
SPEC = 8
BLOCKS = 4
BEAMS = 256


def filter_table(taps, chans):
    length = taps.shape[0]
    position = jnp.arange(length, dtype=jnp.int32) % chans
    channel = jnp.arange(chans, dtype=jnp.int32)
    phase = (position[:, None] * channel[None, :] % chans).astype(jnp.float32) * (
        2.0 * math.pi / chans
    )
    cosine = taps[:, None] * jnp.cos(phase)
    sine = taps[:, None] * jnp.sin(phase)
    upper = jnp.concatenate([cosine, -sine], axis=1)
    lower = jnp.concatenate([sine, cosine], axis=1)
    return jnp.concatenate([upper, lower], axis=0).astype(jnp.bfloat16)


def resynthesize(received, table, taps_count, chans):
    count = received.shape[0]
    spectra_n = received.shape[3]
    table3 = table.reshape(2 * taps_count * chans, 2, chans)
    grid = jnp.einsum("pcht,mch->ptm", received, table3, preferred_element_type=jnp.float32)
    grid = grid.reshape(count, spectra_n, 2, taps_count, chans)
    total = jnp.zeros((count, spectra_n + taps_count - 1, 2, chans), jnp.float32)
    for k in range(taps_count):
        total = total + jnp.pad(
            grid[:, :, :, k, :], ((0, 0), (k, taps_count - 1 - k), (0, 0), (0, 0))
        )
    return jnp.transpose(total, (0, 2, 1, 3)).reshape(
        count, 2, (spectra_n + taps_count - 1) * chans
    )


def local_plain(voltages, taps, input_id, counts, delays, beam_owner):
    n_chan = lax.axis_size("chan")
    n_sub = lax.axis_size("sub")
    inp_dev = voltages.shape[0]
    inputs = input_id.shape[0]
    chans = NCH
    taps_count = TAPS
    spectra_n = BLOCKS * SPEC
    ch_dev = chans // n_chan
    rows = inputs // n_sub
    section = BEAMS // n_sub
    most = min(section, max(2, 2 * section // n_chan))
    table = filter_table(taps, chans)
    position = jnp.arange(spectra_n, dtype=jnp.int32)
    valid = (position % SPEC < jnp.repeat(counts, SPEC)).astype(jnp.float32)
    total = jnp.sum(counts.astype(jnp.float32))
    frames = voltages.reshape(inp_dev, 2, spectra_n + taps_count - 1, chans)
    windows = jnp.concatenate(
        [frames[:, :, k : k + spectra_n, :] for k in range(taps_count)], axis=3
    )
    table3 = table.reshape(2, taps_count * chans, 2 * chans)
    filtered = jnp.einsum("icth,chm->mit", windows, table3, preferred_element_type=jnp.float32)
    filtered = filtered * valid[None, None, :]
    spectra = filtered.reshape(2, chans, inp_dev, spectra_n).astype(jnp.bfloat16)
    slot_of = jnp.zeros((inputs,), jnp.int32).at[input_id].set(jnp.arange(inputs, dtype=jnp.int32))
    turned = lax.all_to_all(spectra, "chan", split_axis=1, concat_axis=2, tiled=True)
    gathered = lax.all_gather(turned, "sub", axis=2, tiled=True)
    chan_part = slot_of // (n_sub * inp_dev)
    sub_part = slot_of // inp_dev % n_sub
    order = (sub_part * n_chan + chan_part) * inp_dev + slot_of % inp_dev
    by_id = jnp.take(gathered, order, axis=2)
    sub_index = lax.axis_index("sub")
    mine = lax.dynamic_slice_in_dim(by_id, sub_index * rows, rows, 2)
    real_part = jnp.einsum("cxit,cxjt->xij", mine, by_id, preferred_element_type=jnp.float32)
    imag_part = jnp.einsum("xit,xjt->xij", mine[1], by_id[0], preferred_element_type=jnp.float32)
    imag_part = imag_part - jnp.einsum(
        "xit,xjt->xij", mine[0], by_id[1], preferred_element_type=jnp.float32
    )
    visibility = (jnp.stack([real_part, imag_part], axis=1) / total).astype(jnp.bfloat16)
    channel = lax.axis_index("chan") * ch_dev + jnp.arange(ch_dev, dtype=jnp.int32)
    phase = (delays[None, :, :] * channel[:, None, None] % chans).astype(jnp.float32) * (
        2.0 * math.pi / chans
    )
    scale = 1.0 / math.sqrt(inputs)
    weight_cos = (jnp.cos(phase) * scale).astype(jnp.bfloat16)
    weight_sin = (jnp.sin(phase) * scale).astype(jnp.bfloat16)
    from_cos = jnp.einsum("xbi,cxit->cxbt", weight_cos, by_id, preferred_element_type=jnp.float32)
    from_sin = jnp.einsum("xbi,cxit->cxbt", weight_sin, by_id, preferred_element_type=jnp.float32)
    beams = jnp.stack([from_cos[0] - from_sin[1], from_cos[1] + from_sin[0]]).astype(jnp.bfloat16)
    owner = lax.dynamic_slice_in_dim(beam_owner[:, 0], sub_index * section, section)
    beam = jnp.arange(section, dtype=jnp.int32)
    earlier = (owner[None, :] == owner[:, None]) & (beam[None, :] < beam[:, None])
    rank = jnp.sum(earlier.astype(jnp.int32), axis=1)
    target = owner * most + rank
    select = (jnp.arange(n_chan * most, dtype=jnp.int32)[:, None] == target[None, :]).astype(
        jnp.bfloat16
    )
    placed = jnp.einsum("pb,cxbt->pcxt", select, beams, preferred_element_type=jnp.float32).astype(
        jnp.bfloat16
    )
    placed = placed.reshape(n_chan, most, 2, ch_dev, spectra_n)
    resynth = resynthesize(
        lax.all_to_all(placed, "chan", split_axis=0, concat_axis=3, tiled=True)[0],
        table,
        taps_count,
        chans,
    )
    return (visibility, resynth)


def turn_of(steps):
    quarter = NCH // 4
    turn = steps & (NCH - 1)
    quadrant = (turn + quarter // 2) >> (quarter.bit_length() - 1)
    x = (turn - quadrant * quarter).astype(jnp.float32) * (2.0 * math.pi / NCH)
    y = x * x
    even = 1.0 + y * (-1 / 2 + y * (1 / 24 + y * (-1 / 720 + y * (1 / 40320))))
    odd = x * (1.0 + y * (-1 / 6 + y * (1 / 120 + y * (-1 / 5040 + y * (1 / 362880)))))
    swap = (quadrant & 1) == 1
    cosine, sine = jnp.where(swap, odd, even), jnp.where(swap, even, odd)
    cosine = jnp.where(((quadrant + 1) & 2) == 2, -cosine, cosine)
    return cosine, jnp.where((quadrant & 2) == 2, -sine, sine)


def weigh(first, scale, delay_ref, out_ref, at, left, high, wide):
    beams_n = delay_ref.shape[0]
    delay = delay_ref[at : at + high, left : left + wide]
    step_cos, step_sin = turn_of(delay)
    cosine, sine = turn_of(delay * first)

    def body(f, held):
        cosine, sine = held
        out_ref[f, at : at + high, left : left + wide] = cosine.astype(jnp.bfloat16)
        low = at + beams_n
        out_ref[f, low : low + high, left : left + wide] = sine.astype(jnp.bfloat16)
        return (
            cosine * step_cos - sine * step_sin,
            sine * step_cos + cosine * step_sin,
        )

    lax.fori_loop(0, out_ref.shape[0], body, (cosine * scale, sine * scale))


QUAD = 4
VOICES = 4


def trig_of(shape, n_grp):
    row = lax.broadcasted_iota(jnp.int32, shape, 0)
    lane = lax.broadcasted_iota(jnp.int32, shape, 1)
    tile = 2 * QUAD
    part = row // QUAD % 2
    channel = row // tile * QUAD + row % QUAD
    to_part = lane // NCH
    cosine, sine = turn_of(channel * (lane % NCH))
    return jnp.where(part == to_part, cosine, jnp.where(to_part == 1, sine, -sine))


def partner(x, lanes):
    pieces = [x[:, at : at + 128] for at in range(0, lanes, 128)]
    after = jnp.concatenate([pltpu.roll(p, 128 - QUAD, 1) for p in pieces], axis=1)
    before = jnp.concatenate([pltpu.roll(p, QUAD, 1) for p in pieces], axis=1)
    lane = lax.broadcasted_iota(jnp.int32, x.shape, 1)
    return lane // QUAD % 2 == 0, after, before


def front_kernel(
    n_chan, n_sub, most,
    volt_ref, taps_ref, counts_ref, name_ref, delay_ref, owner_ref,
    sorted_ref, beams_ref,
    v_ref, wide_ref, x_ref, g_ref, y_ref, d_ref, perm_ref, turn_ref, c_ref, held, weight_ref,
    place_ref, ready,
    load_sem, own_sem, out_sem, keep_sem, zs, zr, xs, xr, cs, cr, es, er,
):
    me_c, me_s = lax.axis_index("chan"), lax.axis_index("sub")
    core, across = me_s % 2, me_s // 2
    n_x = n_sub // 2
    twin = me_s + 1 - 2 * core
    mesh_id = pl.DeviceIdType.MESH
    pieces, per = x_ref.shape[1], x_ref.shape[2]
    n_grp = pieces * per
    spectra_n = BLOCKS * SPEC
    frames_n, rows = v_ref.shape[:2]
    inputs = name_ref.shape[1]
    beams_n = delay_ref.shape[0]
    ch_dev = n_grp * QUAD
    tile = 2 * QUAD
    wide = 2 * NCH
    block = x_ref.shape[3]

    def chan_of(k):
        at = me_c
        bit = 1
        while bit < n_chan:
            if k & bit:
                at = at + bit - 2 * bit * (me_c // bit % 2)
            bit *= 2
        return at

    def sub_of(offset):
        return (across + offset) % n_x * 2 + core

    barrier = pltpu.get_barrier_semaphore()
    for j in range(1, n_chan):
        pl.semaphore_signal(barrier, device_id={"chan": chan_of(j)}, device_id_type=mesh_id)
    for j in range(1, n_x):
        pl.semaphore_signal(barrier, device_id={"sub": sub_of(j)}, device_id_type=mesh_id)
    pl.semaphore_signal(barrier, device_id={"sub": twin}, device_id_type=mesh_id)

    for s in range(frames_n):
        pltpu.make_async_copy(
            volt_ref.at[:, :, pl.ds(s * NCH, NCH)], v_ref.at[s], load_sem
        ).start()

    def z_copy(j, q):
        return pltpu.make_async_remote_copy(
            src_ref=x_ref.at[chan_of(j), q],
            dst_ref=g_ref.at[q, me_c, me_s],
            send_sem=zs,
            recv_sem=zr.at[j - 1, q],
            device_id={"chan": chan_of(j)},
            device_id_type=mesh_id,
        )

    def source(j, q):
        if j == 0:
            return x_ref.at[me_c, q]
        return g_ref.at[q, chan_of(j), me_s]

    def x_copy(dx, j, q):
        return pltpu.make_async_remote_copy(
            src_ref=source(j, q),
            dst_ref=g_ref.at[q, chan_of(j), me_s],
            send_sem=xs,
            recv_sem=xr.at[dx - 1, j, q],
            device_id={"sub": sub_of(dx)},
            device_id_type=mesh_id,
        )

    def core_copy(dx, j, q):
        home = g_ref.at[q, chan_of(j), sub_of(n_x - dx)]
        return pltpu.make_async_remote_copy(
            src_ref=source(j, q) if dx == 0 else home,
            dst_ref=home,
            send_sem=cs,
            recv_sem=cr.at[q],
            device_id={"sub": twin},
            device_id_type=mesh_id,
        )

    def beam_copy(j, q):
        return pltpu.make_async_remote_copy(
            src_ref=ready.at[chan_of(j), q],
            dst_ref=beams_ref.at[me_c, q],
            send_sem=es,
            recv_sem=er,
            device_id={"chan": chan_of(j)},
            device_id_type=mesh_id,
        )

    trig = trig_of((n_chan * n_grp * tile, wide), n_grp)
    high = trig.astype(jnp.bfloat16)
    d_ref[:, :wide] = high
    d_ref[:, wide:] = (trig - high.astype(jnp.float32)).astype(jnp.bfloat16)

    valid = []
    for t in range(spectra_n):
        valid.append(jnp.where(counts_ref[t // SPEC] > t % SPEC, 1.0, 0.0))
    step = 16
    run = 4
    pltpu.make_async_copy(v_ref, v_ref, load_sem).wait()
    for s in range(frames_n):
        wide_ref[s] = v_ref[s].reshape(2 * rows, NCH).astype(jnp.float32)

    for c in range(2):

        @pl.loop(0, rows // step)
        def _(it):
            at = pl.multiple_of(it * step, step)
            taps = [taps_ref[k : k + 1, :] for k in range(TAPS)]
            for first in range(0, spectra_n, run):
                window = [
                    wide_ref[s, pl.ds(2 * at + c, step, stride=2), :]
                    for s in range(first, first + run + TAPS - 1)
                ]
                for j in range(run):
                    t = first + j
                    total = window[j] * taps[0]
                    for k in range(1, TAPS):
                        total = total + window[j + k] * taps[k]
                    total = total * valid[t]
                    high = total.astype(jnp.bfloat16)
                    low = (total - high.astype(jnp.float32)).astype(jnp.bfloat16)
                    slot = t // 2 * 2 + (t % 2 + core) % 2
                    to = pl.multiple_of(slot * rows + at, step)
                    y_ref[pl.ds(to, step), c * NCH : (c + 1) * NCH] = high
                    y_ref[pl.ds(to, step), wide + c * NCH : wide + (c + 1) * NCH] = low

    across_dims = (((1,), (1,)), ((), ()))

    @pl.loop(0, spectra_n // 4)
    def _(u):
        at = pl.multiple_of(u * 4 * rows, 4 * rows)
        high = y_ref[pl.ds(at, 4 * rows), :wide]
        low = y_ref[pl.ds(at, 4 * rows), wide:]
        out = lax.dot_general(d_ref[:, :wide], high, across_dims, preferred_element_type=jnp.float32)
        out = out + lax.dot_general(
            d_ref[:, wide:], high, across_dims, preferred_element_type=jnp.float32
        )
        out = out + lax.dot_general(
            d_ref[:, :wide], low, across_dims, preferred_element_type=jnp.float32
        )
        to = pl.multiple_of(u * 2 * tile, 2 * tile)
        for d in range(n_chan):
            for q in range(pieces):
                for e in range(per):
                    row = ((d * pieces + q) * per + e) * tile
                    both = jnp.concatenate(
                        [out[row : row + tile, :128], out[row : row + tile, 128:]], axis=0
                    )
                    x_ref[d, q, e, pl.ds(to, 2 * tile), :] = both.astype(jnp.bfloat16)

    pl.semaphore_wait(barrier, n_chan + n_x - 1)
    def spread(j, q):
        for dx in range(1, n_x):
            x_copy(dx, j, q).start()
        core_copy(0, j, q).start()

    for q in range(pieces):
        for j in range(1, n_chan):
            z_copy(j, q).start()
    for q in range(pieces):
        spread(0, q)
    for q in range(pieces):
        pltpu.make_async_copy(x_ref.at[me_c, q], g_ref.at[q, me_c, me_s], keep_sem).start()

    half = inputs // 4
    first = me_c * ch_dev
    scale = 1.0 / math.sqrt(inputs)

    def name_unit(m):
        def run_unit():
            low = lax.broadcasted_iota(jnp.int32, (half, inputs), 0) + m * half
            perm_ref[m * half : (m + 1) * half, :] = jnp.where(
                name_ref[...] == low, 1.0, 0.0
            ).astype(jnp.bfloat16)

        return run_unit

    def turn_unit():
        turned = jnp.dot(
            delay_ref[...].astype(jnp.float32).astype(jnp.bfloat16),
            perm_ref[...],
            preferred_element_type=jnp.float32,
        )
        turn_ref[...] = turned.astype(jnp.int32)

    def weigh_unit(at, left):
        return lambda: weigh(first, scale, turn_ref, weight_ref, at, left, 16, 512)

    def place_unit():
        lanes = per * beams_n
        owner = jnp.concatenate([owner_ref[...]] * per, axis=1)
        named = (lax.broadcasted_iota(jnp.int32, (8, lanes), 0) == owner).astype(jnp.float32)
        row = lax.broadcasted_iota(jnp.int32, (lanes, lanes), 0)
        lane = lax.broadcasted_iota(jnp.int32, (lanes, lanes), 1)
        before = (row < lane) & (row // beams_n == lane // beams_n)
        rank = jnp.dot(
            named.astype(jnp.bfloat16),
            jnp.where(before, 1.0, 0.0).astype(jnp.bfloat16),
            preferred_element_type=jnp.float32,
        )
        rank = jnp.sum(named * rank, axis=0, keepdims=True).astype(jnp.int32)
        lane = lax.broadcasted_iota(jnp.int32, (1, lanes), 1)
        slot = (lane // beams_n * n_chan + owner) * (4 * most) + rank
        row = lax.broadcasted_iota(jnp.int32, (place_ref.shape[0], lanes), 0)
        for m in range(4):
            place_ref[:, m * lanes : (m + 1) * lanes] = jnp.where(
                row == slot + m * most, 1.0, 0.0
            ).astype(jnp.bfloat16)

    def join_unit(q):
        def run_unit():
            left = lax.broadcasted_iota(jnp.int32, (block, 128), 1) < 64
            for e in range(per):
                low = 2 * e * block
                for c in range(n_chan):
                    for x in range(n_x):
                        a = g_ref[q, c, 2 * x, e].astype(jnp.float32)
                        b = g_ref[q, c, 2 * x + 1, e].astype(jnp.float32)
                        at = (c * n_x + x) * 128
                        c_ref[low : low + block, at : at + 128] = jnp.where(left, a, b).astype(
                            jnp.bfloat16
                        )
                        c_ref[low + block : low + 2 * block, at : at + 128] = pltpu.roll(
                            jnp.where(left, b, a), 64, 1
                        ).astype(jnp.bfloat16)

        return run_unit

    def sort_unit(q, e, m):
        def run_unit():
            held[q * per + e, m * half : (m + 1) * half, :] = lax.dot_general(
                perm_ref[m * half : (m + 1) * half, :],
                c_ref[2 * e * block : 2 * (e + 1) * block, :],
                across_dims,
                preferred_element_type=jnp.float32,
            ).astype(jnp.bfloat16)

        return run_unit

    mixes = {}

    def mix_unit(q, e):
        def run_unit():
            at = q * per + e
            lane = lax.broadcasted_iota(jnp.int32, (2 * beams_n, 2 * block), 1)
            total = None
            for f in range(QUAD):
                mixed = lax.dot_general(
                    weight_ref[at * QUAD + f],
                    c_ref[2 * e * block : 2 * (e + 1) * block, :],
                    across_dims,
                    preferred_element_type=jnp.float32,
                )
                total = mixed if total is None else jnp.where(lane % QUAD == f, mixed, total)
            real, after, before = partner(total[beams_n:], 2 * block)
            mixes[q, e] = total[:beams_n] + jnp.where(real, -after, before)

        return run_unit

    def place_beams(q):
        def run_unit():
            both = jnp.concatenate([mixes.pop((q, e)) for e in range(per)], axis=0)
            turned = both.T
            parts = []
            for m in range(4):
                parity, u = m % 2, m // 2
                picks = [
                    turned[parity * block + v * 2 * tile + u * tile :][:tile]
                    for v in range(spectra_n // 4)
                ]
                parts.append(jnp.concatenate(picks, axis=0))
            lined = jnp.concatenate(parts, axis=1).astype(jnp.bfloat16)
            out = lax.dot_general(
                lined, place_ref[...], across_dims, preferred_element_type=jnp.float32
            ).astype(jnp.bfloat16)
            for e in range(per):
                for d in range(n_chan):
                    at = (e * n_chan + d) * 128
                    ready[d, q, e] = out[:, at : at + 128]
            for j in range(1, n_chan):
                beam_copy(j, q).start()
            pltpu.make_async_copy(ready.at[me_c, q], beams_ref.at[me_c, q], own_sem).start()

        return run_unit

    def store_unit(q):
        def run_unit():
            part = pl.ds(q * per, per)
            pltpu.make_async_copy(held.at[part], sorted_ref.at[part], out_sem).start()

        return run_unit

    def units_of(q):
        units = [join_unit(q)] + [mix_unit(q, e) for e in range(per)] + [place_beams(q)]
        units += [sort_unit(q, e, m) for e in range(per) for m in range(4)]
        return units + [store_unit(q)]

    def z_step(j, q):
        def run_step():
            z_copy(j, q).wait_recv()
            spread(j, q)

        return run_step

    def x_step(j, q):
        for dx in range(1, n_x):
            x_copy(dx, j, q).wait_recv()
            core_copy(dx, j, q).start()

    def weave(units, steps):
        done = 0
        for i, one in enumerate(steps):
            upto = len(units) * (i + 1) // len(steps)
            for unit in units[done:upto]:
                unit()
            done = upto
            one()
        for unit in units[done:]:
            unit()

    def arrive(q):
        if q == 0:
            pltpu.make_async_copy(x_ref.at[me_c], g_ref.at[:, me_c, me_s], keep_sem).wait()
        part = g_ref.at[q, pl.ds(0, n_chan // 2)]
        pltpu.make_async_copy(part, part, cr.at[q]).wait()

    setup = [name_unit(m) for m in range(4)] + [turn_unit]
    setup += [
        weigh_unit(at, left) for at in range(0, beams_n, 16) for left in range(0, inputs, 512)
    ]
    setup.append(place_unit)
    def z_steps(q):
        return [z_step(j, q) for j in range(1, n_chan)] if q < pieces else []

    def x_steps(q):
        return [functools.partial(x_step, j, q) for j in range(n_chan)]

    def mingle(one, two):
        pairs = [(i / len(one), 0, s) for i, s in enumerate(one)]
        pairs += [((i + 0.5) / len(two), 1, s) for i, s in enumerate(two)]
        return [s for _, _, s in sorted(pairs, key=lambda p: p[:2])]

    weave(setup[:7], z_steps(0))
    for q in range(1, pieces + 1):
        steps = mingle(x_steps(q - 1), z_steps(q))
        if q >= 2:
            arrive(q - 2)
            weave(units_of(q - 2), steps)
        else:
            weave(setup[7:], steps)
    arrive(pieces - 1)
    weave(units_of(pieces - 1), [])
    others = pl.ds(0, n_chan - 1)
    pltpu.make_async_copy(ready.at[others], beams_ref.at[others], er).wait()
    pltpu.make_async_copy(x_ref.at[others], x_ref.at[others], zs).wait()
    for dx in range(1, n_x):
        pltpu.make_async_copy(x_ref, x_ref, xs).wait()
    part = g_ref.at[pl.ds(0, pieces // 2)]
    pltpu.make_async_copy(part, part, cs).wait()
    pltpu.make_async_copy(ready.at[others], ready.at[others], es).wait()
    pltpu.make_async_copy(ready.at[me_c], beams_ref.at[me_c], own_sem).wait()
    pltpu.make_async_copy(held, sorted_ref, out_sem).wait()


def front(voltages, taps, counts, names, delays, owner, n_chan, n_sub, most):
    rows = voltages.shape[0]
    beams_n, inputs = delays.shape
    spectra_n = BLOCKS * SPEC
    ch_dev = NCH // n_chan
    n_grp = ch_dev // QUAD
    per = 2
    pieces = n_grp // per
    n_x = n_sub // 2
    tile = 2 * QUAD
    block = spectra_n // 2 * tile
    dma = pltpu.SemaphoreType.DMA
    vmem = pl.BlockSpec(memory_space=pltpu.VMEM)
    travel = (n_chan, pieces, per, spectra_n // 4 * tile, 128)
    return pl.pallas_call(
        functools.partial(front_kernel, n_chan, n_sub, most),
        in_specs=[
            pl.BlockSpec(memory_space=pl.ANY),
            vmem,
            pl.BlockSpec(memory_space=pltpu.SMEM),
            vmem,
            vmem,
            vmem,
        ],
        out_specs=[pl.BlockSpec(memory_space=pl.ANY)] * 2,
        out_shape=[
            jax.ShapeDtypeStruct((n_grp, inputs, 2 * block), jnp.bfloat16),
            jax.ShapeDtypeStruct(travel, jnp.bfloat16),
        ],
        scratch_shapes=[
            pltpu.VMEM((spectra_n + TAPS - 1, rows, 2, NCH), jnp.bfloat16),
            pltpu.VMEM((spectra_n + TAPS - 1, 2 * rows, NCH), jnp.float32),
            pltpu.VMEM((n_chan, pieces, per, block, 128), jnp.bfloat16),
            pltpu.VMEM((pieces, n_chan, n_sub, per, block, 128), jnp.bfloat16),
            pltpu.VMEM((spectra_n * rows, 4 * NCH), jnp.bfloat16),
            pltpu.VMEM((2 * NCH, 4 * NCH), jnp.bfloat16),
            pltpu.VMEM((inputs, inputs), jnp.bfloat16),
            pltpu.VMEM((beams_n, inputs), jnp.int32),
            pltpu.VMEM((2 * per * block, inputs), jnp.bfloat16),
            pltpu.VMEM((n_grp, inputs, 2 * block), jnp.bfloat16),
            pltpu.VMEM((ch_dev, 2 * beams_n, inputs), jnp.bfloat16),
            pltpu.VMEM((per * n_chan * 128, 4 * per * beams_n), jnp.bfloat16),
            pltpu.VMEM(travel, jnp.bfloat16),
            dma,
            dma,
            dma,
            dma,
            dma,
            dma((n_chan - 1, pieces)),
            dma,
            dma((n_x - 1, n_chan, pieces)),
            dma,
            dma((pieces,)),
            dma,
            dma,
        ],
        compiler_params=pltpu.CompilerParams(collective_id=0, has_side_effects=True),
        name="front",
    )(voltages, taps, counts, names, delays, owner)


def back_kernel(
    sub_ref, counts_ref, sorted_ref, heard_ref, taps_ref,
    out_ref, voices_ref,
    all_ref, beams_ref, left_ref, bank_ref, wave_ref, made_ref, mix_ref, voice_ref,
    in_sem, heard_sem, out_sem, voice_sem,
):
    n_grp, inputs, lanes = all_ref.shape
    rows, wide = made_ref.shape[4:]
    frames_n, count = voice_ref.shape[:2]
    spectra_n = frames_n - TAPS + 1
    n_chan = beams_ref.shape[0]
    tile = 2 * QUAD
    mine = pl.ds(pl.multiple_of(sub_ref[0] * rows, rows), rows)

    def in_copy(g):
        return pltpu.make_async_copy(sorted_ref.at[g], all_ref.at[g], in_sem.at[g])

    def out_copy(g, n):
        return pltpu.make_async_copy(
            made_ref.at[g % 2, n],
            out_ref.at[pl.ds(g * QUAD, QUAD), :, :, pl.ds(n * wide, wide)],
            out_sem.at[g % 2, n],
        )

    heard = pltpu.make_async_copy(heard_ref, beams_ref, heard_sem)
    for g in range(n_grp):
        in_copy(g).start()
        if g == 0:
            heard.start()
    total = counts_ref[0]
    for i in range(1, BLOCKS):
        total = total + counts_ref[i]
    scale = 1.0 / jnp.full((8, 128), total.astype(jnp.float32))
    scale = scale[:1, :1]
    lane = lax.broadcasted_iota(jnp.int32, (16, lanes), 1) % QUAD
    keeps = []
    for i in range(QUAD):
        keep = jnp.where(lane == i, 1.0, 0.0).astype(jnp.bfloat16)
        keeps.append(jnp.concatenate([keep] * (rows // 16), axis=0))

    def fill(g):
        plain = all_ref[g, mine, :]
        real, after, before = partner(plain.astype(jnp.float32), lanes)
        turned = jnp.where(real, after, -before).astype(jnp.bfloat16)
        for i in range(QUAD):
            at = 2 * i * rows
            left_ref[g % 2, at : at + rows, :] = plain * keeps[i]
            left_ref[g % 2, at + rows : at + 2 * rows, :] = turned * keeps[i]

    def correlate(g):
        for n in range(inputs // wide):
            product = lax.dot_general(
                left_ref[g % 2],
                all_ref[g, n * wide : (n + 1) * wide, :],
                (((1,), (1,)), ((), ())),
                preferred_element_type=jnp.float32,
            )
            product = (product * scale).astype(jnp.bfloat16)
            for i in range(QUAD):
                for c in range(2):
                    low = (2 * i + c) * rows
                    made_ref[g % 2, n, i, c] = product[low : low + rows]
            out_copy(g, n).start()

    def line_up():
        heard.wait()
        for u in range(0, spectra_n // 4, 2):
            tiles = [
                beams_ref[c, e, u * tile : (u + 2) * tile, :].astype(jnp.float32)
                for c in range(n_chan)
                for e in range(n_grp)
            ]
            for v in range(2):
                stack = jnp.concatenate([t[v * tile : (v + 1) * tile] for t in tiles], axis=0)
                at = (u + v) * 4 * count
                bank_ref[at : at + 4 * count, :] = stack.T.astype(jnp.bfloat16)

    def transform():
        trig = trig_of((2 * NCH, 2 * NCH), n_grp)
        high = trig.astype(jnp.bfloat16)
        low = (trig - high.astype(jnp.float32)).astype(jnp.bfloat16)
        wave_ref[...] = jnp.dot(
            bank_ref[...], high, preferred_element_type=jnp.float32
        ) + jnp.dot(bank_ref[...], low, preferred_element_type=jnp.float32)

    def speak(first):
        run = min(VOICES, frames_n - first)
        for c in range(2):
            lanes = slice(c * NCH, (c + 1) * NCH)
            taps = [taps_ref[k : k + 1, :] for k in range(TAPS)]
            for p in range(0, count, 8):
                window = {
                    s: wave_ref[s * count + p : s * count + p + 8, lanes]
                    for s in range(max(0, first - TAPS + 1), min(spectra_n, first + run))
                }
                for j in range(run):
                    terms = [
                        window[first + j - k] * taps[k]
                        for k in range(TAPS)
                        if 0 <= first + j - k < spectra_n
                    ]
                    total = terms[0]
                    for term in terms[1:]:
                        total = total + term
                    mix_ref[first + j, pl.ds(2 * p + c, 8, stride=2), :] = total
        for j in range(run):
            voice_ref[first + j] = mix_ref[first + j].reshape(count, 2, NCH)
            pltpu.make_async_copy(
                voice_ref.at[first + j],
                voices_ref.at[:, :, pl.ds((first + j) * NCH, NCH)],
                voice_sem,
            ).start()

    jobs = [line_up, transform]
    jobs += [functools.partial(speak, first) for first in range(0, frames_n, VOICES)]
    shares = n_grp - 1
    done = 0
    in_copy(0).wait()
    fill(0)
    for g in range(n_grp):
        if g >= 2:
            for n in range(inputs // wide):
                out_copy(g - 2, n).wait()
        if g + 1 < n_grp:
            in_copy(g + 1).wait()
            fill(g + 1)
        correlate(g)
        upto = min(len(jobs), -(-len(jobs) * (g + 1) // shares))
        for job in jobs[done:upto]:
            job()
        done = upto
    for g in range(n_grp - 2, n_grp):
        for n in range(inputs // wide):
            out_copy(g, n).wait()
    pltpu.make_async_copy(voice_ref, voice_ref, voice_sem).wait()


def back(by_id, beams, taps, counts, sub_index, rows, count):
    n_grp, inputs, lanes = by_id.shape
    n_chan = beams.shape[0]
    beams = beams.reshape((n_chan, n_grp) + beams.shape[3:])
    spectra_n = BLOCKS * SPEC
    frames_n = spectra_n + TAPS - 1
    wide = 512
    hbm = pl.BlockSpec(memory_space=pl.ANY)
    smem = pl.BlockSpec(memory_space=pltpu.SMEM)
    return pl.pallas_call(
        back_kernel,
        in_specs=[smem, smem, hbm, hbm, pl.BlockSpec(memory_space=pltpu.VMEM)],
        out_specs=[hbm, hbm],
        scratch_shapes=[
            pltpu.VMEM(by_id.shape, jnp.bfloat16),
            pltpu.VMEM(beams.shape, jnp.bfloat16),
            pltpu.VMEM((2, 2 * QUAD * rows, lanes), jnp.bfloat16),
            pltpu.VMEM((spectra_n * count, 2 * NCH), jnp.bfloat16),
            pltpu.VMEM((spectra_n * count, 2 * NCH), jnp.float32),
            pltpu.VMEM((2, inputs // wide, QUAD, 2, rows, wide), jnp.bfloat16),
            pltpu.VMEM((frames_n, 2 * count, NCH), jnp.float32),
            pltpu.VMEM((frames_n, count, 2, NCH), jnp.float32),
            pltpu.SemaphoreType.DMA((n_grp,)),
            pltpu.SemaphoreType.DMA,
            pltpu.SemaphoreType.DMA((2, inputs // wide)),
            pltpu.SemaphoreType.DMA,
        ],
        out_shape=[
            jax.ShapeDtypeStruct((n_grp * QUAD, 2, rows, inputs), jnp.bfloat16),
            jax.ShapeDtypeStruct((count, 2, frames_n * NCH), jnp.float32),
        ],
        name="back",
    )(sub_index, counts, by_id, beams, taps)


def local(voltages, taps, input_id, counts, delays, beam_owner):
    n_chan = lax.axis_size("chan")
    n_sub = lax.axis_size("sub")
    inp_dev = voltages.shape[0]
    inputs = input_id.shape[0]
    spectra_n = BLOCKS * SPEC
    ch_dev = NCH // n_chan
    rows = inputs // n_sub
    section = BEAMS // n_sub
    most = min(section, max(2, 2 * section // n_chan))
    fits = inp_dev == 64 and most == 32 and section == 64 and NCH == 128
    fits = fits and n_sub % 2 == 0 and ch_dev % (2 * QUAD) == 0 and inputs % 512 == 0
    if not fits or n_sub != 4 or n_chan % 2 or n_chan > 8 or rows % 128:
        return local_plain(voltages, taps, input_id, counts, delays, beam_owner)
    sub_index = lax.axis_index("sub")
    owner = lax.dynamic_slice_in_dim(beam_owner[:, 0], sub_index * section, section)[None]
    taps2 = taps.reshape(TAPS, NCH)
    names = input_id[None]
    by_id, beams = front(voltages, taps2, counts, names, delays, owner, n_chan, n_sub, most)
    visibility, resynth = back(
        by_id, beams, taps2, counts, sub_index.astype(jnp.int32)[None], rows, most
    )
    return (visibility, resynth)


def solution(mesh):
    placed = (
        P(("grp", "chan", "sub"), None, None),
        P(),
        P(),
        P("grp"),
        P(("grp", "sub"), None),
        P("grp", None),
    )
    return jax.shard_map(
        local,
        mesh=mesh,
        in_specs=placed,
        out_specs=(P(("grp", "chan"), None, "sub", None), P(("grp", "chan", "sub"), None, None)),
        check_vma=False,
    )
```

```python
import functools
import math

import jax
import jax.numpy as jnp
from jax import lax
from jax.experimental import pallas as pl
from jax.experimental.pallas import tpu as pltpu
from jax.sharding import PartitionSpec as P

NCH = 128
TAPS = 12
SPEC = 8
BLOCKS = 4
BEAMS = 256


def filter_table(taps, chans):
    length = taps.shape[0]
    position = jnp.arange(length, dtype=jnp.int32) % chans
    channel = jnp.arange(chans, dtype=jnp.int32)
    phase = (position[:, None] * channel[None, :] % chans).astype(jnp.float32) * (
        2.0 * math.pi / chans
    )
    cosine = taps[:, None] * jnp.cos(phase)
    sine = taps[:, None] * jnp.sin(phase)
    upper = jnp.concatenate([cosine, -sine], axis=1)
    lower = jnp.concatenate([sine, cosine], axis=1)
    return jnp.concatenate([upper, lower], axis=0).astype(jnp.bfloat16)


def resynthesize(received, table, taps_count, chans):
    count = received.shape[0]
    spectra_n = received.shape[3]
    table3 = table.reshape(2 * taps_count * chans, 2, chans)
    grid = jnp.einsum("pcht,mch->ptm", received, table3, preferred_element_type=jnp.float32)
    grid = grid.reshape(count, spectra_n, 2, taps_count, chans)
    total = jnp.zeros((count, spectra_n + taps_count - 1, 2, chans), jnp.float32)
    for k in range(taps_count):
        total = total + jnp.pad(
            grid[:, :, :, k, :], ((0, 0), (k, taps_count - 1 - k), (0, 0), (0, 0))
        )
    return jnp.transpose(total, (0, 2, 1, 3)).reshape(
        count, 2, (spectra_n + taps_count - 1) * chans
    )


def local_plain(voltages, taps, input_id, counts, delays, beam_owner):
    n_chan = lax.axis_size("chan")
    n_sub = lax.axis_size("sub")
    inp_dev = voltages.shape[0]
    inputs = input_id.shape[0]
    chans = NCH
    taps_count = TAPS
    spectra_n = BLOCKS * SPEC
    ch_dev = chans // n_chan
    rows = inputs // n_sub
    section = BEAMS // n_sub
    most = min(section, max(2, 2 * section // n_chan))
    table = filter_table(taps, chans)
    position = jnp.arange(spectra_n, dtype=jnp.int32)
    valid = (position % SPEC < jnp.repeat(counts, SPEC)).astype(jnp.float32)
    total = jnp.sum(counts.astype(jnp.float32))
    frames = voltages.reshape(inp_dev, 2, spectra_n + taps_count - 1, chans)
    windows = jnp.concatenate(
        [frames[:, :, k : k + spectra_n, :] for k in range(taps_count)], axis=3
    )
    table3 = table.reshape(2, taps_count * chans, 2 * chans)
    filtered = jnp.einsum("icth,chm->mit", windows, table3, preferred_element_type=jnp.float32)
    filtered = filtered * valid[None, None, :]
    spectra = filtered.reshape(2, chans, inp_dev, spectra_n).astype(jnp.bfloat16)
    slot_of = jnp.zeros((inputs,), jnp.int32).at[input_id].set(jnp.arange(inputs, dtype=jnp.int32))
    turned = lax.all_to_all(spectra, "chan", split_axis=1, concat_axis=2, tiled=True)
    gathered = lax.all_gather(turned, "sub", axis=2, tiled=True)
    chan_part = slot_of // (n_sub * inp_dev)
    sub_part = slot_of // inp_dev % n_sub
    order = (sub_part * n_chan + chan_part) * inp_dev + slot_of % inp_dev
    by_id = jnp.take(gathered, order, axis=2)
    sub_index = lax.axis_index("sub")
    mine = lax.dynamic_slice_in_dim(by_id, sub_index * rows, rows, 2)
    real_part = jnp.einsum("cxit,cxjt->xij", mine, by_id, preferred_element_type=jnp.float32)
    imag_part = jnp.einsum("xit,xjt->xij", mine[1], by_id[0], preferred_element_type=jnp.float32)
    imag_part = imag_part - jnp.einsum(
        "xit,xjt->xij", mine[0], by_id[1], preferred_element_type=jnp.float32
    )
    visibility = (jnp.stack([real_part, imag_part], axis=1) / total).astype(jnp.bfloat16)
    channel = lax.axis_index("chan") * ch_dev + jnp.arange(ch_dev, dtype=jnp.int32)
    phase = (delays[None, :, :] * channel[:, None, None] % chans).astype(jnp.float32) * (
        2.0 * math.pi / chans
    )
    scale = 1.0 / math.sqrt(inputs)
    weight_cos = (jnp.cos(phase) * scale).astype(jnp.bfloat16)
    weight_sin = (jnp.sin(phase) * scale).astype(jnp.bfloat16)
    from_cos = jnp.einsum("xbi,cxit->cxbt", weight_cos, by_id, preferred_element_type=jnp.float32)
    from_sin = jnp.einsum("xbi,cxit->cxbt", weight_sin, by_id, preferred_element_type=jnp.float32)
    beams = jnp.stack([from_cos[0] - from_sin[1], from_cos[1] + from_sin[0]]).astype(jnp.bfloat16)
    owner = lax.dynamic_slice_in_dim(beam_owner[:, 0], sub_index * section, section)
    beam = jnp.arange(section, dtype=jnp.int32)
    earlier = (owner[None, :] == owner[:, None]) & (beam[None, :] < beam[:, None])
    rank = jnp.sum(earlier.astype(jnp.int32), axis=1)
    target = owner * most + rank
    select = (jnp.arange(n_chan * most, dtype=jnp.int32)[:, None] == target[None, :]).astype(
        jnp.bfloat16
    )
    placed = jnp.einsum("pb,cxbt->pcxt", select, beams, preferred_element_type=jnp.float32).astype(
        jnp.bfloat16
    )
    placed = placed.reshape(n_chan, most, 2, ch_dev, spectra_n)
    resynth = resynthesize(
        lax.all_to_all(placed, "chan", split_axis=0, concat_axis=3, tiled=True)[0],
        table,
        taps_count,
        chans,
    )
    return (visibility, resynth)


def turn_of(steps):
    quarter = NCH // 4
    turn = steps & (NCH - 1)
    quadrant = (turn + quarter // 2) >> (quarter.bit_length() - 1)
    x = (turn - quadrant * quarter).astype(jnp.float32) * (2.0 * math.pi / NCH)
    y = x * x
    even = 1.0 + y * (-1 / 2 + y * (1 / 24 + y * (-1 / 720 + y * (1 / 40320))))
    odd = x * (1.0 + y * (-1 / 6 + y * (1 / 120 + y * (-1 / 5040 + y * (1 / 362880)))))
    swap = (quadrant & 1) == 1
    cosine, sine = jnp.where(swap, odd, even), jnp.where(swap, even, odd)
    cosine = jnp.where(((quadrant + 1) & 2) == 2, -cosine, cosine)
    return cosine, jnp.where((quadrant & 2) == 2, -sine, sine)


def weigh(first, scale, delay_ref, out_ref, at, left, high, wide):
    beams_n = delay_ref.shape[0]
    delay = delay_ref[at : at + high, left : left + wide]
    step_cos, step_sin = turn_of(delay)
    cosine, sine = turn_of(delay * first)

    def body(f, held):
        cosine, sine = held
        out_ref[f, at : at + high, left : left + wide] = cosine.astype(jnp.bfloat16)
        low = at + beams_n
        out_ref[f, low : low + high, left : left + wide] = sine.astype(jnp.bfloat16)
        return (
            cosine * step_cos - sine * step_sin,
            sine * step_cos + cosine * step_sin,
        )

    lax.fori_loop(0, out_ref.shape[0], body, (cosine * scale, sine * scale))


QUAD = 4
VOICES = 4


def trig_of(shape, n_grp):
    row = lax.broadcasted_iota(jnp.int32, shape, 0)
    lane = lax.broadcasted_iota(jnp.int32, shape, 1)
    tile = 2 * QUAD
    part = row // QUAD % 2
    channel = row // tile * QUAD + row % QUAD
    to_part = lane // NCH
    cosine, sine = turn_of(channel * (lane % NCH))
    return jnp.where(part == to_part, cosine, jnp.where(to_part == 1, sine, -sine))


def partner(x, lanes):
    pieces = [x[:, at : at + 128] for at in range(0, lanes, 128)]
    after = jnp.concatenate([pltpu.roll(p, 128 - QUAD, 1) for p in pieces], axis=1)
    before = jnp.concatenate([pltpu.roll(p, QUAD, 1) for p in pieces], axis=1)
    lane = lax.broadcasted_iota(jnp.int32, x.shape, 1)
    return lane // QUAD % 2 == 0, after, before


def front_kernel(
    n_chan, n_sub, most,
    volt_ref, taps_ref, counts_ref, name_ref, delay_ref, owner_ref,
    sorted_ref, beams_ref,
    v_ref, wide_ref, x_ref, g_ref, y_ref, d_ref, perm_ref, turn_ref, c_ref, held, weight_ref,
    place_ref, ready,
    load_sem, own_sem, out_sem, keep_sem, zs, zr, xs, xr, cs, cr, es, er,
):
    me_c, me_s = lax.axis_index("chan"), lax.axis_index("sub")
    core, across = me_s % 2, me_s // 2
    n_x = n_sub // 2
    twin = me_s + 1 - 2 * core
    mesh_id = pl.DeviceIdType.MESH
    pieces, per = x_ref.shape[1], x_ref.shape[2]
    n_grp = pieces * per
    spectra_n = BLOCKS * SPEC
    frames_n, rows = v_ref.shape[:2]
    inputs = name_ref.shape[1]
    beams_n = delay_ref.shape[0]
    ch_dev = n_grp * QUAD
    tile = 2 * QUAD
    wide = 2 * NCH
    block = x_ref.shape[3]

    def chan_of(k):
        at = me_c
        bit = 1
        while bit < n_chan:
            if k & bit:
                at = at + bit - 2 * bit * (me_c // bit % 2)
            bit *= 2
        return at

    def sub_of(offset):
        return (across + offset) % n_x * 2 + core

    barrier = pltpu.get_barrier_semaphore()
    for j in range(1, n_chan):
        pl.semaphore_signal(barrier, device_id={"chan": chan_of(j)}, device_id_type=mesh_id)
    for j in range(1, n_x):
        pl.semaphore_signal(barrier, device_id={"sub": sub_of(j)}, device_id_type=mesh_id)
    pl.semaphore_signal(barrier, device_id={"sub": twin}, device_id_type=mesh_id)

    for s in range(frames_n):
        pltpu.make_async_copy(
            volt_ref.at[:, :, pl.ds(s * NCH, NCH)], v_ref.at[s], load_sem
        ).start()

    def z_copy(j, q):
        return pltpu.make_async_remote_copy(
            src_ref=x_ref.at[chan_of(j), q],
            dst_ref=g_ref.at[q, me_c, me_s],
            send_sem=zs,
            recv_sem=zr.at[j - 1, q],
            device_id={"chan": chan_of(j)},
            device_id_type=mesh_id,
        )

    def source(j, q):
        if j == 0:
            return x_ref.at[me_c, q]
        return g_ref.at[q, chan_of(j), me_s]

    def x_copy(dx, j, q):
        return pltpu.make_async_remote_copy(
            src_ref=source(j, q),
            dst_ref=g_ref.at[q, chan_of(j), me_s],
            send_sem=xs,
            recv_sem=xr.at[dx - 1, j, q],
            device_id={"sub": sub_of(dx)},
            device_id_type=mesh_id,
        )

    def core_copy(dx, j, q):
        home = g_ref.at[q, chan_of(j), sub_of(n_x - dx)]
        return pltpu.make_async_remote_copy(
            src_ref=source(j, q) if dx == 0 else home,
            dst_ref=home,
            send_sem=cs,
            recv_sem=cr.at[q],
            device_id={"sub": twin},
            device_id_type=mesh_id,
        )

    def beam_copy(j, q):
        return pltpu.make_async_remote_copy(
            src_ref=ready.at[chan_of(j), q],
            dst_ref=beams_ref.at[me_c, q],
            send_sem=es,
            recv_sem=er,
            device_id={"chan": chan_of(j)},
            device_id_type=mesh_id,
        )

    trig = trig_of((n_chan * n_grp * tile, wide), n_grp)
    high = trig.astype(jnp.bfloat16)
    d_ref[:, :wide] = high
    d_ref[:, wide:] = (trig - high.astype(jnp.float32)).astype(jnp.bfloat16)

    valid = []
    for t in range(spectra_n):
        valid.append(jnp.where(counts_ref[t // SPEC] > t % SPEC, 1.0, 0.0))
    step = 16
    run = 4
    pltpu.make_async_copy(v_ref, v_ref, load_sem).wait()
    for s in range(frames_n):
        wide_ref[s] = v_ref[s].reshape(2 * rows, NCH).astype(jnp.float32)

    for c in range(2):

        @pl.loop(0, rows // step)
        def _(it):
            at = pl.multiple_of(it * step, step)
            taps = [taps_ref[k : k + 1, :] for k in range(TAPS)]
            for first in range(0, spectra_n, run):
                window = [
                    wide_ref[s, pl.ds(2 * at + c, step, stride=2), :]
                    for s in range(first, first + run + TAPS - 1)
                ]
                for j in range(run):
                    t = first + j
                    total = window[j] * taps[0]
                    for k in range(1, TAPS):
                        total = total + window[j + k] * taps[k]
                    total = total * valid[t]
                    high = total.astype(jnp.bfloat16)
                    low = (total - high.astype(jnp.float32)).astype(jnp.bfloat16)
                    slot = t // 2 * 2 + (t % 2 + core) % 2
                    to = pl.multiple_of(slot * rows + at, step)
                    y_ref[pl.ds(to, step), c * NCH : (c + 1) * NCH] = high
                    y_ref[pl.ds(to, step), wide + c * NCH : wide + (c + 1) * NCH] = low

    across_dims = (((1,), (1,)), ((), ()))

    @pl.loop(0, spectra_n // 4, unroll=2)
    def _(u):
        at = pl.multiple_of(u * 4 * rows, 4 * rows)
        high = y_ref[pl.ds(at, 4 * rows), :wide]
        low = y_ref[pl.ds(at, 4 * rows), wide:]
        out = lax.dot_general(d_ref[:, :wide], high, across_dims, preferred_element_type=jnp.float32)
        out = out + lax.dot_general(
            d_ref[:, wide:], high, across_dims, preferred_element_type=jnp.float32
        )
        out = out + lax.dot_general(
            d_ref[:, :wide], low, across_dims, preferred_element_type=jnp.float32
        )
        to = pl.multiple_of(u * 2 * tile, 2 * tile)
        for d in range(n_chan):
            for q in range(pieces):
                for e in range(per):
                    row = ((d * pieces + q) * per + e) * tile
                    both = jnp.concatenate(
                        [out[row : row + tile, :128], out[row : row + tile, 128:]], axis=0
                    )
                    x_ref[d, q, e, pl.ds(to, 2 * tile), :] = both.astype(jnp.bfloat16)

    pl.semaphore_wait(barrier, n_chan + n_x - 1)
    def spread(j, q):
        for dx in range(1, n_x):
            x_copy(dx, j, q).start()
        core_copy(0, j, q).start()

    for q in range(pieces):
        for j in range(1, n_chan):
            z_copy(j, q).start()
    for q in range(pieces):
        spread(0, q)
    for q in range(pieces):
        pltpu.make_async_copy(x_ref.at[me_c, q], g_ref.at[q, me_c, me_s], keep_sem).start()

    half = inputs // 4
    first = me_c * ch_dev
    scale = 1.0 / math.sqrt(inputs)

    def name_unit(m):
        def run_unit():
            low = lax.broadcasted_iota(jnp.int32, (half, inputs), 0) + m * half
            perm_ref[m * half : (m + 1) * half, :] = jnp.where(
                name_ref[...] == low, 1.0, 0.0
            ).astype(jnp.bfloat16)

        return run_unit

    def turn_unit():
        turned = jnp.dot(
            delay_ref[...].astype(jnp.float32).astype(jnp.bfloat16),
            perm_ref[...],
            preferred_element_type=jnp.float32,
        )
        turn_ref[...] = turned.astype(jnp.int32)

    def weigh_unit(at, left):
        return lambda: weigh(first, scale, turn_ref, weight_ref, at, left, 16, 512)

    def place_unit():
        lanes = per * beams_n
        own = owner_ref[:, :beams_n] * (me_s == 0).astype(jnp.int32)
        for s in range(1, n_sub):
            own = own + owner_ref[:, s * beams_n : (s + 1) * beams_n] * (me_s == s).astype(
                jnp.int32
            )
        owner = jnp.concatenate([own] * per, axis=1)
        named = (lax.broadcasted_iota(jnp.int32, (8, lanes), 0) == owner).astype(jnp.float32)
        row = lax.broadcasted_iota(jnp.int32, (lanes, lanes), 0)
        lane = lax.broadcasted_iota(jnp.int32, (lanes, lanes), 1)
        before = (row < lane) & (row // beams_n == lane // beams_n)
        rank = jnp.dot(
            named.astype(jnp.bfloat16),
            jnp.where(before, 1.0, 0.0).astype(jnp.bfloat16),
            preferred_element_type=jnp.float32,
        )
        rank = jnp.sum(named * rank, axis=0, keepdims=True).astype(jnp.int32)
        lane = lax.broadcasted_iota(jnp.int32, (1, lanes), 1)
        slot = (lane // beams_n * n_chan + owner) * (4 * most) + rank
        row = lax.broadcasted_iota(jnp.int32, (place_ref.shape[0], lanes), 0)
        for m in range(4):
            place_ref[:, m * lanes : (m + 1) * lanes] = jnp.where(
                row == slot + m * most, 1.0, 0.0
            ).astype(jnp.bfloat16)

    def join_unit(q):
        def run_unit():
            left = lax.broadcasted_iota(jnp.int32, (block, 128), 1) < 64
            for e in range(per):
                low = 2 * e * block
                for c in range(n_chan):
                    for x in range(n_x):
                        a = g_ref[q, c, 2 * x, e].astype(jnp.float32)
                        b = g_ref[q, c, 2 * x + 1, e].astype(jnp.float32)
                        at = (c * n_x + x) * 128
                        c_ref[low : low + block, at : at + 128] = jnp.where(left, a, b).astype(
                            jnp.bfloat16
                        )
                        c_ref[low + block : low + 2 * block, at : at + 128] = pltpu.roll(
                            jnp.where(left, b, a), 64, 1
                        ).astype(jnp.bfloat16)

        return run_unit

    def sort_unit(q, e, m):
        def run_unit():
            held[q * per + e, m * half : (m + 1) * half, :] = lax.dot_general(
                perm_ref[m * half : (m + 1) * half, :],
                c_ref[2 * e * block : 2 * (e + 1) * block, :],
                across_dims,
                preferred_element_type=jnp.float32,
            ).astype(jnp.bfloat16)

        return run_unit

    mixes = {}

    def mix_unit(q, e):
        def run_unit():
            at = q * per + e
            lane = lax.broadcasted_iota(jnp.int32, (2 * beams_n, 2 * block), 1)
            total = None
            for f in range(QUAD):
                mixed = lax.dot_general(
                    weight_ref[at * QUAD + f],
                    c_ref[2 * e * block : 2 * (e + 1) * block, :],
                    across_dims,
                    preferred_element_type=jnp.float32,
                )
                total = mixed if total is None else jnp.where(lane % QUAD == f, mixed, total)
            real, after, before = partner(total[beams_n:], 2 * block)
            mixes[q, e] = total[:beams_n] + jnp.where(real, -after, before)

        return run_unit

    def place_beams(q):
        def run_unit():
            both = jnp.concatenate([mixes.pop((q, e)) for e in range(per)], axis=0)
            turned = both.T
            parts = []
            for m in range(4):
                parity, u = m % 2, m // 2
                picks = [
                    turned[parity * block + v * 2 * tile + u * tile :][:tile]
                    for v in range(spectra_n // 4)
                ]
                parts.append(jnp.concatenate(picks, axis=0))
            lined = jnp.concatenate(parts, axis=1).astype(jnp.bfloat16)
            out = lax.dot_general(
                lined, place_ref[...], across_dims, preferred_element_type=jnp.float32
            ).astype(jnp.bfloat16)
            for e in range(per):
                for d in range(n_chan):
                    at = (e * n_chan + d) * 128
                    ready[d, q, e] = out[:, at : at + 128]
            for j in range(n_chan - 1, 0, -1):
                beam_copy(j, q).start()
            pltpu.make_async_copy(ready.at[me_c, q], beams_ref.at[me_c, q], own_sem).start()

        return run_unit

    def store_unit(q):
        def run_unit():
            part = pl.ds(q * per, per)
            pltpu.make_async_copy(held.at[part], sorted_ref.at[part], out_sem).start()

        return run_unit

    def units_of(q):
        units = [join_unit(q)] + [mix_unit(q, e) for e in range(per)] + [place_beams(q)]
        units += [sort_unit(q, e, m) for e in range(per) for m in range(4)]
        return units + [store_unit(q)]

    def z_step(j, q):
        def run_step():
            z_copy(j, q).wait_recv()
            spread(j, q)

        return run_step

    def x_step(j, q):
        for dx in range(1, n_x):
            x_copy(dx, j, q).wait_recv()
            core_copy(dx, j, q).start()

    def weave(units, steps):
        done = 0
        for i, one in enumerate(steps):
            upto = len(units) * (i + 1) // len(steps)
            for unit in units[done:upto]:
                unit()
            done = upto
            one()
        for unit in units[done:]:
            unit()

    def arrive(q):
        if q == 0:
            pltpu.make_async_copy(x_ref.at[me_c], g_ref.at[:, me_c, me_s], keep_sem).wait()
        part = g_ref.at[q, pl.ds(0, n_chan // 2)]
        pltpu.make_async_copy(part, part, cr.at[q]).wait()

    setup = [name_unit(m) for m in range(4)] + [turn_unit]
    setup += [
        weigh_unit(at, left) for at in range(0, beams_n, 16) for left in range(0, inputs, 512)
    ]
    setup.append(place_unit)
    def z_steps(q):
        return [z_step(j, q) for j in range(1, n_chan)] if q < pieces else []

    def x_steps(q):
        return [functools.partial(x_step, j, q) for j in range(n_chan)]

    def mingle(one, two):
        pairs = [(i / len(one), 0, s) for i, s in enumerate(one)]
        pairs += [((i + 0.5) / len(two), 1, s) for i, s in enumerate(two)]
        return [s for _, _, s in sorted(pairs, key=lambda p: p[:2])]

    weave(setup[:7], z_steps(0))
    for q in range(1, pieces + 1):
        steps = mingle(x_steps(q - 1), z_steps(q))
        if q >= 2:
            arrive(q - 2)
            weave(units_of(q - 2), steps)
        else:
            weave(setup[7:], steps)
    arrive(pieces - 1)
    weave(units_of(pieces - 1), [])
    others = pl.ds(0, n_chan - 1)
    pltpu.make_async_copy(ready.at[others], beams_ref.at[others], er).wait()
    pltpu.make_async_copy(x_ref.at[others], x_ref.at[others], zs).wait()
    for dx in range(1, n_x):
        pltpu.make_async_copy(x_ref, x_ref, xs).wait()
    part = g_ref.at[pl.ds(0, pieces // 2)]
    pltpu.make_async_copy(part, part, cs).wait()
    pltpu.make_async_copy(ready.at[others], ready.at[others], es).wait()
    pltpu.make_async_copy(ready.at[me_c], beams_ref.at[me_c], own_sem).wait()
    pltpu.make_async_copy(held, sorted_ref, out_sem).wait()


def front(voltages, taps, counts, names, delays, owner, n_chan, n_sub, most):
    rows = voltages.shape[0]
    beams_n, inputs = delays.shape
    spectra_n = BLOCKS * SPEC
    ch_dev = NCH // n_chan
    n_grp = ch_dev // QUAD
    per = 2
    pieces = n_grp // per
    n_x = n_sub // 2
    tile = 2 * QUAD
    block = spectra_n // 2 * tile
    dma = pltpu.SemaphoreType.DMA
    vmem = pl.BlockSpec(memory_space=pltpu.VMEM)
    travel = (n_chan, pieces, per, spectra_n // 4 * tile, 128)
    return pl.pallas_call(
        functools.partial(front_kernel, n_chan, n_sub, most),
        in_specs=[
            pl.BlockSpec(memory_space=pl.ANY),
            vmem,
            pl.BlockSpec(memory_space=pltpu.SMEM),
            vmem,
            vmem,
            vmem,
        ],
        out_specs=[pl.BlockSpec(memory_space=pl.ANY)] * 2,
        out_shape=[
            jax.ShapeDtypeStruct((n_grp, inputs, 2 * block), jnp.bfloat16),
            jax.ShapeDtypeStruct(travel, jnp.bfloat16),
        ],
        scratch_shapes=[
            pltpu.VMEM((spectra_n + TAPS - 1, rows, 2, NCH), jnp.bfloat16),
            pltpu.VMEM((spectra_n + TAPS - 1, 2 * rows, NCH), jnp.float32),
            pltpu.VMEM((n_chan, pieces, per, block, 128), jnp.bfloat16),
            pltpu.VMEM((pieces, n_chan, n_sub, per, block, 128), jnp.bfloat16),
            pltpu.VMEM((spectra_n * rows, 4 * NCH), jnp.bfloat16),
            pltpu.VMEM((2 * NCH, 4 * NCH), jnp.bfloat16),
            pltpu.VMEM((inputs, inputs), jnp.bfloat16),
            pltpu.VMEM((beams_n, inputs), jnp.int32),
            pltpu.VMEM((2 * per * block, inputs), jnp.bfloat16),
            pltpu.VMEM((n_grp, inputs, 2 * block), jnp.bfloat16),
            pltpu.VMEM((ch_dev, 2 * beams_n, inputs), jnp.bfloat16),
            pltpu.VMEM((per * n_chan * 128, 4 * per * beams_n), jnp.bfloat16),
            pltpu.VMEM(travel, jnp.bfloat16),
            dma,
            dma,
            dma,
            dma,
            dma,
            dma((n_chan - 1, pieces)),
            dma,
            dma((n_x - 1, n_chan, pieces)),
            dma,
            dma((pieces,)),
            dma,
            dma,
        ],
        compiler_params=pltpu.CompilerParams(collective_id=0, has_side_effects=True),
        name="front",
    )(voltages, taps, counts, names, delays, owner)


def back_kernel(
    sub_ref, counts_ref, sorted_ref, heard_ref, taps_ref,
    out_ref, voices_ref,
    all_ref, beams_ref, left_ref, bank_ref, wave_ref, made_ref, mix_ref, voice_ref,
    in_sem, heard_sem, out_sem, voice_sem,
):
    n_grp, inputs, lanes = all_ref.shape
    rows, wide = made_ref.shape[4:]
    frames_n, count = voice_ref.shape[:2]
    spectra_n = frames_n - TAPS + 1
    n_chan = beams_ref.shape[0]
    tile = 2 * QUAD
    mine = pl.ds(pl.multiple_of(sub_ref[0] * rows, rows), rows)

    def in_copy(g):
        return pltpu.make_async_copy(sorted_ref.at[g], all_ref.at[g], in_sem.at[g])

    def out_copy(g, n):
        return pltpu.make_async_copy(
            made_ref.at[g % 2, n],
            out_ref.at[pl.ds(g * QUAD, QUAD), :, :, pl.ds(n * wide, wide)],
            out_sem.at[g % 2, n],
        )

    heard = pltpu.make_async_copy(heard_ref, beams_ref, heard_sem)
    in_copy(0).start()
    in_copy(1).start()
    heard.start()
    total = counts_ref[0]
    for i in range(1, BLOCKS):
        total = total + counts_ref[i]
    scale = 1.0 / jnp.full((8, 128), total.astype(jnp.float32))
    scale = scale[:1, :1]
    lane = lax.broadcasted_iota(jnp.int32, (16, lanes), 1) % QUAD
    keeps = []
    for i in range(QUAD):
        keep = jnp.where(lane == i, 1.0, 0.0).astype(jnp.bfloat16)
        keeps.append(jnp.concatenate([keep] * (rows // 16), axis=0))

    def fill(g):
        plain = all_ref[g, mine, :]
        real, after, before = partner(plain.astype(jnp.float32), lanes)
        turned = jnp.where(real, after, -before).astype(jnp.bfloat16)
        for i in range(QUAD):
            at = 2 * i * rows
            left_ref[g % 2, at : at + rows, :] = plain * keeps[i]
            left_ref[g % 2, at + rows : at + 2 * rows, :] = turned * keeps[i]

    def correlate(g):
        for n in range(inputs // wide):
            product = lax.dot_general(
                left_ref[g % 2],
                all_ref[g, n * wide : (n + 1) * wide, :],
                (((1,), (1,)), ((), ())),
                preferred_element_type=jnp.float32,
            )
            product = (product * scale).astype(jnp.bfloat16)
            for i in range(QUAD):
                for c in range(2):
                    low = (2 * i + c) * rows
                    made_ref[g % 2, n, i, c] = product[low : low + rows]
            out_copy(g, n).start()

    def line_up():
        heard.wait()
        for u in range(0, spectra_n // 4, 2):
            tiles = [
                beams_ref[c, e, u * tile : (u + 2) * tile, :].astype(jnp.float32)
                for c in range(n_chan)
                for e in range(n_grp)
            ]
            for v in range(2):
                stack = jnp.concatenate([t[v * tile : (v + 1) * tile] for t in tiles], axis=0)
                at = (u + v) * 4 * count
                bank_ref[at : at + 4 * count, :] = stack.T.astype(jnp.bfloat16)

    def transform():
        trig = trig_of((2 * NCH, 2 * NCH), n_grp)
        high = trig.astype(jnp.bfloat16)
        low = (trig - high.astype(jnp.float32)).astype(jnp.bfloat16)
        wave_ref[...] = jnp.dot(
            bank_ref[...], high, preferred_element_type=jnp.float32
        ) + jnp.dot(bank_ref[...], low, preferred_element_type=jnp.float32)

    def speak(first):
        run = min(VOICES, frames_n - first)
        for c in range(2):
            lanes = slice(c * NCH, (c + 1) * NCH)
            taps = [taps_ref[k : k + 1, :] for k in range(TAPS)]
            for p in range(0, count, 8):
                window = {
                    s: wave_ref[s * count + p : s * count + p + 8, lanes]
                    for s in range(max(0, first - TAPS + 1), min(spectra_n, first + run))
                }
                for j in range(run):
                    terms = [
                        window[first + j - k] * taps[k]
                        for k in range(TAPS)
                        if 0 <= first + j - k < spectra_n
                    ]
                    total = terms[0]
                    for term in terms[1:]:
                        total = total + term
                    mix_ref[first + j, pl.ds(2 * p + c, 8, stride=2), :] = total
        for j in range(run):
            voice_ref[first + j] = mix_ref[first + j].reshape(count, 2, NCH)
            pltpu.make_async_copy(
                voice_ref.at[first + j],
                voices_ref.at[:, :, pl.ds((first + j) * NCH, NCH)],
                voice_sem,
            ).start()

    jobs = [line_up, transform]
    jobs += [functools.partial(speak, first) for first in range(0, frames_n, VOICES)]
    shares = n_grp - 1
    done = 0
    in_copy(0).wait()
    fill(0)
    for g in range(n_grp):
        if g >= 2:
            for n in range(inputs // wide):
                out_copy(g - 2, n).wait()
        if g + 1 < n_grp:
            in_copy(g + 1).wait()
            if g + 2 < n_grp:
                in_copy(g + 2).start()
            fill(g + 1)
        correlate(g)
        upto = min(len(jobs), -(-len(jobs) * (g + 1) // shares))
        for job in jobs[done:upto]:
            job()
        done = upto
    for g in range(n_grp - 2, n_grp):
        for n in range(inputs // wide):
            out_copy(g, n).wait()
    pltpu.make_async_copy(voice_ref, voice_ref, voice_sem).wait()


def back(by_id, beams, taps, counts, sub_index, rows, count):
    n_grp, inputs, lanes = by_id.shape
    n_chan = beams.shape[0]
    beams = beams.reshape((n_chan, n_grp) + beams.shape[3:])
    spectra_n = BLOCKS * SPEC
    frames_n = spectra_n + TAPS - 1
    wide = 512
    hbm = pl.BlockSpec(memory_space=pl.ANY)
    smem = pl.BlockSpec(memory_space=pltpu.SMEM)
    return pl.pallas_call(
        back_kernel,
        in_specs=[smem, smem, hbm, hbm, pl.BlockSpec(memory_space=pltpu.VMEM)],
        out_specs=[hbm, hbm],
        scratch_shapes=[
            pltpu.VMEM(by_id.shape, jnp.bfloat16),
            pltpu.VMEM(beams.shape, jnp.bfloat16),
            pltpu.VMEM((2, 2 * QUAD * rows, lanes), jnp.bfloat16),
            pltpu.VMEM((spectra_n * count, 2 * NCH), jnp.bfloat16),
            pltpu.VMEM((spectra_n * count, 2 * NCH), jnp.float32),
            pltpu.VMEM((2, inputs // wide, QUAD, 2, rows, wide), jnp.bfloat16),
            pltpu.VMEM((frames_n, 2 * count, NCH), jnp.float32),
            pltpu.VMEM((frames_n, count, 2, NCH), jnp.float32),
            pltpu.SemaphoreType.DMA((n_grp,)),
            pltpu.SemaphoreType.DMA,
            pltpu.SemaphoreType.DMA((2, inputs // wide)),
            pltpu.SemaphoreType.DMA,
        ],
        out_shape=[
            jax.ShapeDtypeStruct((n_grp * QUAD, 2, rows, inputs), jnp.bfloat16),
            jax.ShapeDtypeStruct((count, 2, frames_n * NCH), jnp.float32),
        ],
        name="back",
    )(sub_index, counts, by_id, beams, taps)


def local(voltages, taps, input_id, counts, delays, beam_owner):
    n_chan = lax.axis_size("chan")
    n_sub = lax.axis_size("sub")
    inp_dev = voltages.shape[0]
    inputs = input_id.shape[0]
    spectra_n = BLOCKS * SPEC
    ch_dev = NCH // n_chan
    rows = inputs // n_sub
    section = BEAMS // n_sub
    most = min(section, max(2, 2 * section // n_chan))
    fits = inp_dev == 64 and most == 32 and section == 64 and NCH == 128
    fits = fits and n_sub % 2 == 0 and ch_dev % (2 * QUAD) == 0 and inputs % 512 == 0
    if not fits or n_sub != 4 or n_chan % 2 or n_chan > 8 or rows % 128:
        return local_plain(voltages, taps, input_id, counts, delays, beam_owner)
    sub_index = lax.axis_index("sub")
    owner = beam_owner.reshape(1, -1)
    taps2 = taps.reshape(TAPS, NCH)
    names = input_id[None]
    by_id, beams = front(voltages, taps2, counts, names, delays, owner, n_chan, n_sub, most)
    visibility, resynth = back(
        by_id, beams, taps2, counts, sub_index.astype(jnp.int32)[None], rows, most
    )
    return (visibility, resynth)


def solution(mesh):
    placed = (
        P(("grp", "chan", "sub"), None, None),
        P(),
        P(),
        P("grp"),
        P(("grp", "sub"), None),
        P("grp", None),
    )
    return jax.shard_map(
        local,
        mesh=mesh,
        in_specs=placed,
        out_specs=(P(("grp", "chan"), None, "sub", None), P(("grp", "chan", "sub"), None, None)),
        check_vma=False,
    )
```

```python
import functools
import math

import jax
import jax.numpy as jnp
from jax import lax
from jax.experimental import pallas as pl
from jax.experimental.pallas import tpu as pltpu
from jax.sharding import PartitionSpec as P

NCH = 128
TAPS = 12
SPEC = 8
BLOCKS = 4
BEAMS = 256


def filter_table(taps, chans):
    length = taps.shape[0]
    position = jnp.arange(length, dtype=jnp.int32) % chans
    channel = jnp.arange(chans, dtype=jnp.int32)
    phase = (position[:, None] * channel[None, :] % chans).astype(jnp.float32) * (
        2.0 * math.pi / chans
    )
    cosine = taps[:, None] * jnp.cos(phase)
    sine = taps[:, None] * jnp.sin(phase)
    upper = jnp.concatenate([cosine, -sine], axis=1)
    lower = jnp.concatenate([sine, cosine], axis=1)
    return jnp.concatenate([upper, lower], axis=0).astype(jnp.bfloat16)


def resynthesize(received, table, taps_count, chans):
    count = received.shape[0]
    spectra_n = received.shape[3]
    table3 = table.reshape(2 * taps_count * chans, 2, chans)
    grid = jnp.einsum("pcht,mch->ptm", received, table3, preferred_element_type=jnp.float32)
    grid = grid.reshape(count, spectra_n, 2, taps_count, chans)
    total = jnp.zeros((count, spectra_n + taps_count - 1, 2, chans), jnp.float32)
    for k in range(taps_count):
        total = total + jnp.pad(
            grid[:, :, :, k, :], ((0, 0), (k, taps_count - 1 - k), (0, 0), (0, 0))
        )
    return jnp.transpose(total, (0, 2, 1, 3)).reshape(
        count, 2, (spectra_n + taps_count - 1) * chans
    )


def local_plain(voltages, taps, input_id, counts, delays, beam_owner):
    n_chan = lax.axis_size("chan")
    n_sub = lax.axis_size("sub")
    inp_dev = voltages.shape[0]
    inputs = input_id.shape[0]
    chans = NCH
    taps_count = TAPS
    spectra_n = BLOCKS * SPEC
    ch_dev = chans // n_chan
    rows = inputs // n_sub
    section = BEAMS // n_sub
    most = min(section, max(2, 2 * section // n_chan))
    table = filter_table(taps, chans)
    position = jnp.arange(spectra_n, dtype=jnp.int32)
    valid = (position % SPEC < jnp.repeat(counts, SPEC)).astype(jnp.float32)
    total = jnp.sum(counts.astype(jnp.float32))
    frames = voltages.reshape(inp_dev, 2, spectra_n + taps_count - 1, chans)
    windows = jnp.concatenate(
        [frames[:, :, k : k + spectra_n, :] for k in range(taps_count)], axis=3
    )
    table3 = table.reshape(2, taps_count * chans, 2 * chans)
    filtered = jnp.einsum("icth,chm->mit", windows, table3, preferred_element_type=jnp.float32)
    filtered = filtered * valid[None, None, :]
    spectra = filtered.reshape(2, chans, inp_dev, spectra_n).astype(jnp.bfloat16)
    slot_of = jnp.zeros((inputs,), jnp.int32).at[input_id].set(jnp.arange(inputs, dtype=jnp.int32))
    turned = lax.all_to_all(spectra, "chan", split_axis=1, concat_axis=2, tiled=True)
    gathered = lax.all_gather(turned, "sub", axis=2, tiled=True)
    chan_part = slot_of // (n_sub * inp_dev)
    sub_part = slot_of // inp_dev % n_sub
    order = (sub_part * n_chan + chan_part) * inp_dev + slot_of % inp_dev
    by_id = jnp.take(gathered, order, axis=2)
    sub_index = lax.axis_index("sub")
    mine = lax.dynamic_slice_in_dim(by_id, sub_index * rows, rows, 2)
    real_part = jnp.einsum("cxit,cxjt->xij", mine, by_id, preferred_element_type=jnp.float32)
    imag_part = jnp.einsum("xit,xjt->xij", mine[1], by_id[0], preferred_element_type=jnp.float32)
    imag_part = imag_part - jnp.einsum(
        "xit,xjt->xij", mine[0], by_id[1], preferred_element_type=jnp.float32
    )
    visibility = (jnp.stack([real_part, imag_part], axis=1) / total).astype(jnp.bfloat16)
    channel = lax.axis_index("chan") * ch_dev + jnp.arange(ch_dev, dtype=jnp.int32)
    phase = (delays[None, :, :] * channel[:, None, None] % chans).astype(jnp.float32) * (
        2.0 * math.pi / chans
    )
    scale = 1.0 / math.sqrt(inputs)
    weight_cos = (jnp.cos(phase) * scale).astype(jnp.bfloat16)
    weight_sin = (jnp.sin(phase) * scale).astype(jnp.bfloat16)
    from_cos = jnp.einsum("xbi,cxit->cxbt", weight_cos, by_id, preferred_element_type=jnp.float32)
    from_sin = jnp.einsum("xbi,cxit->cxbt", weight_sin, by_id, preferred_element_type=jnp.float32)
    beams = jnp.stack([from_cos[0] - from_sin[1], from_cos[1] + from_sin[0]]).astype(jnp.bfloat16)
    owner = lax.dynamic_slice_in_dim(beam_owner[:, 0], sub_index * section, section)
    beam = jnp.arange(section, dtype=jnp.int32)
    earlier = (owner[None, :] == owner[:, None]) & (beam[None, :] < beam[:, None])
    rank = jnp.sum(earlier.astype(jnp.int32), axis=1)
    target = owner * most + rank
    select = (jnp.arange(n_chan * most, dtype=jnp.int32)[:, None] == target[None, :]).astype(
        jnp.bfloat16
    )
    placed = jnp.einsum("pb,cxbt->pcxt", select, beams, preferred_element_type=jnp.float32).astype(
        jnp.bfloat16
    )
    placed = placed.reshape(n_chan, most, 2, ch_dev, spectra_n)
    resynth = resynthesize(
        lax.all_to_all(placed, "chan", split_axis=0, concat_axis=3, tiled=True)[0],
        table,
        taps_count,
        chans,
    )
    return (visibility, resynth)


def turn_of(steps):
    quarter = NCH // 4
    turn = steps & (NCH - 1)
    quadrant = (turn + quarter // 2) >> (quarter.bit_length() - 1)
    x = (turn - quadrant * quarter).astype(jnp.float32) * (2.0 * math.pi / NCH)
    y = x * x
    even = 1.0 + y * (-1 / 2 + y * (1 / 24 + y * (-1 / 720 + y * (1 / 40320))))
    odd = x * (1.0 + y * (-1 / 6 + y * (1 / 120 + y * (-1 / 5040 + y * (1 / 362880)))))
    swap = (quadrant & 1) == 1
    cosine, sine = jnp.where(swap, odd, even), jnp.where(swap, even, odd)
    cosine = jnp.where(((quadrant + 1) & 2) == 2, -cosine, cosine)
    return cosine, jnp.where((quadrant & 2) == 2, -sine, sine)


def weigh(first, scale, delay_ref, out_ref, at, left, high, wide):
    beams_n = delay_ref.shape[0]
    delay = delay_ref[at : at + high, left : left + wide]
    step_cos, step_sin = turn_of(delay)
    cosine, sine = turn_of(delay * first)

    def body(f, held):
        cosine, sine = held
        out_ref[f, at : at + high, left : left + wide] = cosine.astype(jnp.bfloat16)
        low = at + beams_n
        out_ref[f, low : low + high, left : left + wide] = sine.astype(jnp.bfloat16)
        return (
            cosine * step_cos - sine * step_sin,
            sine * step_cos + cosine * step_sin,
        )

    lax.fori_loop(0, out_ref.shape[0], body, (cosine * scale, sine * scale))


QUAD = 4
VOICES = 4


def trig_of(shape, n_grp):
    row = lax.broadcasted_iota(jnp.int32, shape, 0)
    lane = lax.broadcasted_iota(jnp.int32, shape, 1)
    tile = 2 * QUAD
    part = row // QUAD % 2
    channel = row // tile * QUAD + row % QUAD
    to_part = lane // NCH
    cosine, sine = turn_of(channel * (lane % NCH))
    return jnp.where(part == to_part, cosine, jnp.where(to_part == 1, sine, -sine))


def partner(x, lanes):
    pieces = [x[:, at : at + 128] for at in range(0, lanes, 128)]
    after = jnp.concatenate([pltpu.roll(p, 128 - QUAD, 1) for p in pieces], axis=1)
    before = jnp.concatenate([pltpu.roll(p, QUAD, 1) for p in pieces], axis=1)
    lane = lax.broadcasted_iota(jnp.int32, x.shape, 1)
    return lane // QUAD % 2 == 0, after, before


def front_kernel(
    n_chan, n_sub, most,
    volt_ref, taps_ref, counts_ref, name_ref, delay_ref, owner_ref,
    sorted_ref, beams_ref,
    v_ref, wide_ref, x_ref, g_ref, y_ref, d_ref, perm_ref, turn_ref, c_ref, held, weight_ref,
    place_ref, ready,
    load_sem, own_sem, out_sem, keep_sem, zs, zr, xs, xr, cs, cr, es, er,
):
    me_c, me_s = lax.axis_index("chan"), lax.axis_index("sub")
    core, across = me_s % 2, me_s // 2
    n_x = n_sub // 2
    twin = me_s + 1 - 2 * core
    mesh_id = pl.DeviceIdType.MESH
    pieces, per = x_ref.shape[1], x_ref.shape[2]
    n_grp = pieces * per
    spectra_n = BLOCKS * SPEC
    frames_n, rows = v_ref.shape[:2]
    inputs = name_ref.shape[1]
    beams_n = delay_ref.shape[0]
    ch_dev = n_grp * QUAD
    tile = 2 * QUAD
    wide = 2 * NCH
    block = x_ref.shape[3]

    def chan_of(k):
        at = me_c
        bit = 1
        while bit < n_chan:
            if k & bit:
                at = at + bit - 2 * bit * (me_c // bit % 2)
            bit *= 2
        return at

    def sub_of(offset):
        return (across + offset) % n_x * 2 + core

    barrier = pltpu.get_barrier_semaphore()
    for j in range(1, n_chan):
        pl.semaphore_signal(barrier, device_id={"chan": chan_of(j)}, device_id_type=mesh_id)
    for j in range(1, n_x):
        pl.semaphore_signal(barrier, device_id={"sub": sub_of(j)}, device_id_type=mesh_id)
    pl.semaphore_signal(barrier, device_id={"sub": twin}, device_id_type=mesh_id)

    for s in range(frames_n):
        pltpu.make_async_copy(
            volt_ref.at[:, :, pl.ds(s * NCH, NCH)], v_ref.at[s], load_sem
        ).start()

    def z_copy(j, q):
        return pltpu.make_async_remote_copy(
            src_ref=x_ref.at[chan_of(j), q],
            dst_ref=g_ref.at[q, me_c, me_s],
            send_sem=zs,
            recv_sem=zr.at[j - 1, q],
            device_id={"chan": chan_of(j)},
            device_id_type=mesh_id,
        )

    def source(j, q):
        if j == 0:
            return x_ref.at[me_c, q]
        return g_ref.at[q, chan_of(j), me_s]

    def x_copy(dx, j, q):
        return pltpu.make_async_remote_copy(
            src_ref=source(j, q),
            dst_ref=g_ref.at[q, chan_of(j), me_s],
            send_sem=xs,
            recv_sem=xr.at[dx - 1, j, q],
            device_id={"sub": sub_of(dx)},
            device_id_type=mesh_id,
        )

    def core_copy(dx, j, q):
        home = g_ref.at[q, chan_of(j), sub_of(n_x - dx)]
        return pltpu.make_async_remote_copy(
            src_ref=source(j, q) if dx == 0 else home,
            dst_ref=home,
            send_sem=cs,
            recv_sem=cr.at[q],
            device_id={"sub": twin},
            device_id_type=mesh_id,
        )

    def beam_copy(j, q):
        return pltpu.make_async_remote_copy(
            src_ref=ready.at[chan_of(j), q],
            dst_ref=beams_ref.at[me_c, q],
            send_sem=es,
            recv_sem=er,
            device_id={"chan": chan_of(j)},
            device_id_type=mesh_id,
        )

    trig = trig_of((n_chan * n_grp * tile, wide), n_grp)
    high = trig.astype(jnp.bfloat16)
    d_ref[:, :wide] = high
    d_ref[:, wide:] = (trig - high.astype(jnp.float32)).astype(jnp.bfloat16)

    valid = []
    for t in range(spectra_n):
        valid.append(jnp.where(counts_ref[t // SPEC] > t % SPEC, 1.0, 0.0))
    step = 16
    run = 4
    pltpu.make_async_copy(v_ref, v_ref, load_sem).wait()
    for s in range(frames_n):
        wide_ref[s] = v_ref[s].reshape(2 * rows, NCH).astype(jnp.float32)

    for c in range(2):

        @pl.loop(0, rows // step)
        def _(it):
            at = pl.multiple_of(it * step, step)
            taps = [taps_ref[k : k + 1, :] for k in range(TAPS)]
            for first in range(0, spectra_n, run):
                window = [
                    wide_ref[s, pl.ds(2 * at + c, step, stride=2), :]
                    for s in range(first, first + run + TAPS - 1)
                ]
                for j in range(run):
                    t = first + j
                    total = window[j] * taps[0]
                    for k in range(1, TAPS):
                        total = total + window[j + k] * taps[k]
                    total = total * valid[t]
                    high = total.astype(jnp.bfloat16)
                    low = (total - high.astype(jnp.float32)).astype(jnp.bfloat16)
                    slot = t // 2 * 2 + (t % 2 + core) % 2
                    to = pl.multiple_of(slot * rows + at, step)
                    y_ref[pl.ds(to, step), c * NCH : (c + 1) * NCH] = high
                    y_ref[pl.ds(to, step), wide + c * NCH : wide + (c + 1) * NCH] = low

    across_dims = (((1,), (1,)), ((), ()))

    @pl.loop(0, spectra_n // 4, unroll=2)
    def _(u):
        at = pl.multiple_of(u * 4 * rows, 4 * rows)
        high = y_ref[pl.ds(at, 4 * rows), :wide]
        low = y_ref[pl.ds(at, 4 * rows), wide:]
        out = lax.dot_general(d_ref[:, :wide], high, across_dims, preferred_element_type=jnp.float32)
        out = out + lax.dot_general(
            d_ref[:, wide:], high, across_dims, preferred_element_type=jnp.float32
        )
        out = out + lax.dot_general(
            d_ref[:, :wide], low, across_dims, preferred_element_type=jnp.float32
        )
        to = pl.multiple_of(u * 2 * tile, 2 * tile)
        for d in range(n_chan):
            for q in range(pieces):
                for e in range(per):
                    row = ((d * pieces + q) * per + e) * tile
                    both = jnp.concatenate(
                        [out[row : row + tile, :128], out[row : row + tile, 128:]], axis=0
                    )
                    x_ref[d, q, e, pl.ds(to, 2 * tile), :] = both.astype(jnp.bfloat16)

    pl.semaphore_wait(barrier, n_chan + n_x - 1)
    def spread(j, q):
        for dx in range(1, n_x):
            x_copy(dx, j, q).start()
        core_copy(0, j, q).start()

    for q in range(pieces):
        for j in range(1, n_chan):
            z_copy(j, q).start()
    for q in range(pieces):
        spread(0, q)
    for q in range(pieces):
        pltpu.make_async_copy(x_ref.at[me_c, q], g_ref.at[q, me_c, me_s], keep_sem).start()

    half = inputs // 4
    first = me_c * ch_dev
    scale = 1.0 / math.sqrt(inputs)

    def name_unit(m):
        def run_unit():
            low = lax.broadcasted_iota(jnp.int32, (half, inputs), 0) + m * half
            perm_ref[m * half : (m + 1) * half, :] = jnp.where(
                name_ref[...] == low, 1.0, 0.0
            ).astype(jnp.bfloat16)

        return run_unit

    def turn_unit():
        turned = jnp.dot(
            delay_ref[...].astype(jnp.float32).astype(jnp.bfloat16),
            perm_ref[...],
            preferred_element_type=jnp.float32,
        )
        turn_ref[...] = turned.astype(jnp.int32)

    def weigh_unit(at, left):
        return lambda: weigh(first, scale, turn_ref, weight_ref, at, left, 16, 512)

    def place_unit():
        lanes = per * beams_n
        own = owner_ref[:, :beams_n] * (me_s == 0).astype(jnp.int32)
        for s in range(1, n_sub):
            own = own + owner_ref[:, s * beams_n : (s + 1) * beams_n] * (me_s == s).astype(
                jnp.int32
            )
        owner = jnp.concatenate([own] * per, axis=1)
        named = (lax.broadcasted_iota(jnp.int32, (8, lanes), 0) == owner).astype(jnp.float32)
        row = lax.broadcasted_iota(jnp.int32, (lanes, lanes), 0)
        lane = lax.broadcasted_iota(jnp.int32, (lanes, lanes), 1)
        before = (row < lane) & (row // beams_n == lane // beams_n)
        rank = jnp.dot(
            named.astype(jnp.bfloat16),
            jnp.where(before, 1.0, 0.0).astype(jnp.bfloat16),
            preferred_element_type=jnp.float32,
        )
        rank = jnp.sum(named * rank, axis=0, keepdims=True).astype(jnp.int32)
        lane = lax.broadcasted_iota(jnp.int32, (1, lanes), 1)
        slot = (lane // beams_n * n_chan + owner) * (4 * most) + rank
        row = lax.broadcasted_iota(jnp.int32, (place_ref.shape[0], lanes), 0)
        for m in range(4):
            place_ref[:, m * lanes : (m + 1) * lanes] = jnp.where(
                row == slot + m * most, 1.0, 0.0
            ).astype(jnp.bfloat16)

    def join_unit(q):
        def run_unit():
            left = lax.broadcasted_iota(jnp.int32, (block, 128), 1) < 64
            for e in range(per):
                low = 2 * e * block
                for c in range(n_chan):
                    for x in range(n_x):
                        a = g_ref[q, c, 2 * x, e].astype(jnp.float32)
                        b = g_ref[q, c, 2 * x + 1, e].astype(jnp.float32)
                        at = (c * n_x + x) * 128
                        c_ref[q % 2, low : low + block, at : at + 128] = jnp.where(left, a, b).astype(
                            jnp.bfloat16
                        )
                        c_ref[q % 2, low + block : low + 2 * block, at : at + 128] = pltpu.roll(
                            jnp.where(left, b, a), 64, 1
                        ).astype(jnp.bfloat16)

        return run_unit

    def sort_unit(q, e, m):
        def run_unit():
            held[q * per + e, m * half : (m + 1) * half, :] = lax.dot_general(
                perm_ref[m * half : (m + 1) * half, :],
                c_ref[q % 2, 2 * e * block : 2 * (e + 1) * block, :],
                across_dims,
                preferred_element_type=jnp.float32,
            ).astype(jnp.bfloat16)

        return run_unit

    mixes = {}

    def mix_unit(q, e):
        def run_unit():
            at = q * per + e
            lane = lax.broadcasted_iota(jnp.int32, (2 * beams_n, 2 * block), 1)
            total = None
            for f in range(QUAD):
                mixed = lax.dot_general(
                    weight_ref[at * QUAD + f],
                    c_ref[q % 2, 2 * e * block : 2 * (e + 1) * block, :],
                    across_dims,
                    preferred_element_type=jnp.float32,
                )
                total = mixed if total is None else jnp.where(lane % QUAD == f, mixed, total)
            real, after, before = partner(total[beams_n:], 2 * block)
            mixes[q, e] = total[:beams_n] + jnp.where(real, -after, before)

        return run_unit

    def place_beams(q):
        def run_unit():
            both = jnp.concatenate([mixes.pop((q, e)) for e in range(per)], axis=0)
            turned = both.T
            parts = []
            for m in range(4):
                parity, u = m % 2, m // 2
                picks = [
                    turned[parity * block + v * 2 * tile + u * tile :][:tile]
                    for v in range(spectra_n // 4)
                ]
                parts.append(jnp.concatenate(picks, axis=0))
            lined = jnp.concatenate(parts, axis=1).astype(jnp.bfloat16)
            out = lax.dot_general(
                lined, place_ref[...], across_dims, preferred_element_type=jnp.float32
            ).astype(jnp.bfloat16)
            for e in range(per):
                for d in range(n_chan):
                    at = (e * n_chan + d) * 128
                    ready[d, q, e] = out[:, at : at + 128]
            for j in range(n_chan - 1, 0, -1):
                beam_copy(j, q).start()
            pltpu.make_async_copy(ready.at[me_c, q], beams_ref.at[me_c, q], own_sem).start()

        return run_unit

    def store_unit(q):
        def run_unit():
            part = pl.ds(q * per, per)
            pltpu.make_async_copy(held.at[part], sorted_ref.at[part], out_sem).start()

        return run_unit

    def beams_of(q):
        return [join_unit(q)] + [mix_unit(q, e) for e in range(per)] + [place_beams(q)]

    def sorts_of(q):
        units = [sort_unit(q, e, m) for e in range(per) for m in range(4)]
        return units + [store_unit(q)]

    def z_step(j, q):
        def run_step():
            z_copy(j, q).wait_recv()
            spread(j, q)

        return run_step

    def x_step(j, q):
        for dx in range(1, n_x):
            x_copy(dx, j, q).wait_recv()
            core_copy(dx, j, q).start()

    def weave(units, steps):
        done = 0
        for i, one in enumerate(steps):
            upto = len(units) * (i + 1) // len(steps)
            for unit in units[done:upto]:
                unit()
            done = upto
            one()
        for unit in units[done:]:
            unit()

    def arrive(q):
        if q == 0:
            pltpu.make_async_copy(x_ref.at[me_c], g_ref.at[:, me_c, me_s], keep_sem).wait()
        part = g_ref.at[q, pl.ds(0, n_chan // 2)]
        pltpu.make_async_copy(part, part, cr.at[q]).wait()

    setup = [name_unit(m) for m in range(4)] + [turn_unit]
    setup += [
        weigh_unit(at, left) for at in range(0, beams_n, 16) for left in range(0, inputs, 512)
    ]
    setup.append(place_unit)
    def z_steps(q):
        return [z_step(j, q) for j in range(1, n_chan)] if q < pieces else []

    def x_steps(q):
        return [functools.partial(x_step, j, q) for j in range(n_chan)]

    def mingle(one, two):
        pairs = [(i / len(one), 0, s) for i, s in enumerate(one)]
        pairs += [((i + 0.5) / len(two), 1, s) for i, s in enumerate(two)]
        return [s for _, _, s in sorted(pairs, key=lambda p: p[:2])]

    weave(setup[:7], z_steps(0))
    for q in range(1, pieces + 1):
        steps = mingle(x_steps(q - 1), z_steps(q))
        if q >= 2:
            arrive(q - 2)
            weave(beams_of(q - 2) + (sorts_of(q - 2) if q < pieces else []), steps)
        else:
            weave(setup[7:], steps)
    arrive(pieces - 1)
    weave(beams_of(pieces - 1) + sorts_of(pieces - 2) + sorts_of(pieces - 1), [])
    others = pl.ds(0, n_chan - 1)
    pltpu.make_async_copy(ready.at[others], beams_ref.at[others], er).wait()
    pltpu.make_async_copy(x_ref.at[others], x_ref.at[others], zs).wait()
    for dx in range(1, n_x):
        pltpu.make_async_copy(x_ref, x_ref, xs).wait()
    part = g_ref.at[pl.ds(0, pieces // 2)]
    pltpu.make_async_copy(part, part, cs).wait()
    pltpu.make_async_copy(ready.at[others], ready.at[others], es).wait()
    pltpu.make_async_copy(ready.at[me_c], beams_ref.at[me_c], own_sem).wait()
    pltpu.make_async_copy(held, sorted_ref, out_sem).wait()


def front(voltages, taps, counts, names, delays, owner, n_chan, n_sub, most):
    rows = voltages.shape[0]
    beams_n, inputs = delays.shape
    spectra_n = BLOCKS * SPEC
    ch_dev = NCH // n_chan
    n_grp = ch_dev // QUAD
    per = 2
    pieces = n_grp // per
    n_x = n_sub // 2
    tile = 2 * QUAD
    block = spectra_n // 2 * tile
    dma = pltpu.SemaphoreType.DMA
    vmem = pl.BlockSpec(memory_space=pltpu.VMEM)
    travel = (n_chan, pieces, per, spectra_n // 4 * tile, 128)
    return pl.pallas_call(
        functools.partial(front_kernel, n_chan, n_sub, most),
        in_specs=[
            pl.BlockSpec(memory_space=pl.ANY),
            vmem,
            pl.BlockSpec(memory_space=pltpu.SMEM),
            vmem,
            vmem,
            vmem,
        ],
        out_specs=[pl.BlockSpec(memory_space=pl.ANY)] * 2,
        out_shape=[
            jax.ShapeDtypeStruct((n_grp, inputs, 2 * block), jnp.bfloat16),
            jax.ShapeDtypeStruct(travel, jnp.bfloat16),
        ],
        scratch_shapes=[
            pltpu.VMEM((spectra_n + TAPS - 1, rows, 2, NCH), jnp.bfloat16),
            pltpu.VMEM((spectra_n + TAPS - 1, 2 * rows, NCH), jnp.float32),
            pltpu.VMEM((n_chan, pieces, per, block, 128), jnp.bfloat16),
            pltpu.VMEM((pieces, n_chan, n_sub, per, block, 128), jnp.bfloat16),
            pltpu.VMEM((spectra_n * rows, 4 * NCH), jnp.bfloat16),
            pltpu.VMEM((2 * NCH, 4 * NCH), jnp.bfloat16),
            pltpu.VMEM((inputs, inputs), jnp.bfloat16),
            pltpu.VMEM((beams_n, inputs), jnp.int32),
            pltpu.VMEM((2, 2 * per * block, inputs), jnp.bfloat16),
            pltpu.VMEM((n_grp, inputs, 2 * block), jnp.bfloat16),
            pltpu.VMEM((ch_dev, 2 * beams_n, inputs), jnp.bfloat16),
            pltpu.VMEM((per * n_chan * 128, 4 * per * beams_n), jnp.bfloat16),
            pltpu.VMEM(travel, jnp.bfloat16),
            dma,
            dma,
            dma,
            dma,
            dma,
            dma((n_chan - 1, pieces)),
            dma,
            dma((n_x - 1, n_chan, pieces)),
            dma,
            dma((pieces,)),
            dma,
            dma,
        ],
        compiler_params=pltpu.CompilerParams(collective_id=0, has_side_effects=True),
        name="front",
    )(voltages, taps, counts, names, delays, owner)


def back_kernel(
    sub_ref, counts_ref, sorted_ref, heard_ref, taps_ref,
    out_ref, voices_ref,
    all_ref, beams_ref, left_ref, bank_ref, wave_ref, made_ref, mix_ref, voice_ref,
    in_sem, heard_sem, out_sem, voice_sem,
):
    n_grp, inputs, lanes = all_ref.shape
    rows, wide = made_ref.shape[4:]
    frames_n, count = voice_ref.shape[:2]
    spectra_n = frames_n - TAPS + 1
    n_chan = beams_ref.shape[0]
    tile = 2 * QUAD
    mine = pl.ds(pl.multiple_of(sub_ref[0] * rows, rows), rows)

    def in_copy(g):
        return pltpu.make_async_copy(sorted_ref.at[g], all_ref.at[g], in_sem.at[g])

    def out_copy(g, n):
        return pltpu.make_async_copy(
            made_ref.at[g % 2, n],
            out_ref.at[pl.ds(g * QUAD, QUAD), :, :, pl.ds(n * wide, wide)],
            out_sem.at[g % 2, n],
        )

    heard = pltpu.make_async_copy(heard_ref, beams_ref, heard_sem)
    in_copy(0).start()
    in_copy(1).start()
    heard.start()
    total = counts_ref[0]
    for i in range(1, BLOCKS):
        total = total + counts_ref[i]
    scale = 1.0 / jnp.full((8, 128), total.astype(jnp.float32))
    scale = scale[:1, :1]
    lane = lax.broadcasted_iota(jnp.int32, (16, lanes), 1) % QUAD
    keeps = []
    for i in range(QUAD):
        keep = jnp.where(lane == i, 1.0, 0.0).astype(jnp.bfloat16)
        keeps.append(jnp.concatenate([keep] * (rows // 16), axis=0))

    def fill(g):
        plain = all_ref[g, mine, :]
        real, after, before = partner(plain.astype(jnp.float32), lanes)
        turned = jnp.where(real, after, -before).astype(jnp.bfloat16)
        for i in range(QUAD):
            at = 2 * i * rows
            left_ref[g % 2, at : at + rows, :] = plain * keeps[i]
            left_ref[g % 2, at + rows : at + 2 * rows, :] = turned * keeps[i]

    def correlate(g):
        for n in range(inputs // wide):
            product = lax.dot_general(
                left_ref[g % 2],
                all_ref[g, n * wide : (n + 1) * wide, :],
                (((1,), (1,)), ((), ())),
                preferred_element_type=jnp.float32,
            )
            product = (product * scale).astype(jnp.bfloat16)
            for i in range(QUAD):
                for c in range(2):
                    low = (2 * i + c) * rows
                    made_ref[g % 2, n, i, c] = product[low : low + rows]
            out_copy(g, n).start()

    def line_up():
        heard.wait()
        for u in range(0, spectra_n // 4, 2):
            tiles = [
                beams_ref[c, e, u * tile : (u + 2) * tile, :].astype(jnp.float32)
                for c in range(n_chan)
                for e in range(n_grp)
            ]
            for v in range(2):
                stack = jnp.concatenate([t[v * tile : (v + 1) * tile] for t in tiles], axis=0)
                at = (u + v) * 4 * count
                bank_ref[at : at + 4 * count, :] = stack.T.astype(jnp.bfloat16)

    def transform():
        trig = trig_of((2 * NCH, 2 * NCH), n_grp)
        high = trig.astype(jnp.bfloat16)
        low = (trig - high.astype(jnp.float32)).astype(jnp.bfloat16)
        wave_ref[...] = jnp.dot(
            bank_ref[...], high, preferred_element_type=jnp.float32
        ) + jnp.dot(bank_ref[...], low, preferred_element_type=jnp.float32)

    def speak(first):
        run = min(VOICES, frames_n - first)
        for c in range(2):
            lanes = slice(c * NCH, (c + 1) * NCH)
            taps = [taps_ref[k : k + 1, :] for k in range(TAPS)]
            for p in range(0, count, 8):
                window = {
                    s: wave_ref[s * count + p : s * count + p + 8, lanes]
                    for s in range(max(0, first - TAPS + 1), min(spectra_n, first + run))
                }
                for j in range(run):
                    terms = [
                        window[first + j - k] * taps[k]
                        for k in range(TAPS)
                        if 0 <= first + j - k < spectra_n
                    ]
                    total = terms[0]
                    for term in terms[1:]:
                        total = total + term
                    mix_ref[first + j, pl.ds(2 * p + c, 8, stride=2), :] = total
        for j in range(run):
            voice_ref[first + j] = mix_ref[first + j].reshape(count, 2, NCH)
            pltpu.make_async_copy(
                voice_ref.at[first + j],
                voices_ref.at[:, :, pl.ds((first + j) * NCH, NCH)],
                voice_sem,
            ).start()

    jobs = [line_up, transform]
    jobs += [functools.partial(speak, first) for first in range(0, frames_n, VOICES)]
    shares = n_grp - 1
    done = 0
    in_copy(0).wait()
    fill(0)
    for g in range(n_grp):
        if g >= 2:
            for n in range(inputs // wide):
                out_copy(g - 2, n).wait()
        if g + 1 < n_grp:
            in_copy(g + 1).wait()
            if g + 2 < n_grp:
                in_copy(g + 2).start()
            fill(g + 1)
        correlate(g)
        upto = min(len(jobs), -(-len(jobs) * (g + 1) // shares))
        for job in jobs[done:upto]:
            job()
        done = upto
    for g in range(n_grp - 2, n_grp):
        for n in range(inputs // wide):
            out_copy(g, n).wait()
    pltpu.make_async_copy(voice_ref, voice_ref, voice_sem).wait()


def back(by_id, beams, taps, counts, sub_index, rows, count):
    n_grp, inputs, lanes = by_id.shape
    n_chan = beams.shape[0]
    beams = beams.reshape((n_chan, n_grp) + beams.shape[3:])
    spectra_n = BLOCKS * SPEC
    frames_n = spectra_n + TAPS - 1
    wide = 512
    hbm = pl.BlockSpec(memory_space=pl.ANY)
    smem = pl.BlockSpec(memory_space=pltpu.SMEM)
    return pl.pallas_call(
        back_kernel,
        in_specs=[smem, smem, hbm, hbm, pl.BlockSpec(memory_space=pltpu.VMEM)],
        out_specs=[hbm, hbm],
        scratch_shapes=[
            pltpu.VMEM(by_id.shape, jnp.bfloat16),
            pltpu.VMEM(beams.shape, jnp.bfloat16),
            pltpu.VMEM((2, 2 * QUAD * rows, lanes), jnp.bfloat16),
            pltpu.VMEM((spectra_n * count, 2 * NCH), jnp.bfloat16),
            pltpu.VMEM((spectra_n * count, 2 * NCH), jnp.float32),
            pltpu.VMEM((2, inputs // wide, QUAD, 2, rows, wide), jnp.bfloat16),
            pltpu.VMEM((frames_n, 2 * count, NCH), jnp.float32),
            pltpu.VMEM((frames_n, count, 2, NCH), jnp.float32),
            pltpu.SemaphoreType.DMA((n_grp,)),
            pltpu.SemaphoreType.DMA,
            pltpu.SemaphoreType.DMA((2, inputs // wide)),
            pltpu.SemaphoreType.DMA,
        ],
        out_shape=[
            jax.ShapeDtypeStruct((n_grp * QUAD, 2, rows, inputs), jnp.bfloat16),
            jax.ShapeDtypeStruct((count, 2, frames_n * NCH), jnp.float32),
        ],
        name="back",
    )(sub_index, counts, by_id, beams, taps)


def local(voltages, taps, input_id, counts, delays, beam_owner):
    n_chan = lax.axis_size("chan")
    n_sub = lax.axis_size("sub")
    inp_dev = voltages.shape[0]
    inputs = input_id.shape[0]
    spectra_n = BLOCKS * SPEC
    ch_dev = NCH // n_chan
    rows = inputs // n_sub
    section = BEAMS // n_sub
    most = min(section, max(2, 2 * section // n_chan))
    fits = inp_dev == 64 and most == 32 and section == 64 and NCH == 128
    fits = fits and n_sub % 2 == 0 and ch_dev % (2 * QUAD) == 0 and inputs % 512 == 0
    if not fits or n_sub != 4 or n_chan & (n_chan - 1) or n_chan > 8 or rows % 128:
        return local_plain(voltages, taps, input_id, counts, delays, beam_owner)
    sub_index = lax.axis_index("sub")
    owner = beam_owner.reshape(1, -1)
    taps2 = taps.reshape(TAPS, NCH)
    names = input_id[None]
    by_id, beams = front(voltages, taps2, counts, names, delays, owner, n_chan, n_sub, most)
    visibility, resynth = back(
        by_id, beams, taps2, counts, sub_index.astype(jnp.int32)[None], rows, most
    )
    return (visibility, resynth)


def solution(mesh):
    placed = (
        P(("grp", "chan", "sub"), None, None),
        P(),
        P(),
        P("grp"),
        P(("grp", "sub"), None),
        P("grp", None),
    )
    return jax.shard_map(
        local,
        mesh=mesh,
        in_specs=placed,
        out_specs=(P(("grp", "chan"), None, "sub", None), P(("grp", "chan", "sub"), None, None)),
        check_vma=False,
    )
```
